32 devices in a mesh: dp: 16 (over z, y, core), mp: 2 (over x).
Axes of the slice: x: 2, y: 2, z: 4, core: 2. Of those that a mesh axis runs over, the one named last changes fastest.
Arguments:
- tokens: bfloat16 [32, 1024, 768], P('dp'), may hold values from -6 to 6
- valid: int32 [32, 1024], P('dp'), may hold values from 0 to 1, as said below
- steps: int32 [32], replicated, may hold values from 0 to 999
- labels: int32 [32], replicated, may hold values from 0 to 999
- w_mod: bfloat16 [768, 4608], replicated, may hold values from -0.21875 to 0.21875
- step_table: bfloat16 [1000, 768], replicated, may hold values from -4 to 4
- class_table: bfloat16 [1000, 768], replicated, may hold values from -4 to 4
- conv_attn: bfloat16 [9, 768], replicated, may hold values from -2 to 2
- w_qkv: bfloat16 [768, 3, 768], P(None, None, 'mp'), may hold values from -0.21875 to 0.21875
- w_out: bfloat16 [768, 768], P(None, 'mp'), may hold values from -0.875 to 0.875
- conv_ffn: bfloat16 [9, 3072], P(None, 'mp'), may hold values from -2 to 2
- w_up: bfloat16 [768, 3072], P(None, 'mp'), may hold values from -0.21875 to 0.21875
- w_down: bfloat16 [768, 3072], P(None, 'mp'), may hold values from -0.109375 to 0.109375
- cotangent: bfloat16 [32, 1024, 768], P('dp'), may hold values from -6 to 6
Outputs:
- output: bfloat16 [32, 1024, 768], P('dp')
- grad_tokens: bfloat16 [32, 1024, 768], P('dp')
- grad_w_mod: float32 [768, 4608], P('dp')
- grad_step_table: float32 [1000, 768], replicated
- grad_class_table: float32 [1000, 768], replicated
- grad_conv_attn: float32 [9, 768], replicated
- grad_w_qkv: float32 [768, 3, 768], P('dp', None, 'mp')
- grad_w_out: float32 [768, 768], P('dp', 'mp')
- grad_conv_ffn: float32 [9, 3072], P(None, 'mp')
- grad_w_up: float32 [768, 3072], P('dp', 'mp')
- grad_w_down: float32 [768, 3072], P('dp', 'mp')
The draws below stay inside these ranges and needn't reach their ends.
Inputs may be any that keep to these rules, and one draw needn't show every extreme that they name: tokens 0, 1, 32 and 33 of every latent are valid, so each group has a valid key.
All inputs are finite; a program needn't handle non-finite values.
Results may differ from the reference program's by a relative error of at most 0.017.
The reference program's roundings to bfloat16 on the way count: a program that leaves them out, or rounds other values in their place, can miss the bound.
Values may be sent and summed in bfloat16 or wider, within the bound.
No kernel may reach another device: no remote copies, remote signals or barrier semaphores. Data moves between devices by JAX's collectives and lax.ppermute only.
A program may use at most 384 MiB of HBM per device.

```python
import jax
import jax.numpy as jnp
from jax import lax

D = 768
HEADS = 12
FF = 3072
TSTEPS = 1000
CLASSES = 1000
SIDE = 32
HEAD_DIM = 64
LATENTS = 32


def draw_valid(key, part):
    coins = jax.random.randint(key, (LATENTS, SIDE * SIDE), 0, 4)
    keep_mask = jnp.where(coins > 0, 1, 0).astype(jnp.int32)
    column = jnp.arange(SIDE * SIDE, dtype=jnp.int32)
    corner = (column == 0) | (column == 1) | (column == SIDE) | (column == SIDE + 1)
    return jnp.where(corner[None, :], 1, keep_mask).astype(jnp.int32)


def set_ends(drawn, rng, low, high):
    extent = drawn.shape
    index_at = [jax.random.randint(jax.random.fold_in(rng, axis), (), 0, extent[axis]) for axis in range(len(extent))]
    drawn = drawn.at[tuple(index_at)].set(low)
    longest = extent.index(max(extent))
    index_at[longest] = (index_at[longest] + 1) % extent[longest]
    return drawn.at[tuple(index_at)].set(high)


def block_scale(stream_key, dims, split, smallest, high):
    def one(axis_at, blocks):
        heights = jax.random.uniform(jax.random.fold_in(jax.random.fold_in(stream_key, 6), axis_at), (blocks,), jnp.float32, smallest / len(split), high / len(split))
        return jnp.repeat(jnp.exp(heights), dims[axis_at] // blocks).reshape((-1,) + (1,) * (len(dims) - axis_at - 1))

    gain = one(*split[0])
    for cut in split[1:]:
        gain = gain * one(*cut)
    return gain


def centred(key, dims, deviation, most, shards=(), held_as=jnp.bfloat16):
    entries = jax.random.normal(key, dims, jnp.float32) * deviation
    if len(shards) > 0:
        entries = block_scale(key, dims, shards, -0.22, 0.18) * entries
    return jnp.clip(entries, min=-most, max=most).astype(held_as)


def setup_inputs(seed: int = 0) -> dict:
    seeds = jax.random.split(jax.random.key(seed), 15)
    tokens = centred(seeds[0], (LATENTS, SIDE * SIDE, D), 1.0, 6.0, ((0, 16),))
    valid = draw_valid(jax.random.fold_in(seeds[14], 71), 0)
    steps = set_ends(jax.random.randint(seeds[2], (LATENTS,), 0, TSTEPS), jax.random.fold_in(seeds[2], 1), 0, TSTEPS - 1).astype(jnp.int32)
    labels = set_ends(jax.random.randint(seeds[3], (LATENTS,), 0, CLASSES), jax.random.fold_in(seeds[3], 1), 0, CLASSES - 1).astype(jnp.int32)
    w_mod = centred(seeds[4], (D, 6 * D), D ** -0.5, 0.21875)
    step_table = centred(seeds[5], (TSTEPS, D), 0.7, 4.0)
    class_table = centred(seeds[6], (CLASSES, D), 0.7, 4.0)
    conv_attn = centred(seeds[7], (9, D), 9 ** -0.5, 2.0)
    w_qkv = centred(seeds[8], (D, 3, D), D ** -0.5, 0.21875, ((2, 2),))
    w_out = centred(seeds[9], (D, D), (D // 16) ** -0.5, 0.875, ((1, 2),))
    conv_ffn = centred(seeds[10], (9, FF), 9 ** -0.5, 2.0, ((1, 2),))
    w_up = centred(seeds[11], (D, FF), D ** -0.5, 0.21875, ((1, 2),))
    w_down = centred(seeds[12], (D, FF), FF ** -0.5, 0.109375, ((1, 2),))
    cotangent = centred(seeds[13], (LATENTS, SIDE * SIDE, D), 1.0, 6.0, ((0, 16),))
    return dict(tokens=tokens, valid=valid, steps=steps, labels=labels, w_mod=w_mod, step_table=step_table, class_table=class_table, conv_attn=conv_attn, w_qkv=w_qkv, w_out=w_out, conv_ffn=conv_ffn, w_up=w_up, w_down=w_down, cotangent=cotangent)


@jax.custom_vjp
def low(v):
    return lax.optimization_barrier(v.astype(jnp.bfloat16)).astype(jnp.float32)

@jax.custom_vjp
def low_back(v):
    return v

def low_keep(v):
    return (low(v), None)

def low_pass(kept, grad):
    return (grad,)

def back_keep(v):
    return (v, None)

def back_low(kept, grad):
    return (low(grad),)
low.defvjp(low_keep, low_pass)
low_back.defvjp(back_keep, back_low)
eps_norm = 1e-06
highest = lax.Precision.HIGHEST

def layer_norm(values_in):
    centre = values_in - lax.optimization_barrier(jnp.mean(values_in, axis=-1, keepdims=True))
    return centre * lax.rsqrt(lax.optimization_barrier(jnp.mean(centre * centre, axis=-1, keepdims=True)) + eps_norm)

def depthwise(values_in, kernel):
    batches = values_in.shape[0]
    channels = values_in.shape[-1]
    blocked = values_in.reshape(batches, SIDE, SIDE, channels)
    padded = jnp.pad(blocked, ((0, 0), (1, 1), (1, 1), (0, 0)))
    summed = jnp.zeros_like(blocked)
    for row_off in range(3):
        for col_off in range(3):
            window = padded[:, row_off:row_off + SIDE, col_off:col_off + SIDE, :]
            summed = summed + kernel[row_off * 3 + col_off] * window
    return summed.reshape(values_in.shape)

def unshuffle(tokens_in):
    halfside = SIDE // 2
    batches = tokens_in.shape[0]
    channels = tokens_in.shape[-1]
    blocked = tokens_in.reshape(batches, halfside, 2, halfside, 2, channels)
    return blocked.transpose(0, 2, 4, 1, 3, 5).reshape(batches, 4, halfside * halfside, channels)

def reshuffle(groups_in):
    halfside = SIDE // 2
    batches = groups_in.shape[0]
    channels = groups_in.shape[-1]
    blocked = groups_in.reshape(batches, 2, 2, halfside, halfside, channels)
    return blocked.transpose(0, 3, 1, 4, 2, 5).reshape(batches, SIDE * SIDE, channels)

def silu_of(values_in):
    return values_in * jax.nn.sigmoid(values_in)

def layer_one(weights, inputs):
    kernel_a, qkv_weight, out_weight, kernel_f, up_weight, down_weight = weights
    tok_in, modulation, keep_mask = inputs
    normed = layer_norm(tok_in) * (1.0 + modulation[1]) + modulation[0]
    conved = low(depthwise(normed[None], kernel_a))
    grouped = unshuffle(conved)[0]
    group_len = grouped.shape[1]
    qkv = low(low_back(jnp.einsum('gtd,dch->gtch', grouped, qkv_weight, precision=highest)))
    head_view = qkv.reshape(4, group_len, 3, HEADS, HEAD_DIM)
    queries = head_view[:, :, 0]
    keyset = head_view[:, :, 1]
    values = head_view[:, :, 2]
    raw_scores = low_back(jnp.einsum('gqhe,gkhe->ghqk', queries, keyset, precision=highest))
    scores = jnp.where(keep_mask[:, None, None, :] > 0, raw_scores * HEAD_DIM ** (-0.5), -1e+30)
    shifted = scores - lax.optimization_barrier(jnp.max(scores, axis=-1, keepdims=True))
    exponent = jnp.exp(shifted)
    weights_soft = exponent / lax.optimization_barrier(jnp.sum(exponent, axis=-1, keepdims=True))
    mixed = jnp.einsum('ghqk,gkhe->gqhe', low(weights_soft), values, precision=highest)
    mixed = low(low_back(mixed)).reshape(1, 4, group_len, HEADS * HEAD_DIM)
    mixed_tokens = reshuffle(mixed)[0]
    attn = low_back(jnp.einsum('pe,de->pd', mixed_tokens, out_weight, precision=highest))
    residual = tok_in + modulation[2] * attn
    normed_two = low(layer_norm(residual) * (1.0 + modulation[4]) + modulation[3])
    upper_proj = low_back(jnp.einsum('pd,df->pf', normed_two, up_weight, precision=highest))
    active = low(jax.nn.gelu(depthwise(upper_proj[None], kernel_f)[0]))
    down = low_back(jnp.einsum('pf,df->pd', active, down_weight, precision=highest))
    return residual + modulation[5] * down

def reference(tokens, valid, steps, labels, w_mod, step_table, class_table, conv_attn, w_qkv, w_out, conv_ffn, w_up, w_down, cotangent):
    floats = tuple((array_in.astype(jnp.float32) for array_in in (tokens, w_mod, step_table, class_table, conv_attn, w_qkv, w_out, conv_ffn, w_up, w_down)))
    keep_all = unshuffle(valid[:, :, None])[..., 0]
    lat_total = tokens.shape[0]

    def forward(tok_in, mod_weight, step_rows, class_rows, kernel_a, qkv_weight, out_weight, kernel_f, up_weight, down_weight):
        embedding = jnp.take(step_rows, steps, axis=0) + jnp.take(class_rows, labels, axis=0)
        modulation = low_back(jnp.dot(low(silu_of(embedding)), mod_weight, precision=highest))
        modulation = modulation.reshape(lat_total, 6, 1, -1)
        weights = (kernel_a, qkv_weight, out_weight, kernel_f, up_weight, down_weight)

        def one_latent(inputs):
            return layer_one(weights, inputs)
        return lax.map(jax.checkpoint(one_latent), (tok_in, modulation, keep_all))
    result, pullback = jax.vjp(forward, *floats)
    gradients = pullback(cotangent.astype(jnp.float32))
    return (result.astype(jnp.bfloat16), gradients[0].astype(jnp.bfloat16), gradients[1], gradients[2], gradients[3], gradients[4], gradients[5], gradients[6], gradients[7], gradients[8], gradients[9])
```

```python
from functools import partial

import jax
import jax.numpy as jnp
from jax import lax
from jax.experimental import pallas as pl
from jax.experimental.pallas import tpu as pltpu
from jax.sharding import PartitionSpec as P

SIDE = 32
HALF = SIDE // 2
HEAD_DIM = 64
GROUPS = 4
LANES = 128
TILE = 256
EPS = 1e-06
PITCH = HALF + 8
GROUP_ROWS = (HALF + 2) * PITCH + 8
PAD_ROWS = GROUPS * GROUP_ROWS
GELU_A = 0.7978845608028654
GELU_B = 0.044715
F32 = jnp.float32
BF16 = jnp.bfloat16
VMEM_BYTES = 60 * 1024 * 1024


def params(count=1):
    return pltpu.CompilerParams(
        dimension_semantics=("arbitrary",) * count, vmem_limit_bytes=VMEM_BYTES
    )


def whole(shape):
    zeros = (0,) * len(shape)
    return pl.BlockSpec(shape, lambda *_: zeros, pipeline_mode=pl.Buffered(1))


def dot(left, right):
    return jnp.dot(left, right, preferred_element_type=F32)


def dot_nt(left, right):
    return lax.dot_general(left, right, (((1,), (1,)), ((), ())), preferred_element_type=F32)


def pad_row(group, row, shift=0):
    return group * GROUP_ROWS + (row + 1) * PITCH + 8 + shift


AROUND = ((1, -1), (0, 0), (1, 0), (0, 1))


def neighbours(grid_ref, lane_block, row):
    found = []
    for row_par, row_off in AROUND:
        line = []
        for col_par, col_off in AROUND:
            const = pad_row(row_par * 2 + col_par, row_off, col_off)
            line.append(grid_ref[lane_block, pl.ds(row * PITCH + const, HALF), :])
        found.append(line)
    return found


def taps_of(kern_ref, lanes):
    return [
        jnp.broadcast_to(kern_ref[tap : tap + 1, lanes].astype(F32), (HALF, LANES))
        for tap in range(9)
    ]


def conv_at(found, taps, row_par, col_par):
    total = None
    for row_off in range(3):
        for col_off in range(3):
            term = taps[row_off * 3 + col_off] * found[row_par + row_off][col_par + col_off]
            total = term if total is None else total + term
    return total


def conv_back_at(found, taps, sums, source, row_par, col_par):
    total = None
    sums = list(sums)
    for row_off in range(3):
        for col_off in range(3):
            tap = row_off * 3 + col_off
            near = found[row_par + 2 - row_off][col_par + 2 - col_off]
            term = taps[tap] * near
            total = term if total is None else total + term
            part = source * near
            sums[tap] = sums[tap] + (part[:8] + part[8:])
    return total, tuple(sums)


def no_sums():
    return tuple(jnp.zeros((8, LANES), F32) for _ in range(9))


def split_lanes(values_in):
    count = values_in.shape[-1] // LANES
    return [values_in[:, j * LANES : (j + 1) * LANES] for j in range(count)]


def norm_parts(parts):
    width = len(parts) * LANES
    mean = jnp.sum(sum(parts[1:], parts[0]), axis=-1, keepdims=True) * (1.0 / width)
    centre = [part - mean for part in parts]
    squares = [part * part for part in centre]
    var = jnp.sum(sum(squares[1:], squares[0]), axis=-1, keepdims=True) * (1.0 / width)
    rstd = lax.rsqrt(var + EPS)
    return [part * rstd for part in centre], rstd


def norm_rows(values_in):
    mean = jnp.mean(values_in, axis=-1, keepdims=True)
    centre = values_in - mean
    rstd = lax.rsqrt(jnp.mean(centre * centre, axis=-1, keepdims=True) + EPS)
    return centre * rstd, rstd


def group_of(row_par, col_par):
    return row_par * 2 + col_par


def first_kernel(
    idx, tok_ref, cot_ref, mod_ref, kern_ref, conv_out, tok_out, cot_out, tok_tmp, cot_tmp, grid
):
    width = tok_ref.shape[-1]
    count = width // LANES
    grid[...] = jnp.zeros(grid.shape, F32)

    def one_row(row, carry):
        for row_par in range(2):
            start = pl.multiple_of((row * 2 + row_par) * SIDE, SIDE)
            values = tok_ref[0, pl.ds(start, SIDE), :].astype(F32)
            grads = cot_ref[0, pl.ds(start, SIDE), :].astype(F32)
            for j in range(count):
                tok_tmp[row_par, j] = values[:, j * LANES : (j + 1) * LANES]
                cot_tmp[row_par, j] = grads[:, j * LANES : (j + 1) * LANES]
            for col_par in range(2):
                group = group_of(row_par, col_par)
                out_row = pl.multiple_of(group * TILE + row * HALF, HALF)
                parts = [tok_tmp[row_par, j, pl.ds(col_par, HALF, stride=2), :] for j in range(count)]
                for j in range(count):
                    lanes = slice(j * LANES, (j + 1) * LANES)
                    tok_out[pl.ds(out_row, HALF), lanes] = parts[j].astype(BF16)
                    cot_out[pl.ds(out_row, HALF), lanes] = cot_tmp[
                        row_par, j, pl.ds(col_par, HALF, stride=2), :
                    ].astype(BF16)
                normed, _ = norm_parts(parts)
                for j in range(count):
                    lanes = slice(j * LANES, (j + 1) * LANES)
                    value = normed[j] * (1.0 + mod_ref[1:2, lanes]) + mod_ref[0:1, lanes]
                    grid[j, pl.ds(row * PITCH + pad_row(group, 0), HALF), :] = value
        return carry

    lax.fori_loop(0, HALF, one_row, 0)
    for j in range(count):
        lanes = slice(j * LANES, (j + 1) * LANES)
        taps = taps_of(kern_ref, lanes)

        def one_conv(row, carry, j=j, lanes=lanes, taps=taps):
            found = neighbours(grid, j, row)
            for row_par in range(2):
                for col_par in range(2):
                    out_row = pl.multiple_of(group_of(row_par, col_par) * TILE + row * HALF, HALF)
                    value = conv_at(found, taps, row_par, col_par)
                    conv_out[pl.ds(out_row, HALF), lanes] = value.astype(BF16)
            return carry

        lax.fori_loop(0, HALF, one_conv, 0)


def first_stage(idx, tokens, cotangent, mod, kern):
    _, length, width = tokens.shape
    shape = jax.ShapeDtypeStruct((length, width), BF16)
    mine = pl.BlockSpec((1, length, width), lambda i, idx: (idx[0], 0, 0))
    return pl.pallas_call(
        first_kernel,
        out_shape=(shape, shape, shape),
        grid_spec=pltpu.PrefetchScalarGridSpec(
            num_scalar_prefetch=1,
            grid=(1,),
            in_specs=[mine, mine, whole(mod.shape), whole(kern.shape)],
            out_specs=[whole((length, width))] * 3,
            scratch_shapes=[
                pltpu.VMEM((2, width // LANES, SIDE, LANES), F32),
                pltpu.VMEM((2, width // LANES, SIDE, LANES), F32),
                pltpu.VMEM((width // LANES, PAD_ROWS, LANES), F32),
            ],
        ),
        compiler_params=params(),
        name="norm_conv",
        cost_estimate=pl.CostEstimate(flops=40_000_000, bytes_accessed=8_000_000, transcendentals=0),
    )(idx, tokens, cotangent, mod, kern)


def head_mask(values_in, which):
    lane = lax.broadcasted_iota(jnp.int32, values_in.shape, 1)
    keep = lane < HEAD_DIM if which == 0 else lane >= HEAD_DIM
    return jnp.where(keep, values_in, jnp.zeros_like(values_in))


def soft_keys(keys, queries, keep):
    raw = dot_nt(keys, queries)
    scores = jnp.where(keep, raw * (HEAD_DIM**-0.5), -1e30)
    exponent = jnp.exp(scores - jnp.max(scores, axis=0, keepdims=True))
    return exponent * (1.0 / jnp.sum(exponent, axis=0, keepdims=True))


def attend_kernel(
    conv_ref, valid_ref, wa_ref, wb_ref, oa_ref, ob_ref, tok_ref, cot_ref, mod_ref,
    qkv_out, mixed_out, attn_out, res_out, norm_out, gdown_out,
):
    share = wa_ref.shape[-1]
    conved = conv_ref[...]
    keep = jnp.broadcast_to(valid_ref[0], (TILE, TILE)) > 0
    for side, weight_ref in enumerate((wa_ref, wb_ref)):
        for which in range(3):
            qkv_out[side, :, which * share : (which + 1) * share] = dot(
                conved, weight_ref[which]
            ).astype(BF16)
        for pair in range(share // LANES):
            lanes = [slice(t * share + pair * LANES, t * share + (pair + 1) * LANES) for t in range(3)]
            queries = qkv_out[side, :, lanes[0]]
            keys = qkv_out[side, :, lanes[1]]
            values_t = qkv_out[side, :, lanes[2]].astype(F32).T.astype(BF16)
            halves = []
            for which in range(2):
                probs = soft_keys(head_mask(keys, which), queries, keep).astype(BF16)
                halves.append(dot(values_t[which * HEAD_DIM : (which + 1) * HEAD_DIM], probs))
            mixed_t = jnp.concatenate(halves, axis=0)
            first = side * share + pair * LANES
            mixed_out[:, first : first + LANES] = mixed_t.T.astype(BF16)
    attn = dot_nt(mixed_out[:, :share], oa_ref[...]) + dot_nt(mixed_out[:, share:], ob_ref[...])
    attn_out[...] = attn
    residual = tok_ref[...].astype(F32) + mod_ref[2:3, :] * attn
    res_out[...] = residual
    normed, _ = norm_rows(residual)
    norm_out[...] = (normed * (1.0 + mod_ref[4:5, :]) + mod_ref[3:4, :]).astype(BF16)
    gdown_out[...] = (mod_ref[5:6, :] * cot_ref[...].astype(F32)).astype(BF16)


def attend_stage(conved, valid, w_own, w_other, o_own, o_other, tok, cot, mod):
    length, width = conved.shape
    share = w_own.shape[-1]
    rows = pl.BlockSpec((TILE, width), lambda g: (g, 0))
    qkv_rows = pl.BlockSpec((2, TILE, 3 * share), lambda g: (0, g, 0))
    low = jax.ShapeDtypeStruct((length, width), BF16)
    high = jax.ShapeDtypeStruct((length, width), F32)
    return pl.pallas_call(
        attend_kernel,
        out_shape=(jax.ShapeDtypeStruct((2, length, 3 * share), BF16), low, high, high, low, low),
        grid=(GROUPS,),
        in_specs=[
            rows,
            pl.BlockSpec((1, TILE, 1), lambda g: (g, 0, 0)),
            whole(w_own.shape),
            whole(w_other.shape),
            whole(o_own.shape),
            whole(o_other.shape),
            rows,
            rows,
            whole(mod.shape),
        ],
        out_specs=[qkv_rows, rows, rows, rows, rows, rows],
        compiler_params=params(),
        name="attend",
        cost_estimate=pl.CostEstimate(
            flops=8_000_000_000, bytes_accessed=30_000_000, transcendentals=3_200_000
        ),
    )(conved, valid, w_own, w_other, o_own, o_other, tok, cot, mod)


def gelu_pair(value):
    square = value * value
    inner = jnp.tanh(GELU_A * (value + GELU_B * (square * value)))
    cdf = 0.5 * (1.0 + inner)
    slope = cdf + (value * (0.5 * GELU_A)) * (1.0 - inner * inner) * (1.0 + (3.0 * GELU_B) * square)
    return value * cdf, slope


def ffn_kernel(
    idx, perm_ref, norm_ref, gdown_ref, up_ref, down_ref, kern_ref,
    up_keep, up_send, down_keep, down_send, kern_out, sum_out, gnorm_out,
    norm_t, gdown_t, grid_up, grid_gz, gact, active, gupper,
):
    width = norm_ref.shape[-1]
    chunk = up_ref.shape[-1]
    half_rows = up_keep.shape[0]
    first = pl.program_id(0) == 0

    @pl.when(first)
    def _():
        norm_t[...] = dot_nt(perm_ref[...], norm_ref[...]).astype(BF16)
        gdown_t[...] = dot_nt(perm_ref[...], gdown_ref[...]).astype(BF16)
        grid_up[...] = jnp.zeros(grid_up.shape, F32)
        grid_gz[...] = jnp.zeros(grid_gz.shape, F32)

    for block in range(chunk // TILE):
        cols = slice(block * TILE, (block + 1) * TILE)
        upper = dot(norm_ref[...], up_ref[:, cols])
        grads = dot(gdown_ref[...], down_ref[:, cols])
        for side in range(TILE // LANES):
            j = block * (TILE // LANES) + side
            lanes = slice(side * LANES, (side + 1) * LANES)
            gact[j] = grads[:, lanes]
            for group in range(GROUPS):
                for row in range(HALF):
                    at = group * TILE + row * HALF
                    grid_up[j, pl.ds(pad_row(group, row), HALF), :] = upper[at : at + HALF, lanes]

    def one_block(j, carry):
        lanes = pl.ds(pl.multiple_of(j * LANES, LANES), LANES)
        taps = taps_of(kern_ref, lanes)

        def forward(row, carry):
            found = neighbours(grid_up, j, row)
            for row_par in range(2):
                for col_par in range(2):
                    group = group_of(row_par, col_par)
                    out_row = pl.multiple_of(group * TILE + row * HALF, HALF)
                    act, slope = gelu_pair(conv_at(found, taps, row_par, col_par))
                    active[pl.ds(out_row, HALF), lanes] = act.astype(BF16)
                    grid_gz[j, pl.ds(row * PITCH + pad_row(group, 0), HALF), :] = (
                        gact[j, pl.ds(out_row, HALF), :] * slope
                    )
            return carry

        lax.fori_loop(0, HALF, forward, 0)

        def backward(row, sums):
            found = neighbours(grid_gz, j, row)
            for row_par in range(2):
                for col_par in range(2):
                    group = group_of(row_par, col_par)
                    out_row = pl.multiple_of(group * TILE + row * HALF, HALF)
                    source = grid_up[j, pl.ds(row * PITCH + pad_row(group, 0), HALF), :]
                    grad, sums = conv_back_at(found, taps, sums, source, row_par, col_par)
                    gupper[pl.ds(out_row, HALF), lanes] = grad.astype(BF16)
            return sums

        sums = lax.fori_loop(0, HALF, backward, no_sums())
        for tap in range(9):
            kern_out[tap : tap + 1, lanes] = jnp.sum(sums[tap], axis=0, keepdims=True)
        return carry

    lax.fori_loop(0, chunk // LANES, one_block, 0)

    mine = pl.multiple_of(idx[1] * half_rows, half_rows)
    theirs = pl.multiple_of((1 - idx[1]) * half_rows, half_rows)
    for block in range(chunk // TILE):
        cols = slice(block * TILE, (block + 1) * TILE)
        act = active[:, cols]
        gup = gupper[:, cols]
        down_send[:, cols] = dot(gdown_t[pl.ds(theirs, half_rows), :], act).astype(BF16)
        up_send[:, cols] = dot(norm_t[pl.ds(theirs, half_rows), :], gup).astype(BF16)
        down_keep[:, cols] = dot(gdown_t[pl.ds(mine, half_rows), :], act)
        up_keep[:, cols] = dot(norm_t[pl.ds(mine, half_rows), :], gup)
    for block in range(width // TILE):
        cols = slice(block * TILE, (block + 1) * TILE)
        part = dot_nt(active[...], down_ref[cols, :])
        gpart = dot_nt(gupper[...], up_ref[cols, :])

        @pl.when(first)
        def _(cols=cols, part=part, gpart=gpart):
            sum_out[:, cols] = part
            gnorm_out[:, cols] = gpart

        @pl.when(jnp.logical_not(first))
        def _(cols=cols, part=part, gpart=gpart):
            sum_out[:, cols] += part
            gnorm_out[:, cols] += gpart


def ffn_stage(idx, perm, normed, gdown, w_up, w_down, kern, chunk):
    length, width = normed.shape
    hidden = w_up.shape[-1]
    half_rows = width // 2
    cols = pl.BlockSpec((width, chunk), lambda i, idx: (0, i))
    half = pl.BlockSpec((half_rows, chunk), lambda i, idx: (0, i))
    small = pl.BlockSpec((9, chunk), lambda i, idx: (0, i))
    count = chunk // LANES
    keep = jax.ShapeDtypeStruct((half_rows, hidden), F32)
    send = jax.ShapeDtypeStruct((half_rows, hidden), BF16)
    full = jax.ShapeDtypeStruct((length, width), F32)
    return pl.pallas_call(
        ffn_kernel,
        out_shape=(keep, send, keep, send, jax.ShapeDtypeStruct((9, hidden), F32), full, full),
        grid_spec=pltpu.PrefetchScalarGridSpec(
            num_scalar_prefetch=1,
            grid=(hidden // chunk,),
            in_specs=[
                whole(perm.shape),
                whole(normed.shape),
                whole(gdown.shape),
                cols,
                cols,
                small,
            ],
            out_specs=[half, half, half, half, small, whole(full.shape), whole(full.shape)],
            scratch_shapes=[
                pltpu.VMEM((width, length), BF16),
                pltpu.VMEM((width, length), BF16),
                pltpu.VMEM((count, PAD_ROWS, LANES), F32),
                pltpu.VMEM((count, PAD_ROWS, LANES), F32),
                pltpu.VMEM((count, length, LANES), F32),
                pltpu.VMEM((length, chunk), BF16),
                pltpu.VMEM((length, chunk), BF16),
            ],
        ),
        compiler_params=params(),
        name="ffn",
        cost_estimate=pl.CostEstimate(
            flops=12 * length * width * hidden,
            bytes_accessed=4 * 1024 * 1024 * 6,
            transcendentals=length * hidden,
        ),
    )(idx, perm, normed, gdown, w_up, w_down, kern)


def middle_kernel(
    idx, perm_ref, res_ref, attn_ref, da_ref, db_ref, ga_ref, gb_ref, cot_ref, mixed_ref, oa_ref, ob_ref,
    mod_ref, out_ref, gres_out, gmix_out, sums_out, keep_out, send_out, ordered, total,
):
    share = oa_ref.shape[-1]
    width = res_ref.shape[-1]
    group = pl.program_id(0)
    residual = res_ref[...]
    cot = cot_ref[...].astype(F32)
    down = da_ref[...] + db_ref[...]
    result = residual + mod_ref[5:6, :] * down
    parity = (group // 2) * SIDE + lax.rem(group, 2)
    for row in range(HALF):
        for j in range(width // LANES):
            ordered[j, pl.ds(parity + row * 2 * SIDE, HALF, stride=2), :] = result[
                row * HALF : (row + 1) * HALF, j * LANES : (j + 1) * LANES
            ]
    grad_n = ga_ref[...] + gb_ref[...]
    normed, rstd = norm_rows(residual)
    scaled = grad_n * (1.0 + mod_ref[4:5, :])
    mean_a = jnp.mean(scaled, axis=-1, keepdims=True)
    mean_b = jnp.mean(scaled * normed, axis=-1, keepdims=True)
    gres = cot + rstd * (scaled - mean_a - normed * mean_b)
    gres_out[...] = gres
    sums = jnp.concatenate(
        [
            jnp.sum(gres * attn_ref[...], axis=0, keepdims=True),
            jnp.sum(grad_n, axis=0, keepdims=True),
            jnp.sum(grad_n * normed, axis=0, keepdims=True),
            jnp.sum(cot * down, axis=0, keepdims=True),
        ],
        axis=0,
    )
    gattn = (mod_ref[2:3, :] * gres).astype(BF16)
    gmix_out[:, :share] = dot(gattn, oa_ref[...]).astype(BF16)
    gmix_out[:, share:] = dot(gattn, ob_ref[...]).astype(BF16)
    part = dot(dot_nt(perm_ref[...], gattn).astype(BF16), mixed_ref[...])

    @pl.when(group == 0)
    def _():
        sums_out[...] = sums
        total[...] = part

    @pl.when(group > 0)
    def _():
        sums_out[...] += sums
        total[...] += part

    @pl.when(group == GROUPS - 1)
    def _():
        half_rows = width // 2
        keep_out[...] = total[pl.ds(pl.multiple_of(idx[1] * half_rows, half_rows), half_rows), :]
        send_out[...] = total[
            pl.ds(pl.multiple_of((1 - idx[1]) * half_rows, half_rows), half_rows), :
        ].astype(BF16)
        for j in range(width // LANES):
            out_ref[:, j * LANES : (j + 1) * LANES] = ordered[j].astype(BF16)


def middle_stage(idx, perm, res, attn, da, db, ga, gb, cot, mixed, o_own, o_other, mod):
    length, width = res.shape
    rows = pl.BlockSpec((TILE, width), lambda g, idx: (g, 0))
    half_rows = width // 2
    low = jax.ShapeDtypeStruct((length, width), BF16)
    return pl.pallas_call(
        middle_kernel,
        out_shape=(
            low,
            jax.ShapeDtypeStruct((length, width), F32),
            low,
            jax.ShapeDtypeStruct((4, width), F32),
            jax.ShapeDtypeStruct((half_rows, width), F32),
            jax.ShapeDtypeStruct((half_rows, width), BF16),
        ),
        grid_spec=pltpu.PrefetchScalarGridSpec(
            num_scalar_prefetch=1,
            grid=(GROUPS,),
            in_specs=[whole(perm.shape)]
            + [rows] * 8
            + [whole(o_own.shape), whole(o_other.shape), whole(mod.shape)],
            out_specs=[
                whole((length, width)),
                rows,
                rows,
                whole((4, width)),
                whole((half_rows, width)),
                whole((half_rows, width)),
            ],
            scratch_shapes=[
                pltpu.VMEM((width // LANES, length, LANES), F32),
                pltpu.VMEM((width, width), F32),
            ],
        ),
        compiler_params=params(),
        name="middle",
        cost_estimate=pl.CostEstimate(
            flops=4_000_000_000, bytes_accessed=32_000_000, transcendentals=0
        ),
    )(idx, perm, res, attn, da, db, ga, gb, cot, mixed, o_own, o_other, mod)


def attend_back_kernel(qkv_ref, gmix_ref, valid_ref, gqkv_out):
    share = qkv_ref.shape[-1] // 3
    keep = jnp.broadcast_to(valid_ref[0], (TILE, TILE)) > 0
    lane = lax.broadcasted_iota(jnp.int32, (TILE, LANES), 1)
    for side in range(2):
        for pair in range(share // LANES):
            lanes = [slice(t * share + pair * LANES, t * share + (pair + 1) * LANES) for t in range(3)]
            queries = qkv_ref[side, :, lanes[0]]
            keys = qkv_ref[side, :, lanes[1]]
            values = qkv_ref[side, :, lanes[2]]
            first = side * share + pair * LANES
            gmix = gmix_ref[:, first : first + LANES]
            keys_t = keys.astype(F32).T.astype(BF16)
            gq, gk, gv = [], [], []
            for which in range(2):
                probs = soft_keys(head_mask(keys, which), queries, keep)
                gprobs = dot_nt(head_mask(values, which), gmix)
                gv.append(dot(probs.astype(BF16), gmix))
                weighted = probs * gprobs
                gscores = weighted - probs * jnp.sum(weighted, axis=0, keepdims=True)
                graw = (gscores * (HEAD_DIM**-0.5)).astype(BF16)
                gk.append(dot(graw, queries))
                gq.append(dot(keys_t[which * HEAD_DIM : (which + 1) * HEAD_DIM], graw))
            gqkv_out[side, :, lanes[0]] = jnp.concatenate(gq, axis=0).T.astype(BF16)
            gqkv_out[side, :, lanes[1]] = jnp.where(lane < HEAD_DIM, gk[0], gk[1]).astype(BF16)
            gqkv_out[side, :, lanes[2]] = jnp.where(lane < HEAD_DIM, gv[0], gv[1]).astype(BF16)


def attend_back_stage(qkv, gmix, valid):
    length, width = gmix.shape
    rows = pl.BlockSpec((TILE, width), lambda g: (g, 0))
    qkv_rows = pl.BlockSpec((2, TILE, qkv.shape[-1]), lambda g: (0, g, 0))
    return pl.pallas_call(
        attend_back_kernel,
        out_shape=jax.ShapeDtypeStruct(qkv.shape, BF16),
        grid=(GROUPS,),
        in_specs=[qkv_rows, rows, pl.BlockSpec((1, TILE, 1), lambda g: (g, 0, 0))],
        out_specs=qkv_rows,
        compiler_params=params(),
        name="attend_back",
        cost_estimate=pl.CostEstimate(
            flops=12_000_000_000, bytes_accessed=12_000_000, transcendentals=3_200_000
        ),
    )(qkv, gmix, valid)


def qkv_grad_kernel(idx, perm_ref, conv_ref, gqkv_ref, keep_out, send_out, conv_t):
    @pl.when(pl.program_id(0) == 0)
    def _():
        conv_t[...] = dot_nt(perm_ref[...], conv_ref[...]).astype(BF16)

    half_rows = keep_out.shape[1]
    share = keep_out.shape[-1] // 3
    mine = pl.multiple_of(idx[1] * half_rows, half_rows)
    theirs = pl.multiple_of((1 - idx[1]) * half_rows, half_rows)
    for which in range(3):
        cols = slice(which * share, (which + 1) * share)
        grads = gqkv_ref[0, :, cols]
        send_out[0, :, cols] = dot(conv_t[pl.ds(theirs, half_rows), :], grads).astype(BF16)
        keep_out[0, :, cols] = dot(conv_t[pl.ds(mine, half_rows), :], grads)


def qkv_grad_stage(idx, perm, conved, gqkv):
    length, width = conved.shape
    cols = gqkv.shape[-1]
    half_rows = width // 2
    rows = pl.BlockSpec((1, half_rows, cols), lambda i, idx: (i, 0, 0))
    return pl.pallas_call(
        qkv_grad_kernel,
        out_shape=(
            jax.ShapeDtypeStruct((2, half_rows, cols), F32),
            jax.ShapeDtypeStruct((2, half_rows, cols), BF16),
        ),
        grid_spec=pltpu.PrefetchScalarGridSpec(
            num_scalar_prefetch=1,
            grid=(2,),
            in_specs=[
                whole(perm.shape),
                whole(conved.shape),
                pl.BlockSpec((1, length, cols), lambda i, idx: (i, 0, 0)),
            ],
            out_specs=[rows, rows],
            scratch_shapes=[pltpu.VMEM((width, length), BF16)],
        ),
        compiler_params=params(),
        name="qkv_grad",
        cost_estimate=pl.CostEstimate(
            flops=4_000_000_000, bytes_accessed=14_000_000, transcendentals=0
        ),
    )(idx, perm, conved, gqkv)


def last_kernel(
    gqkv_ref, wa_ref, wb_ref, tok_ref, gres_ref, mod_ref, kern_ref,
    gtok_out, sums_out, kern_out, grid_g, normed_s, grads_s, rstd_s,
):
    length, width = tok_ref.shape
    count = width // LANES
    share = wa_ref.shape[-1]
    grid_g[...] = jnp.zeros(grid_g.shape, F32)
    for block in range(width // TILE):
        rows = slice(block * TILE, (block + 1) * TILE)
        total = None
        for side, weight_ref in enumerate((wa_ref, wb_ref)):
            for which in range(3):
                part = dot_nt(
                    gqkv_ref[side, :, which * share : (which + 1) * share], weight_ref[which, rows, :]
                )
                total = part if total is None else total + part
        for side in range(TILE // LANES):
            j = block * (TILE // LANES) + side
            lanes = slice(side * LANES, (side + 1) * LANES)
            for group in range(GROUPS):
                for row in range(HALF):
                    at = group * TILE + row * HALF
                    grid_g[j, pl.ds(pad_row(group, row), HALF), :] = total[at : at + HALF, lanes]

    def one_norm(row, carry):
        at = pl.multiple_of(row * SIDE, SIDE)
        parts = split_lanes(tok_ref[pl.ds(at, SIDE), :].astype(F32))
        normed, rstd = norm_parts(parts)
        for j in range(count):
            normed_s[j, pl.ds(at, SIDE), :] = normed[j]
        rstd_s[pl.ds(at, SIDE), :] = jnp.broadcast_to(rstd, (SIDE, LANES))
        return carry

    lax.fori_loop(0, length // SIDE, one_norm, 0)

    for j in range(count):
        lanes = slice(j * LANES, (j + 1) * LANES)
        taps = taps_of(kern_ref, lanes)

        def backward(row, sums, j=j, lanes=lanes, taps=taps):
            found = neighbours(grid_g, j, row)
            for row_par in range(2):
                for col_par in range(2):
                    at = pl.multiple_of(group_of(row_par, col_par) * TILE + row * HALF, HALF)
                    source = normed_s[j, pl.ds(at, HALF), :] * (
                        1.0 + mod_ref[1:2, lanes]
                    ) + mod_ref[0:1, lanes]
                    grad, sums = conv_back_at(found, taps, sums, source, row_par, col_par)
                    grads_s[j, pl.ds(at, HALF), :] = grad
            return sums

        sums = lax.fori_loop(0, HALF, backward, no_sums())
        for tap in range(9):
            kern_out[tap : tap + 1, lanes] = jnp.sum(sums[tap], axis=0, keepdims=True)

    ordered = grid_g

    def one_back(row, carry):
        shifts, scales = carry
        shifts, scales = list(shifts), list(scales)
        for group in range(GROUPS):
            at = pl.multiple_of(group * TILE + row * HALF, HALF)
            normed = [normed_s[j, pl.ds(at, HALF), :] for j in range(count)]
            grads = [grads_s[j, pl.ds(at, HALF), :] for j in range(count)]
            rstd = rstd_s[pl.ds(at, HALF), :]
            scaled = []
            for j in range(count):
                lanes = slice(j * LANES, (j + 1) * LANES)
                prod = grads[j] * normed[j]
                shifts[j] = shifts[j] + (grads[j][:8] + grads[j][8:])
                scales[j] = scales[j] + (prod[:8] + prod[8:])
                scaled.append(grads[j] * (1.0 + mod_ref[1:2, lanes]))
            mixed = [scaled[j] * normed[j] for j in range(count)]
            mean_a = jnp.sum(sum(scaled[1:], scaled[0]), axis=-1, keepdims=True) * (1.0 / width)
            mean_b = jnp.sum(sum(mixed[1:], mixed[0]), axis=-1, keepdims=True) * (1.0 / width)
            start = (group // 2) * SIDE + group % 2
            for j in range(count):
                lanes = slice(j * LANES, (j + 1) * LANES)
                value = gres_ref[pl.ds(at, HALF), lanes] + rstd * (
                    scaled[j] - mean_a - normed[j] * mean_b
                )
                ordered[j, pl.ds(start + row * (2 * SIDE), HALF, stride=2), :] = value
        return tuple(shifts), tuple(scales)

    zero = tuple(jnp.zeros((8, LANES), F32) for _ in range(count))
    shifts, scales = lax.fori_loop(0, HALF, one_back, (zero, zero))
    for j in range(count):
        lanes = slice(j * LANES, (j + 1) * LANES)
        sums_out[0:1, lanes] = jnp.sum(shifts[j], axis=0, keepdims=True)
        sums_out[1:2, lanes] = jnp.sum(scales[j], axis=0, keepdims=True)
        gtok_out[:, lanes] = ordered[j, pl.ds(0, length), :].astype(BF16)


def last_stage(gqkv, w_own, w_other, tok, gres, mod, kern):
    length, width = tok.shape
    count = width // LANES
    operands = (gqkv, w_own, w_other, tok, gres, mod, kern)
    return pl.pallas_call(
        last_kernel,
        out_shape=(
            jax.ShapeDtypeStruct((length, width), BF16),
            jax.ShapeDtypeStruct((2, width), F32),
            jax.ShapeDtypeStruct((9, width), F32),
        ),
        grid=(1,),
        in_specs=[whole(each.shape) for each in operands],
        out_specs=[whole((length, width)), whole((2, width)), whole((9, width))],
        scratch_shapes=[
            pltpu.VMEM((count, PAD_ROWS, LANES), F32),
            pltpu.VMEM((count, length, LANES), F32),
            pltpu.VMEM((count, length, LANES), F32),
            pltpu.VMEM((length, LANES), F32),
        ],
        compiler_params=params(),
        name="conv_norm_back",
        cost_estimate=pl.CostEstimate(
            flops=4_000_000_000, bytes_accessed=16_000_000, transcendentals=0
        ),
    )(*operands)


def silu_of(values_in):
    return values_in * jax.nn.sigmoid(values_in)


def swap(values_in, axis, bit):
    size = lax.axis_size(axis)
    return lax.ppermute(values_in, axis, [(i, i ^ bit) for i in range(size)])


def spread(size, position):
    if size < 4:
        return position
    quarter = size // 4
    low, rest = position // (2 * quarter), position % (2 * quarter)
    return (rest % quarter) * 4 + (rest // quarter) * 2 + low


def row_permutation(size, width):
    block = width // size
    order = [spread(size, i // block) * block + i % block for i in range(width)]
    source = jnp.array(order, jnp.int32)
    return (source[:, None] == jnp.arange(width, dtype=jnp.int32)[None, :]).astype(BF16)


def halve(total, bit_set):
    rows = total.shape[0] // 2
    split = total.reshape((2, rows) + total.shape[1:])
    mine = lax.dynamic_index_in_dim(split, bit_set, 0, keepdims=False)
    theirs = lax.dynamic_index_in_dim(split, 1 - bit_set, 0, keepdims=False)
    return mine, theirs.astype(BF16)


def sum_rows(keep, send):
    size = lax.axis_size("dp")
    me = lax.axis_index("dp")
    total = keep + swap(send, "dp", 1).astype(F32)
    bits = [2]
    rest = size // 4
    while rest > 1:
        bits.append(rest * 2)
        rest //= 2
    for bit in bits:
        if bit >= size:
            continue
        mine, theirs = halve(total, (me // bit) % 2)
        total = mine + swap(theirs, "dp", bit).astype(F32)
    return total


def share_back(own, other):
    return own + swap(other.astype(BF16), "mp", 1).astype(F32)


def unshuffle(tokens_in):
    blocked = tokens_in.reshape(HALF, 2, HALF, 2)
    return blocked.transpose(1, 3, 0, 2).reshape(GROUPS, TILE)


def local(
    tokens,
    valid,
    steps,
    labels,
    w_mod,
    step_table,
    class_table,
    conv_attn,
    w_qkv,
    w_out,
    conv_ffn,
    w_up,
    w_down,
    cotangent,
):
    dp_size = lax.axis_size("dp")
    width = tokens.shape[-1]
    dp_at = lax.axis_index("dp")
    mp_at = lax.axis_index("mp")
    latent = dp_at * tokens.shape[0] + mp_at
    idx = jnp.stack([mp_at, dp_at % 2]).astype(jnp.int32)
    perm = row_permutation(dp_size, width)

    qkv_own = w_qkv.transpose(1, 0, 2)
    qkv_other = swap(qkv_own, "mp", 1)
    out_other = swap(w_out, "mp", 1)
    up_other = swap(w_up, "mp", 1)
    down_other = swap(w_down, "mp", 1)
    kern_other = swap(conv_ffn, "mp", 1)

    embedding = jnp.take(step_table, steps, axis=0).astype(F32) + jnp.take(
        class_table, labels, axis=0
    ).astype(F32)
    silu_value, silu_pull = jax.vjp(silu_of, embedding)
    silu_low = silu_value.astype(BF16)
    my_silu = lax.dynamic_slice_in_dim(silu_low, latent, 1)
    mod = jnp.dot(my_silu, w_mod, preferred_element_type=F32).reshape(6, width)

    my_valid = lax.dynamic_index_in_dim(valid, mp_at, 0, keepdims=False)
    keep = unshuffle(my_valid)[:, :, None]

    conved, tok, cot = first_stage(idx, tokens, cotangent, mod, conv_attn)
    qkv, mixed, attn, res, normed, gdown = attend_stage(
        conved, keep, qkv_own, qkv_other, w_out, out_other, tok, cot, mod
    )
    chunk = w_up.shape[-1] // 2
    first = ffn_stage(idx, perm, normed, gdown, w_up, w_down, conv_ffn, chunk)
    second = ffn_stage(idx, perm, normed, gdown, up_other, down_other, kern_other, chunk)
    output, gres, gmix, sums_mid, out_keep, out_send = middle_stage(
        idx, perm, res, attn, first[5], second[5], first[6], second[6], cot, mixed, w_out, out_other, mod
    )
    output_other = swap(output, "mp", 1)
    gqkv = attend_back_stage(qkv, gmix, keep)
    qkv_keep, qkv_send = qkv_grad_stage(idx, perm, conved, gqkv)
    gtok, sums_last, kern_a = last_stage(gqkv, qkv_own, qkv_other, tok, gres, mod, conv_attn)
    gtok_other = swap(gtok, "mp", 1)

    def both(mine, theirs):
        pair = jnp.stack([mine, theirs])
        return jnp.where(mp_at == 0, pair, pair[::-1])

    grad_up = share_back(sum_rows(first[0], first[1]), sum_rows(second[0], second[1]))
    grad_down = share_back(sum_rows(first[2], first[3]), sum_rows(second[2], second[3]))
    share = w_out.shape[-1]
    out_sum = sum_rows(out_keep, out_send)
    grad_out = share_back(out_sum[:, :share], out_sum[:, share:])
    qkv_own_sum = sum_rows(qkv_keep[0], qkv_send[0])
    qkv_other_sum = sum_rows(qkv_keep[1], qkv_send[1])
    grad_qkv = share_back(qkv_own_sum, qkv_other_sum)
    grad_qkv = grad_qkv.reshape(grad_qkv.shape[0], 3, share)

    kern_f = lax.psum(
        jnp.where(
            mp_at == 0,
            jnp.concatenate([first[4], second[4]], axis=1),
            jnp.concatenate([second[4], first[4]], axis=1),
        ),
        ("dp", "mp"),
    )
    kern_f = lax.dynamic_slice_in_dim(kern_f, mp_at * first[4].shape[1], first[4].shape[1], axis=1)
    kern_a = lax.psum(kern_a, ("dp", "mp"))

    grad_mod = jnp.concatenate(
        [sums_last[0:1], sums_last[1:2], sums_mid[0:1], sums_mid[1:2], sums_mid[2:3], sums_mid[3:4]],
        axis=0,
    )
    grad_mod_low = lax.all_gather(
        grad_mod.reshape(1, -1).astype(BF16), ("dp", "mp"), axis=0, tiled=True
    )
    rows = width // dp_size
    my_cols = lax.dynamic_slice_in_dim(silu_low, dp_at * rows, rows, axis=1)
    grad_w_mod = jnp.einsum("lk,lc->kc", my_cols, grad_mod_low, preferred_element_type=F32)
    grad_silu = jnp.einsum("lc,kc->lk", grad_mod_low, w_mod, preferred_element_type=F32)
    (grad_embedding,) = silu_pull(grad_silu)

    def table_grad(indices, count):
        onehot = (jnp.arange(count, dtype=jnp.int32)[:, None] == indices[None, :]).astype(F32)
        return jnp.dot(onehot, grad_embedding, precision=lax.Precision.HIGHEST)

    return (
        both(output, output_other),
        both(gtok, gtok_other),
        grad_w_mod,
        table_grad(steps, step_table.shape[0]),
        table_grad(labels, class_table.shape[0]),
        kern_a,
        grad_qkv,
        grad_out,
        kern_f,
        grad_up,
        grad_down,
    )


def solution(mesh):
    in_specs = (
        P("dp", None, None),
        P("dp", None),
        P(),
        P(),
        P(),
        P(),
        P(),
        P(),
        P(None, None, "mp"),
        P(None, "mp"),
        P(None, "mp"),
        P(None, "mp"),
        P(None, "mp"),
        P("dp", None, None),
    )
    out_specs = (
        P("dp", None, None),
        P("dp", None, None),
        P("dp", None),
        P(),
        P(),
        P(),
        P("dp", None, "mp"),
        P("dp", "mp"),
        P(None, "mp"),
        P("dp", "mp"),
        P("dp", "mp"),
    )
    return jax.shard_map(local, mesh=mesh, in_specs=in_specs, out_specs=out_specs, check_vma=False)
```

```python
from functools import partial

import jax
import jax.numpy as jnp
from jax import lax
from jax.experimental import pallas as pl
from jax.experimental.pallas import tpu as pltpu
from jax.sharding import PartitionSpec as P

SIDE = 32
HALF = SIDE // 2
HEAD_DIM = 64
GROUPS = 4
LANES = 128
TILE = 256
EPS = 1e-06
PITCH = HALF + 8
GROUP_ROWS = (HALF + 2) * PITCH + 8
PAD_ROWS = GROUPS * GROUP_ROWS
GELU_A = 0.7978845608028654
GELU_B = 0.044715
F32 = jnp.float32
BF16 = jnp.bfloat16
VMEM_BYTES = 60 * 1024 * 1024
SMALL_COST = pl.CostEstimate(flops=1000, bytes_accessed=1000, transcendentals=0)


def params(count=1):
    return pltpu.CompilerParams(
        dimension_semantics=("arbitrary",) * count, vmem_limit_bytes=VMEM_BYTES
    )


def whole(shape):
    zeros = (0,) * len(shape)
    return pl.BlockSpec(shape, lambda *_: zeros, pipeline_mode=pl.Buffered(1))


def leading(array, count):
    tail = array.shape[1:]
    return pl.BlockSpec((count,) + tail, lambda *_: (0,) * array.ndim, pipeline_mode=pl.Buffered(1))


def entry(array, which):
    tail = (0,) * (array.ndim - 1)
    return pl.BlockSpec(
        (None,) + array.shape[1:], lambda *_: (which,) + tail, pipeline_mode=pl.Buffered(1)
    )


def dot(left, right):
    return jnp.dot(left, right, preferred_element_type=F32)


def dot_nt(left, right):
    return lax.dot_general(left, right, (((1,), (1,)), ((), ())), preferred_element_type=F32)


def pad_row(group, row, shift=0):
    return group * GROUP_ROWS + (row + 1) * PITCH + 8 + shift


AROUND = ((1, -1), (0, 0), (1, 0), (0, 1))


def neighbours(grid_ref, lane_block, row):
    found = []
    for row_par, row_off in AROUND:
        line = []
        for col_par, col_off in AROUND:
            const = pad_row(row_par * 2 + col_par, row_off, col_off)
            line.append(grid_ref[lane_block, pl.ds(row * PITCH + const, HALF), :])
        found.append(line)
    return found


def taps_of(kern_ref, lanes):
    return [
        jnp.broadcast_to(kern_ref[tap : tap + 1, lanes].astype(F32), (HALF, LANES))
        for tap in range(9)
    ]


def conv_at(found, taps, row_par, col_par):
    total = None
    for row_off in range(3):
        for col_off in range(3):
            term = taps[row_off * 3 + col_off] * found[row_par + row_off][col_par + col_off]
            total = term if total is None else total + term
    return total


def conv_back_at(found, taps, sums, source, row_par, col_par):
    total = None
    sums = list(sums)
    for row_off in range(3):
        for col_off in range(3):
            tap = row_off * 3 + col_off
            near = found[row_par + 2 - row_off][col_par + 2 - col_off]
            term = taps[tap] * near
            total = term if total is None else total + term
            part = source * near
            sums[tap] = sums[tap] + (part[:8] + part[8:])
    return total, tuple(sums)


def no_sums():
    return tuple(jnp.zeros((8, LANES), F32) for _ in range(9))


def split_lanes(values_in):
    count = values_in.shape[-1] // LANES
    return [values_in[:, j * LANES : (j + 1) * LANES] for j in range(count)]


def norm_parts(parts):
    width = len(parts) * LANES
    mean = jnp.sum(sum(parts[1:], parts[0]), axis=-1, keepdims=True) * (1.0 / width)
    centre = [part - mean for part in parts]
    squares = [part * part for part in centre]
    var = jnp.sum(sum(squares[1:], squares[0]), axis=-1, keepdims=True) * (1.0 / width)
    rstd = lax.rsqrt(var + EPS)
    return [part * rstd for part in centre], rstd


def norm_rows(values_in):
    mean = jnp.mean(values_in, axis=-1, keepdims=True)
    centre = values_in - mean
    rstd = lax.rsqrt(jnp.mean(centre * centre, axis=-1, keepdims=True) + EPS)
    return centre * rstd, rstd


def modulation_kernel(silu_ref, weight_ref, mod_out):
    left = jnp.broadcast_to(silu_ref[...].astype(F32), (16, silu_ref.shape[-1])).astype(BF16)
    mod_out[pl.ds(pl.program_id(0), 1), :] = dot(left, weight_ref[...])[:1]


def modulation_stage(silu_low, w_mod):
    width = silu_low.shape[-1]
    return pl.pallas_call(
        modulation_kernel,
        out_shape=jax.ShapeDtypeStruct((w_mod.shape[-1] // width, width), F32),
        grid=(w_mod.shape[-1] // width,),
        in_specs=[whole(silu_low.shape), pl.BlockSpec((width, width), lambda i: (0, i))],
        out_specs=whole((w_mod.shape[-1] // width, width)),
        compiler_params=params(),
        name="modulation",
        cost_estimate=SMALL_COST,
    )(silu_low, w_mod)


def group_of(row_par, col_par):
    return row_par * 2 + col_par


def first_kernel(
    idx, tok_ref, cot_ref, mod_ref, kern_ref, conv_out, tok_out, cot_out, tok_tmp, cot_tmp, grid
):
    width = tok_ref.shape[-1]
    count = width // LANES
    grid[...] = jnp.zeros(grid.shape, F32)

    def one_row(row, carry):
        for row_par in range(2):
            start = pl.multiple_of((row * 2 + row_par) * SIDE, SIDE)
            values = tok_ref[0, pl.ds(start, SIDE), :].astype(F32)
            grads = cot_ref[0, pl.ds(start, SIDE), :].astype(F32)
            for j in range(count):
                tok_tmp[row_par, j] = values[:, j * LANES : (j + 1) * LANES]
                cot_tmp[row_par, j] = grads[:, j * LANES : (j + 1) * LANES]
            for col_par in range(2):
                group = group_of(row_par, col_par)
                out_row = pl.multiple_of(group * TILE + row * HALF, HALF)
                parts = [tok_tmp[row_par, j, pl.ds(col_par, HALF, stride=2), :] for j in range(count)]
                for j in range(count):
                    lanes = slice(j * LANES, (j + 1) * LANES)
                    tok_out[pl.ds(out_row, HALF), lanes] = parts[j].astype(BF16)
                    cot_out[pl.ds(out_row, HALF), lanes] = cot_tmp[
                        row_par, j, pl.ds(col_par, HALF, stride=2), :
                    ].astype(BF16)
                normed, _ = norm_parts(parts)
                for j in range(count):
                    lanes = slice(j * LANES, (j + 1) * LANES)
                    value = normed[j] * (1.0 + mod_ref[1:2, lanes]) + mod_ref[0:1, lanes]
                    grid[j, pl.ds(row * PITCH + pad_row(group, 0), HALF), :] = value
        return carry

    lax.fori_loop(0, HALF, one_row, 0)
    for j in range(count):
        lanes = slice(j * LANES, (j + 1) * LANES)
        taps = taps_of(kern_ref, lanes)

        def one_conv(row, carry, j=j, lanes=lanes, taps=taps):
            found = neighbours(grid, j, row)
            for row_par in range(2):
                for col_par in range(2):
                    out_row = pl.multiple_of(group_of(row_par, col_par) * TILE + row * HALF, HALF)
                    value = conv_at(found, taps, row_par, col_par)
                    conv_out[pl.ds(out_row, HALF), lanes] = value.astype(BF16)
            return carry

        lax.fori_loop(0, HALF, one_conv, 0)


def first_stage(idx, tokens, cotangent, mod, kern):
    _, length, width = tokens.shape
    shape = jax.ShapeDtypeStruct((length, width), BF16)
    mine = pl.BlockSpec((1, length, width), lambda i, idx: (idx[0], 0, 0))
    return pl.pallas_call(
        first_kernel,
        out_shape=(shape, shape, shape),
        grid_spec=pltpu.PrefetchScalarGridSpec(
            num_scalar_prefetch=1,
            grid=(1,),
            in_specs=[mine, mine, whole(mod.shape), whole(kern.shape)],
            out_specs=[whole((length, width))] * 3,
            scratch_shapes=[
                pltpu.VMEM((2, width // LANES, SIDE, LANES), F32),
                pltpu.VMEM((2, width // LANES, SIDE, LANES), F32),
                pltpu.VMEM((width // LANES, PAD_ROWS, LANES), F32),
            ],
        ),
        compiler_params=params(),
        name="norm_conv",
        cost_estimate=SMALL_COST,
    )(idx, tokens, cotangent, mod, kern)


def head_mask(values_in, which):
    lane = lax.broadcasted_iota(jnp.int32, values_in.shape, 1)
    keep = lane < HEAD_DIM if which == 0 else lane >= HEAD_DIM
    return jnp.where(keep, values_in, jnp.zeros_like(values_in))


def soft_keys(keys, queries, keep):
    raw = dot_nt(keys, queries)
    scores = jnp.where(keep, raw * (HEAD_DIM**-0.5), -1e30)
    exponent = jnp.exp(scores - jnp.max(scores, axis=0, keepdims=True))
    return exponent * (1.0 / jnp.sum(exponent, axis=0, keepdims=True))


def attend_heads(conved, keep, weight_ref, qkv_out, mixed_out):
    share = weight_ref.shape[-1]
    for which in range(3):
        qkv_out[:, which * share : (which + 1) * share] = dot(conved, weight_ref[which]).astype(BF16)
    for pair in range(share // LANES):
        lanes = [slice(t * share + pair * LANES, t * share + (pair + 1) * LANES) for t in range(3)]
        queries = qkv_out[:, lanes[0]]
        keys = qkv_out[:, lanes[1]]
        values_t = qkv_out[:, lanes[2]].astype(F32).T.astype(BF16)
        halves = []
        for which in range(2):
            probs = soft_keys(head_mask(keys, which), queries, keep).astype(BF16)
            halves.append(dot(values_t[which * HEAD_DIM : (which + 1) * HEAD_DIM], probs))
        mixed_out[:, pair * LANES : (pair + 1) * LANES] = jnp.concatenate(halves, axis=0).T.astype(BF16)


def attend_own_kernel(conv_ref, valid_ref, weight_ref, perm_ref, convt_out, qkv_out, mixed_out):
    conved = conv_ref[...]
    convt_out[...] = dot_nt(perm_ref[...], conved).astype(BF16)
    keep = jnp.broadcast_to(valid_ref[0], (TILE, TILE)) > 0
    attend_heads(conved, keep, weight_ref, qkv_out, mixed_out)


def attend_other_kernel(
    conv_ref, valid_ref, weight_ref, mown_ref, oa_ref, ob_ref, tok_ref, cot_ref, mod_ref,
    qkv_out, mixed_out, attn_out, res_out, norm_out, gdown_out,
):
    keep = jnp.broadcast_to(valid_ref[0], (TILE, TILE)) > 0
    attend_heads(conv_ref[...], keep, weight_ref, qkv_out, mixed_out)
    attn = dot_nt(mown_ref[...], oa_ref[...]) + dot_nt(mixed_out[...], ob_ref[...])
    attn_out[...] = attn
    residual = tok_ref[...].astype(F32) + mod_ref[2:3, :] * attn
    res_out[...] = residual
    normed, _ = norm_rows(residual)
    norm_out[...] = (normed * (1.0 + mod_ref[4:5, :]) + mod_ref[3:4, :]).astype(BF16)
    gdown_out[...] = (mod_ref[5:6, :] * cot_ref[...].astype(F32)).astype(BF16)


def group_rows(cols):
    return pl.BlockSpec((TILE, cols), lambda g: (g, 0))


def attend_own_stage(conved, valid, w_own, perm):
    length, width = conved.shape
    share = w_own.shape[-1]
    return pl.pallas_call(
        attend_own_kernel,
        out_shape=(
            jax.ShapeDtypeStruct((width, length), BF16),
            jax.ShapeDtypeStruct((length, 3 * share), BF16),
            jax.ShapeDtypeStruct((length, share), BF16),
        ),
        grid=(GROUPS,),
        in_specs=[
            group_rows(width),
            pl.BlockSpec((1, TILE, 1), lambda g: (g, 0, 0)),
            whole(w_own.shape),
            whole(perm.shape),
        ],
        out_specs=[
            pl.BlockSpec((width, TILE), lambda g: (0, g)),
            group_rows(3 * share),
            group_rows(share),
        ],
        compiler_params=params(),
        name="attend_own",
        cost_estimate=SMALL_COST,
    )(conved, valid, w_own, perm)


def attend_other_stage(conved, valid, other, mixed_own, o_own, tok, cot, mod):
    length, width = conved.shape
    share = other.shape[-1]
    low = jax.ShapeDtypeStruct((length, width), BF16)
    high = jax.ShapeDtypeStruct((length, width), F32)
    return pl.pallas_call(
        attend_other_kernel,
        out_shape=(
            jax.ShapeDtypeStruct((length, 3 * share), BF16),
            jax.ShapeDtypeStruct((length, share), BF16),
            high,
            high,
            low,
            low,
        ),
        grid=(GROUPS,),
        in_specs=[
            group_rows(width),
            pl.BlockSpec((1, TILE, 1), lambda g: (g, 0, 0)),
            leading(other, 3),
            group_rows(share),
            whole(o_own.shape),
            entry(other, 3),
            group_rows(width),
            group_rows(width),
            whole(mod.shape),
        ],
        out_specs=[group_rows(3 * share), group_rows(share)] + [group_rows(width)] * 4,
        compiler_params=params(),
        name="attend_other",
        cost_estimate=SMALL_COST,
    )(conved, valid, other, mixed_own, o_own, other, tok, cot, mod)


def gelu_pair(value):
    square = value * value
    inner = jnp.tanh(GELU_A * (value + GELU_B * (square * value)))
    cdf = 0.5 * (1.0 + inner)
    slope = cdf + (value * (0.5 * GELU_A)) * (1.0 - inner * inner) * (1.0 + (3.0 * GELU_B) * square)
    return value * cdf, slope


def ffn_kernel(split, *refs):
    idx, perm_ref, norm_ref, gdown_ref, up_ref, down_ref, kern_ref = refs[:7]
    grads_out = refs[7 : 9 if split else 8]
    kern_out, sum_out, gnorm_out = refs[len(grads_out) + 7 : len(grads_out) + 10]
    norm_t, gdown_t, grid_up, grid_gz, gact, active, gupper = refs[len(grads_out) + 10 :]
    width = norm_ref.shape[-1]
    chunk = up_ref.shape[-1]
    first = pl.program_id(0) == 0

    @pl.when(first)
    def _():
        norm_t[...] = dot_nt(perm_ref[...], norm_ref[...]).astype(BF16)
        gdown_t[...] = dot_nt(perm_ref[...], gdown_ref[...]).astype(BF16)
        grid_up[...] = jnp.zeros(grid_up.shape, F32)
        grid_gz[...] = jnp.zeros(grid_gz.shape, F32)

    for block in range(chunk // TILE):
        cols = slice(block * TILE, (block + 1) * TILE)
        upper = dot(norm_ref[...], up_ref[:, cols])
        grads = dot(gdown_ref[...], down_ref[:, cols])
        for side in range(TILE // LANES):
            j = block * (TILE // LANES) + side
            lanes = slice(side * LANES, (side + 1) * LANES)
            gact[j] = grads[:, lanes]
            for group in range(GROUPS):
                for row in range(HALF):
                    at = group * TILE + row * HALF
                    grid_up[j, pl.ds(pad_row(group, row), HALF), :] = upper[at : at + HALF, lanes]

    def one_block(j, carry):
        lanes = pl.ds(pl.multiple_of(j * LANES, LANES), LANES)
        taps = taps_of(kern_ref, lanes)

        def forward(row, carry):
            found = neighbours(grid_up, j, row)
            for row_par in range(2):
                for col_par in range(2):
                    group = group_of(row_par, col_par)
                    out_row = pl.multiple_of(group * TILE + row * HALF, HALF)
                    act, slope = gelu_pair(conv_at(found, taps, row_par, col_par))
                    active[pl.ds(out_row, HALF), lanes] = act.astype(BF16)
                    grid_gz[j, pl.ds(row * PITCH + pad_row(group, 0), HALF), :] = (
                        gact[j, pl.ds(out_row, HALF), :] * slope
                    )
            return carry

        lax.fori_loop(0, HALF, forward, 0)

        def backward(row, sums):
            found = neighbours(grid_gz, j, row)
            for row_par in range(2):
                for col_par in range(2):
                    group = group_of(row_par, col_par)
                    out_row = pl.multiple_of(group * TILE + row * HALF, HALF)
                    source = grid_up[j, pl.ds(row * PITCH + pad_row(group, 0), HALF), :]
                    grad, sums = conv_back_at(found, taps, sums, source, row_par, col_par)
                    gupper[pl.ds(out_row, HALF), lanes] = grad.astype(BF16)
            return sums

        sums = lax.fori_loop(0, HALF, backward, no_sums())
        for tap in range(9):
            kern_out[tap : tap + 1, lanes] = jnp.sum(sums[tap], axis=0, keepdims=True)
        return carry

    lax.fori_loop(0, chunk // LANES, one_block, 0)

    half_rows = width // 2
    mine = pl.multiple_of(idx[1] * half_rows, half_rows)
    theirs = pl.multiple_of((1 - idx[1]) * half_rows, half_rows)
    for block in range(chunk // TILE):
        cols = slice(block * TILE, (block + 1) * TILE)
        for which, (left, right) in enumerate(((norm_t, gupper), (gdown_t, active))):
            out_cols = slice(which * chunk + block * TILE, which * chunk + (block + 1) * TILE)
            if split:
                keep_out, send_out = grads_out
                send_out[:, out_cols] = dot(left[pl.ds(theirs, half_rows), :], right[:, cols]).astype(BF16)
                keep_out[:, out_cols] = dot(left[pl.ds(mine, half_rows), :], right[:, cols])
            else:
                grads_out[0][:, out_cols] = dot(left[...], right[:, cols]).astype(BF16)
    for block in range(width // TILE):
        cols = slice(block * TILE, (block + 1) * TILE)
        part = dot_nt(active[...], down_ref[cols, :])
        gpart = dot_nt(gupper[...], up_ref[cols, :])

        @pl.when(first)
        def _(cols=cols, part=part, gpart=gpart):
            sum_out[:, cols] = part
            gnorm_out[:, cols] = gpart

        @pl.when(jnp.logical_not(first))
        def _(cols=cols, part=part, gpart=gpart):
            sum_out[:, cols] += part
            gnorm_out[:, cols] += gpart


def ffn_stage(idx, perm, normed, gdown, weights, kern, chunk, split):
    length, width = normed.shape
    hidden = kern.shape[-1]
    if isinstance(weights, tuple):
        w_up, w_down = weights
        up_spec = down_spec = pl.BlockSpec((width, chunk), lambda i, idx: (0, i))
    else:
        w_up = w_down = weights
        up_spec = pl.BlockSpec((None, width, chunk), lambda i, idx: (0, 0, i))
        down_spec = pl.BlockSpec((None, width, chunk), lambda i, idx: (1, 0, i))
    small = pl.BlockSpec((9, chunk), lambda i, idx: (0, i))
    count = chunk // LANES
    full = jax.ShapeDtypeStruct((length, width), F32)
    rows = width // 2 if split else width
    grads = [jax.ShapeDtypeStruct((rows, 2 * hidden), BF16)]
    if split:
        grads.insert(0, jax.ShapeDtypeStruct((rows, 2 * hidden), F32))
    grads_spec = pl.BlockSpec((rows, 2 * chunk), lambda i, idx: (0, i))
    return pl.pallas_call(
        partial(ffn_kernel, split),
        out_shape=(*grads, jax.ShapeDtypeStruct((9, hidden), F32), full, full),
        grid_spec=pltpu.PrefetchScalarGridSpec(
            num_scalar_prefetch=1,
            grid=(hidden // chunk,),
            in_specs=[
                whole(perm.shape),
                whole(normed.shape),
                whole(gdown.shape),
                up_spec,
                down_spec,
                small,
            ],
            out_specs=[grads_spec] * len(grads) + [small, whole(full.shape), whole(full.shape)],
            scratch_shapes=[
                pltpu.VMEM((width, length), BF16),
                pltpu.VMEM((width, length), BF16),
                pltpu.VMEM((count, PAD_ROWS, LANES), F32),
                pltpu.VMEM((count, PAD_ROWS, LANES), F32),
                pltpu.VMEM((count, length, LANES), F32),
                pltpu.VMEM((length, chunk), BF16),
                pltpu.VMEM((length, chunk), BF16),
            ],
        ),
        compiler_params=params(),
        name="ffn",
        cost_estimate=SMALL_COST,
    )(idx, perm, normed, gdown, w_up, w_down, kern)


def middle_kernel(
    idx, perm_ref, res_ref, attn_ref, da_ref, db_ref, dc_ref, ga_ref, gb_ref, gc_ref, cot_ref, ma_ref, mb_ref,
    oa_ref, ob_ref, mod_ref, out_ref, gres_out, gmix_out, sums_out, keep_out, send_out, ordered, total,
):
    share = oa_ref.shape[-1]
    width = res_ref.shape[-1]
    group = pl.program_id(0)
    residual = res_ref[...]
    cot = cot_ref[...].astype(F32)
    down = (da_ref[...] + db_ref[...]) + dc_ref[...]
    result = residual + mod_ref[5:6, :] * down
    parity = (group // 2) * SIDE + lax.rem(group, 2)
    for row in range(HALF):
        for j in range(width // LANES):
            ordered[j, pl.ds(parity + row * 2 * SIDE, HALF, stride=2), :] = result[
                row * HALF : (row + 1) * HALF, j * LANES : (j + 1) * LANES
            ]
    grad_n = (ga_ref[...] + gb_ref[...]) + gc_ref[...]
    normed, rstd = norm_rows(residual)
    scaled = grad_n * (1.0 + mod_ref[4:5, :])
    mean_a = jnp.mean(scaled, axis=-1, keepdims=True)
    mean_b = jnp.mean(scaled * normed, axis=-1, keepdims=True)
    gres = cot + rstd * (scaled - mean_a - normed * mean_b)
    gres_out[...] = gres
    sums = jnp.concatenate(
        [
            jnp.sum(gres * attn_ref[...], axis=0, keepdims=True),
            jnp.sum(grad_n, axis=0, keepdims=True),
            jnp.sum(grad_n * normed, axis=0, keepdims=True),
            jnp.sum(cot * down, axis=0, keepdims=True),
        ],
        axis=0,
    )
    gattn = (mod_ref[2:3, :] * gres).astype(BF16)
    gmix_out[:, :share] = dot(gattn, oa_ref[...]).astype(BF16)
    gmix_out[:, share:] = dot(gattn, ob_ref[...]).astype(BF16)
    gattn_t = dot_nt(perm_ref[...], gattn).astype(BF16)
    part = jnp.concatenate([dot(gattn_t, ma_ref[...]), dot(gattn_t, mb_ref[...])], axis=1)

    @pl.when(group == 0)
    def _():
        sums_out[...] = sums
        total[...] = part

    @pl.when(group > 0)
    def _():
        sums_out[...] += sums
        total[...] += part

    @pl.when(group == GROUPS - 1)
    def _():
        half_rows = width // 2
        keep_out[...] = total[pl.ds(pl.multiple_of(idx[1] * half_rows, half_rows), half_rows), :]
        send_out[...] = total[
            pl.ds(pl.multiple_of((1 - idx[1]) * half_rows, half_rows), half_rows), :
        ].astype(BF16)
        for j in range(width // LANES):
            out_ref[:, j * LANES : (j + 1) * LANES] = ordered[j].astype(BF16)


def middle_stage(idx, perm, res, attn, downs, gnorms, cot, mixed, o_own, other, mod):
    half = pl.BlockSpec((TILE, o_own.shape[-1]), lambda g, idx: (g, 0))
    length, width = res.shape
    rows = pl.BlockSpec((TILE, width), lambda g, idx: (g, 0))
    half_rows = width // 2
    low = jax.ShapeDtypeStruct((length, width), BF16)
    return pl.pallas_call(
        middle_kernel,
        out_shape=(
            low,
            jax.ShapeDtypeStruct((length, width), F32),
            low,
            jax.ShapeDtypeStruct((4, width), F32),
            jax.ShapeDtypeStruct((half_rows, width), F32),
            jax.ShapeDtypeStruct((half_rows, width), BF16),
        ),
        grid_spec=pltpu.PrefetchScalarGridSpec(
            num_scalar_prefetch=1,
            grid=(GROUPS,),
            in_specs=[whole(perm.shape)]
            + [rows] * 9
            + [half] * 2
            + [whole(o_own.shape), entry(other, 3), whole(mod.shape)],
            out_specs=[
                whole((length, width)),
                rows,
                rows,
                whole((4, width)),
                whole((half_rows, width)),
                whole((half_rows, width)),
            ],
            scratch_shapes=[
                pltpu.VMEM((width // LANES, length, LANES), F32),
                pltpu.VMEM((width, width), F32),
            ],
        ),
        compiler_params=params(),
        name="middle",
        cost_estimate=SMALL_COST,
    )(idx, perm, res, attn, *downs, *gnorms, cot, *mixed, o_own, other, mod)


def attend_back_kernel(qkv_ref, gmix_ref, valid_ref, gqkv_out):
    share = qkv_ref.shape[-1] // 3
    keep = jnp.broadcast_to(valid_ref[0], (TILE, TILE)) > 0
    lane = lax.broadcasted_iota(jnp.int32, (TILE, LANES), 1)
    for pair in range(share // LANES):
        lanes = [slice(t * share + pair * LANES, t * share + (pair + 1) * LANES) for t in range(3)]
        queries = qkv_ref[:, lanes[0]]
        keys = qkv_ref[:, lanes[1]]
        values = qkv_ref[:, lanes[2]]
        gmix = gmix_ref[:, pair * LANES : (pair + 1) * LANES]
        keys_t = keys.astype(F32).T.astype(BF16)
        gq, gk, gv = [], [], []
        for which in range(2):
            probs = soft_keys(head_mask(keys, which), queries, keep)
            gprobs = dot_nt(head_mask(values, which), gmix)
            gv.append(dot(probs.astype(BF16), gmix))
            weighted = probs * gprobs
            gscores = weighted - probs * jnp.sum(weighted, axis=0, keepdims=True)
            graw = (gscores * (HEAD_DIM**-0.5)).astype(BF16)
            gk.append(dot(graw, queries))
            gq.append(dot(keys_t[which * HEAD_DIM : (which + 1) * HEAD_DIM], graw))
        gqkv_out[:, lanes[0]] = jnp.concatenate(gq, axis=0).T.astype(BF16)
        gqkv_out[:, lanes[1]] = jnp.where(lane < HEAD_DIM, gk[0], gk[1]).astype(BF16)
        gqkv_out[:, lanes[2]] = jnp.where(lane < HEAD_DIM, gv[0], gv[1]).astype(BF16)


def attend_back_stage(qkv, gmix, valid, side):
    length = gmix.shape[0]
    cols = qkv.shape[-1]
    return pl.pallas_call(
        attend_back_kernel,
        out_shape=jax.ShapeDtypeStruct((length, cols), BF16),
        grid=(GROUPS,),
        in_specs=[
            group_rows(cols),
            pl.BlockSpec((TILE, cols // 3), lambda g: (g, side)),
            pl.BlockSpec((1, TILE, 1), lambda g: (g, 0, 0)),
        ],
        out_specs=pl.BlockSpec((TILE, cols), lambda g: (g, 0)),
        compiler_params=params(),
        name="attend_back",
        cost_estimate=SMALL_COST,
    )(qkv, gmix, valid)


def qkv_grad_kernel(idx, conv_ref, gqkv_ref, okeep_ref, osend_ref, keep_out, send_out):
    half_rows = keep_out.shape[0]
    share = okeep_ref.shape[-1]
    mine = pl.multiple_of(idx[1] * half_rows, half_rows)
    theirs = pl.multiple_of((1 - idx[1]) * half_rows, half_rows)
    for which in range(3):
        cols = slice(which * share, (which + 1) * share)
        grads = gqkv_ref[:, cols]
        send_out[:, cols] = dot(conv_ref[pl.ds(theirs, half_rows), :], grads).astype(BF16)
        keep_out[:, cols] = dot(conv_ref[pl.ds(mine, half_rows), :], grads)
    keep_out[:, 3 * share :] = okeep_ref[...]
    send_out[:, 3 * share :] = osend_ref[...]


def qkv_grad_stage(idx, conv_t, gqkv, out_keep, out_send, side):
    width = conv_t.shape[0]
    half_rows = width // 2
    share = gqkv.shape[-1] // 3
    shape = (half_rows, 4 * share)
    part = pl.BlockSpec((half_rows, share), lambda i, idx: (0, side))
    return pl.pallas_call(
        qkv_grad_kernel,
        out_shape=(jax.ShapeDtypeStruct(shape, F32), jax.ShapeDtypeStruct(shape, BF16)),
        grid_spec=pltpu.PrefetchScalarGridSpec(
            num_scalar_prefetch=1,
            grid=(1,),
            in_specs=[whole(conv_t.shape), whole(gqkv.shape), part, part],
            out_specs=[whole(shape), whole(shape)],
        ),
        compiler_params=params(),
        name="qkv_grad",
        cost_estimate=SMALL_COST,
    )(idx, conv_t, gqkv, out_keep, out_send)


def conv_back_kernel(
    ga_ref, gb_ref, wa_ref, wb_ref, tok_ref, mod_ref, kern_ref,
    grads_out, kern_out, sums_out, grid_g, normed_s,
):
    length, width = tok_ref.shape
    count = width // LANES
    share = wa_ref.shape[-1]
    grid_g[...] = jnp.zeros(grid_g.shape, F32)
    for block in range(width // TILE):
        rows = slice(block * TILE, (block + 1) * TILE)
        total = None
        for grads_ref, weight_ref in ((ga_ref, wa_ref), (gb_ref, wb_ref)):
            for which in range(3):
                part = dot_nt(
                    grads_ref[:, which * share : (which + 1) * share], weight_ref[which, rows, :]
                )
                total = part if total is None else total + part
        for side in range(TILE // LANES):
            j = block * (TILE // LANES) + side
            lanes = slice(side * LANES, (side + 1) * LANES)
            for group in range(GROUPS):
                for row in range(HALF):
                    at = group * TILE + row * HALF
                    grid_g[j, pl.ds(pad_row(group, row), HALF), :] = total[at : at + HALF, lanes]

    def one_norm(row, carry):
        at = pl.multiple_of(row * SIDE, SIDE)
        normed, _ = norm_parts(split_lanes(tok_ref[pl.ds(at, SIDE), :].astype(F32)))
        for j in range(count):
            normed_s[j, pl.ds(at, SIDE), :] = normed[j]
        return carry

    lax.fori_loop(0, length // SIDE, one_norm, 0)

    for j in range(count):
        lanes = slice(j * LANES, (j + 1) * LANES)
        taps = taps_of(kern_ref, lanes)

        scale, shift = 1.0 + mod_ref[1:2, lanes], mod_ref[0:1, lanes]

        def backward(row, carry, j=j, lanes=lanes, taps=taps, scale=scale, shift=shift):
            sums, (shift_sum, scale_sum) = carry
            found = neighbours(grid_g, j, row)
            for row_par in range(2):
                for col_par in range(2):
                    at = pl.multiple_of(group_of(row_par, col_par) * TILE + row * HALF, HALF)
                    normed = normed_s[j, pl.ds(at, HALF), :]
                    grad, sums = conv_back_at(found, taps, sums, normed * scale + shift, row_par, col_par)
                    grads_out[pl.ds(at, HALF), lanes] = grad
                    prod = grad * normed
                    shift_sum = shift_sum + (grad[:8] + grad[8:])
                    scale_sum = scale_sum + (prod[:8] + prod[8:])
            return sums, (shift_sum, scale_sum)

        zero = jnp.zeros((8, LANES), F32)
        sums, pair = lax.fori_loop(0, HALF, backward, (no_sums(), (zero, zero)))
        for which in range(2):
            sums_out[which : which + 1, lanes] = jnp.sum(pair[which], axis=0, keepdims=True)
        for tap in range(9):
            kern_out[tap : tap + 1, lanes] = jnp.sum(sums[tap], axis=0, keepdims=True)


def conv_back_stage(g_own, g_other, w_own, other, tok, mod, kern):
    length, width = tok.shape
    count = width // LANES
    operands = (g_own, g_other, w_own, other, tok, mod, kern)
    return pl.pallas_call(
        conv_back_kernel,
        out_shape=(
            jax.ShapeDtypeStruct((length, width), F32),
            jax.ShapeDtypeStruct((9, width), F32),
            jax.ShapeDtypeStruct((2, width), F32),
        ),
        grid=(1,),
        in_specs=[leading(each, 3) if each is other else whole(each.shape) for each in operands],
        out_specs=[whole((length, width)), whole((9, width)), whole((2, width))],
        scratch_shapes=[
            pltpu.VMEM((count, PAD_ROWS, LANES), F32),
            pltpu.VMEM((count, length, LANES), F32),
        ],
        compiler_params=params(),
        name="conv_back",
        cost_estimate=SMALL_COST,
    )(*operands)


def norm_back_kernel(grads_ref, tok_ref, gres_ref, mod_ref, gtok_out, ordered):
    width = tok_ref.shape[-1]
    group = pl.program_id(0)
    grads = grads_ref[...]
    normed, rstd = norm_rows(tok_ref[...].astype(F32))
    scaled = grads * (1.0 + mod_ref[1:2, :])
    mean_a = jnp.mean(scaled, axis=-1, keepdims=True)
    mean_b = jnp.mean(scaled * normed, axis=-1, keepdims=True)
    result = gres_ref[...] + rstd * (scaled - mean_a - normed * mean_b)
    parity = (group // 2) * SIDE + lax.rem(group, 2)
    for row in range(HALF):
        for j in range(width // LANES):
            ordered[j, pl.ds(parity + row * 2 * SIDE, HALF, stride=2), :] = result[
                row * HALF : (row + 1) * HALF, j * LANES : (j + 1) * LANES
            ]

    @pl.when(group == GROUPS - 1)
    def _():
        for j in range(width // LANES):
            gtok_out[:, j * LANES : (j + 1) * LANES] = ordered[j].astype(BF16)


def norm_back_stage(grads, tok, gres, mod):
    length, width = tok.shape
    return pl.pallas_call(
        norm_back_kernel,
        out_shape=jax.ShapeDtypeStruct((length, width), BF16),
        grid=(GROUPS,),
        in_specs=[group_rows(width), group_rows(width), group_rows(width), whole(mod.shape)],
        out_specs=whole((length, width)),
        scratch_shapes=[pltpu.VMEM((width // LANES, length, LANES), F32)],
        compiler_params=params(),
        name="norm_back",
        cost_estimate=SMALL_COST,
    )(grads, tok, gres, mod)


def silu_of(values_in):
    return values_in * jax.nn.sigmoid(values_in)


def swap(values_in, axis, bit):
    size = lax.axis_size(axis)
    return lax.ppermute(values_in, axis, [(i, i ^ bit) for i in range(size)])


def spread(size, position):
    if size < 4:
        return position
    quarter = size // 4
    low, rest = position // (2 * quarter), position % (2 * quarter)
    return (rest % quarter) * 4 + (rest // quarter) * 2 + low


def row_permutation(size, width):
    block = width // size
    order = [spread(size, i // block) * block + i % block for i in range(width)]
    source = jnp.array(order, jnp.int32)
    return (source[:, None] == jnp.arange(width, dtype=jnp.int32)[None, :]).astype(BF16)


def tie(values_in, *first):
    return lax.optimization_barrier((values_in, first))[0]


def halving_bits(size):
    bits = [2] if size > 2 else []
    rest = size // 4
    while rest > 1:
        bits.append(rest * 2)
        rest //= 2
    return bits


def unshuffle(tokens_in):
    blocked = tokens_in.reshape(HALF, 2, HALF, 2)
    return blocked.transpose(1, 3, 0, 2).reshape(GROUPS, TILE)


def local(
    tokens,
    valid,
    steps,
    labels,
    w_mod,
    step_table,
    class_table,
    conv_attn,
    w_qkv,
    w_out,
    conv_ffn,
    w_up,
    w_down,
    cotangent,
):
    dp_size = lax.axis_size("dp")
    width = tokens.shape[-1]
    dp_at = lax.axis_index("dp")
    mp_at = lax.axis_index("mp")
    latent = dp_at * tokens.shape[0] + mp_at
    idx = jnp.stack([mp_at, dp_at % 2]).astype(jnp.int32)
    perm = row_permutation(dp_size, width)

    core = dp_at % 2
    half_rows = width // 2
    hidden = w_up.shape[-1]
    chunk = hidden // 2
    share = w_out.shape[-1]
    rows = width // dp_size
    bits = halving_bits(dp_size)

    def split_rows(total, bit):
        rows = total.shape[-2] // 2
        parts = total.reshape(total.shape[:-2] + (2, rows) + total.shape[-1:])
        axis = parts.ndim - 3
        flag = (dp_at // bit) % 2
        mine = lax.dynamic_index_in_dim(parts, flag, axis, keepdims=False)
        theirs = lax.dynamic_index_in_dim(parts, 1 - flag, axis, keepdims=False)
        return mine, theirs.astype(BF16)

    def ordered_pair(first, second, axis):
        return jnp.concatenate(
            [jnp.where(core == 0, first, second), jnp.where(core == 0, second, first)], axis=axis
        )

    def both(mine, theirs):
        place = lax.broadcasted_iota(jnp.int32, (2,) + mine.shape, 0)
        return jnp.where(place == mp_at, mine[None], theirs[None])

    qkv_own = w_qkv.transpose(1, 0, 2)
    stack = jnp.concatenate([qkv_own, w_out[None]], axis=0)
    part_a = swap(lax.dynamic_slice_in_dim(stack, core * half_rows, half_rows, axis=1), "mp", 1)
    kern_other = swap(conv_ffn, "mp", 1)

    embedding = jnp.take(step_table, steps, axis=0).astype(F32) + jnp.take(
        class_table, labels, axis=0
    ).astype(F32)
    silu_value, silu_pull = jax.vjp(silu_of, embedding)
    silu_low = silu_value.astype(BF16)
    my_silu = lax.dynamic_slice_in_dim(silu_low, latent, 1)
    mod = modulation_stage(my_silu, w_mod)

    my_valid = lax.dynamic_index_in_dim(valid, mp_at, 0, keepdims=False)
    keep = unshuffle(my_valid)[:, :, None]

    conved, tok, cot = first_stage(idx, tokens, cotangent, mod, conv_attn)
    conv_t, qkv_x, mixed_x = attend_own_stage(conved, keep, qkv_own, perm)

    part_a = tie(part_a, mixed_x)
    part_b = swap(part_a, "dp", 1)
    up_part, down_part = tie((w_up, w_down), part_a)
    ffn_part = jnp.stack(
        [
            lax.dynamic_slice_in_dim(up_part, core * chunk, chunk, axis=1),
            lax.dynamic_slice_in_dim(down_part, core * chunk, chunk, axis=1),
        ]
    )
    ffn_a = swap(ffn_part, "mp", 1)
    other = ordered_pair(part_a, part_b, 1)
    qkv_y, mixed_y, attn, res, normed, gdown = attend_other_stage(
        tie(conved, ffn_part), keep, other, mixed_x, w_out, tok, cot, mod
    )

    plain = jnp.eye(width, dtype=BF16)
    grads_x, kern_x, down_x, gnorm_x = ffn_stage(
        idx, plain, normed, gdown, (w_up, w_down), conv_ffn, chunk, False
    )
    sum_x = lax.psum_scatter(grads_x, "dp", scatter_dimension=0, tiled=True)
    ffn_a = tie(ffn_a, down_x)
    ffn_b = swap(ffn_a, "dp", 1)
    kern_part = lax.dynamic_slice_in_dim(kern_other, core * chunk, chunk, axis=1)
    keep_y, send_y, kern_y, down_y, gnorm_y = ffn_stage(
        idx, perm, normed, gdown, ffn_a, kern_part, chunk, True
    )
    got_y = swap(send_y, "dp", 1)
    kern_part = lax.dynamic_slice_in_dim(kern_other, (1 - core) * chunk, chunk, axis=1)
    keep_z, send_z, kern_z, down_z, gnorm_z = ffn_stage(
        idx, perm, tie(normed, down_y), gdown, ffn_b, kern_part, chunk, True
    )
    got_z = swap(send_z, "dp", 1)
    output, gres, gmix, sums_mid, out_keep, out_send = middle_stage(
        idx, perm, res, attn, (down_x, down_y, down_z), (gnorm_x, gnorm_y, tie(gnorm_z, got_y)),
        cot, (mixed_x, mixed_y), w_out, other, mod,
    )
    got_y, got_z = tie((got_y, got_z), gmix)
    total_f = jnp.stack([keep_y + got_z.astype(F32), keep_z + got_y.astype(F32)])
    mine_f, theirs = split_rows(total_f, bits[0])
    got_f = swap(theirs, "dp", bits[0])
    gmix = tie(gmix, theirs)
    output_other = swap(tie(output, theirs), "mp", 1)

    g_other = attend_back_stage(qkv_y, gmix, keep, 1)
    c_keep, c_send = qkv_grad_stage(idx, conv_t, g_other, out_keep, out_send, 1)
    c_got = swap(c_send, "dp", 1)
    g_own = attend_back_stage(qkv_x, tie(gmix, c_send), keep, 0)
    c_got, got_f = tie((c_got, got_f), g_own)
    total_c = (c_keep + c_got.astype(F32)).astype(BF16)
    from_x = swap(total_c, "mp", 1)
    total_f = mine_f + got_f.astype(F32)
    mine_f, theirs = split_rows(total_f, bits[1])
    got_f = swap(theirs, "dp", bits[1])
    d_keep, d_send = qkv_grad_stage(
        idx, conv_t, tie(g_own, total_c, theirs), out_keep, out_send, 0
    )
    d_got = swap(d_send, "dp", 1)
    whole_output = both(output, output_other)
    grads, kern_a, sums_last = conv_back_stage(
        tie(g_own, d_send, whole_output), g_other, qkv_own, other, tok, mod, conv_attn
    )

    d_got, from_x, got_f = tie((d_got, from_x, got_f), grads)
    total_d = d_keep + d_got.astype(F32) + from_x.astype(F32)
    mine_d, theirs = split_rows(total_d, bits[0])
    got_d = swap(theirs, "dp", bits[0])
    total_f = mine_f + got_f.astype(F32)
    mine_f, theirs_f = split_rows(total_f, bits[2])
    got_f = swap(theirs_f, "dp", bits[2])

    kern_there = ordered_pair(kern_y, kern_z, 1)
    sent = jnp.concatenate([kern_there.reshape(-1, width), kern_a], axis=0)
    held = jnp.concatenate([kern_x.reshape(-1, width), kern_a], axis=0)
    grad_mod = jnp.concatenate([sums_last, sums_mid], axis=0)
    mine = grad_mod.reshape(1, -1).astype(BF16)
    mod_there, held_there = swap(mine, "mp", 1), swap(sent, "mp", 1)
    gtok = norm_back_stage(tie(grads, theirs, theirs_f, mine, sent), tok, gres, mod)

    gtok_other = swap(tie(gtok, mod_there, held_there), "mp", 1)
    got_f, got_d, mod_there, held_there = tie((got_f, got_d, mod_there, held_there), gtok)
    total_f = mine_f + got_f.astype(F32)
    for bit in bits[3:]:
        mine_f, theirs = split_rows(total_f, bit)
        total_f = mine_f + swap(theirs, "dp", bit).astype(F32)
    from_f = swap(total_f.astype(BF16), "mp", 1)
    total_d = mine_d + got_d.astype(F32)
    for bit in bits[1:]:
        mine_d, theirs = split_rows(total_d, bit)
        total_d = mine_d + swap(theirs, "dp", bit).astype(F32)
    grad_qkv = total_d[:, : 3 * share].reshape(rows, 3, share)
    grad_out = total_d[:, 3 * share :]
    from_f = from_f.reshape(2, rows, 2 * chunk)
    from_f = jnp.where(core == 0, from_f, from_f[::-1]).astype(F32)
    both_ffn = sum_x.reshape(rows, 2, 2, chunk).transpose(2, 1, 0, 3).astype(F32) + from_f.reshape(
        2, rows, 2, chunk
    ).transpose(2, 0, 1, 3)
    grad_up = both_ffn[0].transpose(1, 0, 2).reshape(rows, hidden)
    grad_down = both_ffn[1].transpose(1, 0, 2).reshape(rows, hidden)

    gathered = jnp.concatenate([mine, mod_there], axis=0)
    held = held + held_there
    step = 1
    while step < dp_size:
        if 4 * step <= dp_size:
            others = [swap(gathered, "dp", step * by) for by in (1, 2, 3)]
            gathered = jnp.concatenate([gathered, *others], axis=0)
            step *= 4
        else:
            gathered = jnp.concatenate([gathered, swap(gathered, "dp", step)], axis=0)
            step *= 2
    step = 1
    while step < dp_size:
        held = held + swap(held, "dp", step)
        step *= 2
    kern_f = held[:-9].reshape(9, hidden)
    kern_a = held[-9:]
    latents = steps.shape[0]
    order = jnp.arange(latents, dtype=jnp.int32) ^ latent.astype(jnp.int32)
    sort = (order[None, :] == jnp.arange(latents, dtype=jnp.int32)[:, None]).astype(BF16)
    grad_mod_low = jnp.dot(sort, gathered, preferred_element_type=F32).astype(BF16)

    my_cols = lax.dynamic_slice_in_dim(silu_low, dp_at * rows, rows, axis=1)
    grad_w_mod = jnp.einsum("lk,lc->kc", my_cols, grad_mod_low, preferred_element_type=F32)
    grad_silu = jnp.einsum("lc,kc->lk", grad_mod_low, w_mod, preferred_element_type=F32)
    (grad_embedding,) = silu_pull(grad_silu)

    def table_grad(indices, count):
        onehot = (jnp.arange(count, dtype=jnp.int32)[:, None] == indices[None, :]).astype(F32)
        return jnp.dot(onehot, grad_embedding, precision=lax.Precision.HIGHEST)

    return (
        whole_output,
        both(gtok, gtok_other),
        grad_w_mod,
        table_grad(steps, step_table.shape[0]),
        table_grad(labels, class_table.shape[0]),
        kern_a,
        grad_qkv,
        grad_out,
        kern_f,
        grad_up,
        grad_down,
    )


def solution(mesh):
    in_specs = (
        P("dp", None, None),
        P("dp", None),
        P(),
        P(),
        P(),
        P(),
        P(),
        P(),
        P(None, None, "mp"),
        P(None, "mp"),
        P(None, "mp"),
        P(None, "mp"),
        P(None, "mp"),
        P("dp", None, None),
    )
    out_specs = (
        P("dp", None, None),
        P("dp", None, None),
        P("dp", None),
        P(),
        P(),
        P(),
        P("dp", None, "mp"),
        P("dp", "mp"),
        P(None, "mp"),
        P("dp", "mp"),
        P("dp", "mp"),
    )
    return jax.shard_map(local, mesh=mesh, in_specs=in_specs, out_specs=out_specs, check_vma=False)
```

```python
from functools import partial

import jax
import jax.numpy as jnp
from jax import lax
from jax.experimental import pallas as pl
from jax.experimental.pallas import tpu as pltpu
from jax.sharding import PartitionSpec as P

SIDE = 32
HALF = SIDE // 2
HEAD_DIM = 64
GROUPS = 4
LANES = 128
TILE = 256
EPS = 1e-06
PITCH = HALF + 8
GROUP_ROWS = (HALF + 2) * PITCH + 8
PAD_ROWS = GROUPS * GROUP_ROWS
GELU_A = 0.7978845608028654
GELU_B = 0.044715
F32 = jnp.float32
BF16 = jnp.bfloat16
VMEM_BYTES = 60 * 1024 * 1024


def cost(micros):
    return pl.CostEstimate(flops=int(micros * COST_RATE), bytes_accessed=1000, transcendentals=0)


COST_RATE = 400_000_000


def params(count=1):
    return pltpu.CompilerParams(
        dimension_semantics=("arbitrary",) * count, vmem_limit_bytes=VMEM_BYTES
    )


def whole(shape):
    zeros = (0,) * len(shape)
    return pl.BlockSpec(shape, lambda *_: zeros, pipeline_mode=pl.Buffered(1))


def leading(array, count):
    tail = array.shape[1:]
    return pl.BlockSpec((count,) + tail, lambda *_: (0,) * array.ndim, pipeline_mode=pl.Buffered(1))


def entry(array, which):
    tail = (0,) * (array.ndim - 1)
    return pl.BlockSpec(
        (None,) + array.shape[1:], lambda *_: (which,) + tail, pipeline_mode=pl.Buffered(1)
    )


def dot(left, right):
    return jnp.dot(left, right, preferred_element_type=F32)


def dot_nt(left, right):
    return lax.dot_general(left, right, (((1,), (1,)), ((), ())), preferred_element_type=F32)


def pad_row(group, row, shift=0):
    return group * GROUP_ROWS + (row + 1) * PITCH + 8 + shift


AROUND = ((1, -1), (0, 0), (1, 0), (0, 1))


def neighbours(grid_ref, lane_block, row):
    found = []
    for row_par, row_off in AROUND:
        line = []
        for col_par, col_off in AROUND:
            const = pad_row(row_par * 2 + col_par, row_off, col_off)
            line.append(grid_ref[lane_block, pl.ds(row * PITCH + const, HALF), :])
        found.append(line)
    return found


def taps_of(kern_ref, lanes):
    return [
        jnp.broadcast_to(kern_ref[tap : tap + 1, lanes].astype(F32), (HALF, LANES))
        for tap in range(9)
    ]


def conv_at(found, taps, row_par, col_par):
    total = None
    for row_off in range(3):
        for col_off in range(3):
            term = taps[row_off * 3 + col_off] * found[row_par + row_off][col_par + col_off]
            total = term if total is None else total + term
    return total


def conv_back_at(found, taps, sums, source, row_par, col_par):
    total = None
    sums = list(sums)
    for row_off in range(3):
        for col_off in range(3):
            tap = row_off * 3 + col_off
            near = found[row_par + 2 - row_off][col_par + 2 - col_off]
            term = taps[tap] * near
            total = term if total is None else total + term
            part = source * near
            sums[tap] = sums[tap] + (part[:8] + part[8:])
    return total, tuple(sums)


def no_sums():
    return tuple(jnp.zeros((8, LANES), F32) for _ in range(9))


def split_lanes(values_in):
    count = values_in.shape[-1] // LANES
    return [values_in[:, j * LANES : (j + 1) * LANES] for j in range(count)]


def norm_parts(parts):
    width = len(parts) * LANES
    mean = jnp.sum(sum(parts[1:], parts[0]), axis=-1, keepdims=True) * (1.0 / width)
    centre = [part - mean for part in parts]
    squares = [part * part for part in centre]
    var = jnp.sum(sum(squares[1:], squares[0]), axis=-1, keepdims=True) * (1.0 / width)
    rstd = lax.rsqrt(var + EPS)
    return [part * rstd for part in centre], rstd


def norm_rows(values_in):
    mean = jnp.mean(values_in, axis=-1, keepdims=True)
    centre = values_in - mean
    rstd = lax.rsqrt(jnp.mean(centre * centre, axis=-1, keepdims=True) + EPS)
    return centre * rstd, rstd


def modulation_kernel(silu_ref, weight_ref, mod_out):
    width = silu_ref.shape[-1]
    left = jnp.broadcast_to(silu_ref[...].astype(F32), (16, width)).astype(BF16)
    for which in range(weight_ref.shape[-1] // width):
        row = pl.program_id(0) * 2 + which
        mod_out[pl.ds(row, 1), :] = dot(left, weight_ref[:, which * width : (which + 1) * width])[:1]


def modulation_stage(silu_low, w_mod):
    width = silu_low.shape[-1]
    return pl.pallas_call(
        modulation_kernel,
        out_shape=jax.ShapeDtypeStruct((w_mod.shape[-1] // width, width), F32),
        grid=(w_mod.shape[-1] // (2 * width),),
        in_specs=[whole(silu_low.shape), pl.BlockSpec((width, 2 * width), lambda i: (0, i))],
        out_specs=whole((w_mod.shape[-1] // width, width)),
        compiler_params=params(),
        name="modulation",
        cost_estimate=cost(5),
    )(silu_low, w_mod)


def group_of(row_par, col_par):
    return row_par * 2 + col_par


def first_kernel(
    idx, tok_ref, cot_ref, mod_ref, kern_ref, conv_out, tok_out, cot_out, tok_tmp, cot_tmp, grid
):
    width = tok_ref.shape[-1]
    count = width // LANES
    grid[...] = jnp.zeros(grid.shape, F32)

    def one_row(row, carry):
        for row_par in range(2):
            start = pl.multiple_of((row * 2 + row_par) * SIDE, SIDE)
            values = tok_ref[0, pl.ds(start, SIDE), :].astype(F32)
            grads = cot_ref[0, pl.ds(start, SIDE), :].astype(F32)
            for j in range(count):
                tok_tmp[row_par, j] = values[:, j * LANES : (j + 1) * LANES]
                cot_tmp[row_par, j] = grads[:, j * LANES : (j + 1) * LANES]
            for col_par in range(2):
                group = group_of(row_par, col_par)
                out_row = pl.multiple_of(group * TILE + row * HALF, HALF)
                parts = [tok_tmp[row_par, j, pl.ds(col_par, HALF, stride=2), :] for j in range(count)]
                for j in range(count):
                    lanes = slice(j * LANES, (j + 1) * LANES)
                    tok_out[pl.ds(out_row, HALF), lanes] = parts[j].astype(BF16)
                    cot_out[pl.ds(out_row, HALF), lanes] = cot_tmp[
                        row_par, j, pl.ds(col_par, HALF, stride=2), :
                    ].astype(BF16)
                normed, _ = norm_parts(parts)
                for j in range(count):
                    lanes = slice(j * LANES, (j + 1) * LANES)
                    value = normed[j] * (1.0 + mod_ref[1:2, lanes]) + mod_ref[0:1, lanes]
                    grid[j, pl.ds(row * PITCH + pad_row(group, 0), HALF), :] = value
        return carry

    lax.fori_loop(0, HALF, one_row, 0)
    for j in range(count):
        lanes = slice(j * LANES, (j + 1) * LANES)
        taps = taps_of(kern_ref, lanes)

        def one_conv(row, carry, j=j, lanes=lanes, taps=taps):
            found = neighbours(grid, j, row)
            for row_par in range(2):
                for col_par in range(2):
                    out_row = pl.multiple_of(group_of(row_par, col_par) * TILE + row * HALF, HALF)
                    value = conv_at(found, taps, row_par, col_par)
                    conv_out[pl.ds(out_row, HALF), lanes] = value.astype(BF16)
            return carry

        lax.fori_loop(0, HALF, one_conv, 0)


def first_stage(idx, tokens, cotangent, mod, kern):
    _, length, width = tokens.shape
    shape = jax.ShapeDtypeStruct((length, width), BF16)
    mine = pl.BlockSpec((1, length, width), lambda i, idx: (idx[0], 0, 0))
    return pl.pallas_call(
        first_kernel,
        out_shape=(shape, shape, shape),
        grid_spec=pltpu.PrefetchScalarGridSpec(
            num_scalar_prefetch=1,
            grid=(1,),
            in_specs=[mine, mine, whole(mod.shape), whole(kern.shape)],
            out_specs=[whole((length, width))] * 3,
            scratch_shapes=[
                pltpu.VMEM((2, width // LANES, SIDE, LANES), F32),
                pltpu.VMEM((2, width // LANES, SIDE, LANES), F32),
                pltpu.VMEM((width // LANES, PAD_ROWS, LANES), F32),
            ],
        ),
        compiler_params=params(),
        name="norm_conv",
        cost_estimate=cost(11),
    )(idx, tokens, cotangent, mod, kern)


def head_mask(values_in, which):
    lane = lax.broadcasted_iota(jnp.int32, values_in.shape, 1)
    keep = lane < HEAD_DIM if which == 0 else lane >= HEAD_DIM
    return jnp.where(keep, values_in, jnp.zeros_like(values_in))


def soft_keys(keys, queries, keep):
    raw = dot_nt(keys, queries)
    scores = jnp.where(keep, raw * (HEAD_DIM**-0.5), -1e30)
    exponent = jnp.exp(scores - jnp.max(scores, axis=0, keepdims=True))
    return exponent * (1.0 / jnp.sum(exponent, axis=0, keepdims=True))


def attend_heads(keep, share, qkv_out, mixed_out):
    for pair in range(share // LANES):
        lanes = [slice(t * share + pair * LANES, t * share + (pair + 1) * LANES) for t in range(3)]
        queries = qkv_out[:, lanes[0]]
        keys = qkv_out[:, lanes[1]]
        values_t = qkv_out[:, lanes[2]].astype(F32).T.astype(BF16)
        halves = []
        for which in range(2):
            probs = soft_keys(head_mask(keys, which), queries, keep).astype(BF16)
            halves.append(dot(values_t[which * HEAD_DIM : (which + 1) * HEAD_DIM], probs))
        mixed_out[:, pair * LANES : (pair + 1) * LANES] = jnp.concatenate(halves, axis=0).T.astype(BF16)


def half_offsets(core, size):
    mine = pl.multiple_of(core * size, size)
    theirs = pl.multiple_of((1 - core) * size, size)
    return mine, theirs


def attend_own_kernel(conv_ref, valid_ref, weight_ref, perm_ref, convt_out, qkv_out, mixed_out):
    conved = conv_ref[...]
    share = weight_ref.shape[-1]
    for which in range(3):
        qkv_out[:, which * share : (which + 1) * share] = dot(conved, weight_ref[which]).astype(BF16)
    convt_out[...] = dot_nt(perm_ref[...], conved).astype(BF16)
    keep = jnp.broadcast_to(valid_ref[0], (TILE, TILE)) > 0
    attend_heads(keep, share, qkv_out, mixed_out)


def attend_other_kernel(
    idx, conv_ref, valid_ref, wa_ref, wb_ref, mown_ref, own_ref, tok_ref, cot_ref, mod_ref,
    qkv_out, mixed_out, attn_out, res_out, norm_out, gdown_out, normt_out, gdownt_out,
):
    keep = jnp.broadcast_to(valid_ref[0], (TILE, TILE)) > 0
    share = wa_ref.shape[-1]
    half = wa_ref.shape[1]
    mine, theirs = half_offsets(idx[1], half)
    left_a, left_b = conv_ref[:, pl.ds(mine, half)], conv_ref[:, pl.ds(theirs, half)]
    for which in range(3):
        qkv_out[:, which * share : (which + 1) * share] = (
            dot(left_a, wa_ref[which]) + dot(left_b, wb_ref[which])
        ).astype(BF16)
    attend_heads(keep, share, qkv_out, mixed_out)
    for offset, weight_ref in ((mine, wa_ref), (theirs, wb_ref)):
        attn_out[:, pl.ds(offset, half)] = dot_nt(
            mown_ref[...], own_ref[pl.ds(offset, half), :]
        ) + dot_nt(mixed_out[...], weight_ref[3])
    attn = attn_out[...]
    residual = tok_ref[...].astype(F32) + mod_ref[2:3, :] * attn
    res_out[...] = residual
    normed, _ = norm_rows(residual)
    normed = normed * (1.0 + mod_ref[4:5, :]) + mod_ref[3:4, :]
    norm_out[...] = normed.astype(BF16)
    normt_out[...] = normed.T.astype(BF16)
    gdown = mod_ref[5:6, :] * cot_ref[...].astype(F32)
    gdown_out[...] = gdown.astype(BF16)
    gdownt_out[...] = gdown.T.astype(BF16)


def group_rows(cols):
    return pl.BlockSpec((TILE, cols), lambda g, *_: (g, 0))


def attend_own_stage(conved, valid, w_own, perm):
    length, width = conved.shape
    share = w_own.shape[-1]
    return pl.pallas_call(
        attend_own_kernel,
        out_shape=(
            jax.ShapeDtypeStruct((width, length), BF16),
            jax.ShapeDtypeStruct((length, 3 * share), BF16),
            jax.ShapeDtypeStruct((length, share), BF16),
        ),
        grid=(GROUPS,),
        in_specs=[
            group_rows(width),
            pl.BlockSpec((1, TILE, 1), lambda g: (g, 0, 0)),
            whole(w_own.shape),
            whole(perm.shape),
        ],
        out_specs=[
            pl.BlockSpec((width, TILE), lambda g: (0, g)),
            group_rows(3 * share),
            group_rows(share),
        ],
        compiler_params=params(),
        name="attend_own",
        cost_estimate=cost(14),
    )(conved, valid, w_own, perm)


def attend_other_stage(idx, conved, valid, part_a, part_b, mixed_own, o_own, tok, cot, mod):
    length, width = conved.shape
    share = part_a.shape[-1]
    low = jax.ShapeDtypeStruct((length, width), BF16)
    high = jax.ShapeDtypeStruct((length, width), F32)
    turned = jax.ShapeDtypeStruct((width, length), BF16)
    return pl.pallas_call(
        attend_other_kernel,
        out_shape=(
            jax.ShapeDtypeStruct((length, 3 * share), BF16),
            jax.ShapeDtypeStruct((length, share), BF16),
            high,
            high,
            low,
            low,
            turned,
            turned,
        ),
        grid_spec=pltpu.PrefetchScalarGridSpec(
            num_scalar_prefetch=1,
            grid=(GROUPS,),
            in_specs=[
                group_rows(width),
                pl.BlockSpec((1, TILE, 1), lambda g, idx: (g, 0, 0)),
                whole(part_a.shape),
                whole(part_b.shape),
                group_rows(share),
                whole(o_own.shape),
                group_rows(width),
                group_rows(width),
                whole(mod.shape),
            ],
            out_specs=[group_rows(3 * share), group_rows(share)]
            + [group_rows(width)] * 4
            + [pl.BlockSpec((width, TILE), lambda g, idx: (0, g))] * 2,
        ),
        compiler_params=params(),
        name="attend_other",
        cost_estimate=cost(20),
    )(idx, conved, valid, part_a, part_b, mixed_own, o_own, tok, cot, mod)


def gelu_pair(value):
    square = value * value
    inner = jnp.tanh(GELU_A * (value + GELU_B * (square * value)))
    cdf = 0.5 * (1.0 + inner)
    slope = cdf + (value * (0.5 * GELU_A)) * (1.0 - inner * inner) * (1.0 + (3.0 * GELU_B) * square)
    return value * cdf, slope


def ffn_kernel(
    carried, idx, norm_ref, gdown_ref, up_ref, down_ref, kern_ref, normt_hbm, gdownt_hbm, *refs
):
    if carried:
        sum_in, gnorm_in, _ = refs[:3]
        refs = refs[3:]
    sum_hbm, gnorm_hbm, grads_out, kern_out = refs[:4]
    normt, gdownt, sums, gnorms, grid_up, grid_gz, gact, active, gupper, in_sems, out_sems = refs[4:]
    width = norm_ref.shape[-1]
    chunk = up_ref.shape[-1]
    step = pl.program_id(0)
    loads = [(normt_hbm, normt), (gdownt_hbm, gdownt)]
    if carried:
        loads += [(sum_in, sums), (gnorm_in, gnorms)]
    loads = [pltpu.make_async_copy(src, dst, in_sems.at[i]) for i, (src, dst) in enumerate(loads)]

    @pl.when(step == 0)
    def _():
        for load in loads:
            load.start()
        grid_up[...] = jnp.zeros(grid_up.shape, F32)
        grid_gz[...] = jnp.zeros(grid_gz.shape, F32)
        if not carried:
            sums[...] = jnp.zeros(sums.shape, F32)
            gnorms[...] = jnp.zeros(gnorms.shape, F32)

    for block in range(chunk // TILE):
        cols = slice(block * TILE, (block + 1) * TILE)
        upper = dot(norm_ref[...], up_ref[:, cols])
        grads = dot(gdown_ref[...], down_ref[:, cols])
        for side in range(TILE // LANES):
            j = block * (TILE // LANES) + side
            lanes = slice(side * LANES, (side + 1) * LANES)
            gact[j] = grads[:, lanes]
            for group in range(GROUPS):
                for row in range(HALF):
                    at = group * TILE + row * HALF
                    grid_up[j, pl.ds(pad_row(group, row), HALF), :] = upper[at : at + HALF, lanes]

    def one_block(j, carry):
        lanes = pl.ds(pl.multiple_of(j * LANES, LANES), LANES)
        taps = taps_of(kern_ref, lanes)

        def forward(row, carry):
            found = neighbours(grid_up, j, row)
            for row_par in range(2):
                for col_par in range(2):
                    group = group_of(row_par, col_par)
                    out_row = pl.multiple_of(group * TILE + row * HALF, HALF)
                    act, slope = gelu_pair(conv_at(found, taps, row_par, col_par))
                    active[pl.ds(out_row, HALF), lanes] = act.astype(BF16)
                    grid_gz[j, pl.ds(row * PITCH + pad_row(group, 0), HALF), :] = (
                        gact[j, pl.ds(out_row, HALF), :] * slope
                    )
            return carry

        lax.fori_loop(0, HALF, forward, 0)

        def backward(row, sums):
            found = neighbours(grid_gz, j, row)
            for row_par in range(2):
                for col_par in range(2):
                    group = group_of(row_par, col_par)
                    out_row = pl.multiple_of(group * TILE + row * HALF, HALF)
                    source = grid_up[j, pl.ds(row * PITCH + pad_row(group, 0), HALF), :]
                    grad, sums = conv_back_at(found, taps, sums, source, row_par, col_par)
                    gupper[pl.ds(out_row, HALF), lanes] = grad.astype(BF16)
            return sums

        tap_sums = lax.fori_loop(0, HALF, backward, no_sums())
        for tap in range(9):
            kern_out[tap : tap + 1, lanes] = jnp.sum(tap_sums[tap], axis=0, keepdims=True)
        return carry

    lax.fori_loop(0, chunk // LANES, one_block, 0)

    @pl.when(step == 0)
    def _():
        for load in loads:
            load.wait()

    for block in range(chunk // TILE):
        cols = slice(block * TILE, (block + 1) * TILE)
        out_cols = slice(chunk + block * TILE, chunk + (block + 1) * TILE)
        grads_out[:, cols] = dot(normt[...], gupper[:, cols]).astype(BF16)
        grads_out[:, out_cols] = dot(gdownt[...], active[:, cols]).astype(BF16)
    last = step == pl.num_programs(0) - 1
    stores = []
    for block in range(width // TILE):
        cols = slice(block * TILE, (block + 1) * TILE)
        sums[:, cols] += dot_nt(active[...], down_ref[cols, :])
        gnorms[:, cols] += dot_nt(gupper[...], up_ref[cols, :])
        for which, (held, out_hbm) in enumerate(((sums, sum_hbm), (gnorms, gnorm_hbm))):
            store = pltpu.make_async_copy(
                held.at[:, cols], out_hbm.at[:, cols], out_sems.at[block, which]
            )
            stores.append(store)
            pl.when(last)(store.start)

    @pl.when(last)
    def _():
        for store in stores:
            store.wait()


def ffn_stage(idx, normed, gdown, normed_t, gdown_t, w_up, w_down, kern, chunk, first, count, slots, carried):
    length, width = normed.shape
    into, total = slots
    cols = pl.BlockSpec((width, chunk), lambda i, idx: (0, first + i))
    small = pl.BlockSpec((9, chunk), lambda i, idx: (0, first + i))
    anywhere = pl.BlockSpec(memory_space=pl.ANY)
    lines = chunk // LANES
    full = jax.ShapeDtypeStruct((length, width), F32)
    extra = () if carried is None else carried
    aliases = {} if carried is None else {8: 0, 9: 1, 10: 2}
    return pl.pallas_call(
        partial(ffn_kernel, carried is not None),
        out_shape=(
            full,
            full,
            jax.ShapeDtypeStruct((width, total * 2 * chunk), BF16),
            jax.ShapeDtypeStruct((9, count * chunk), F32),
        ),
        grid_spec=pltpu.PrefetchScalarGridSpec(
            num_scalar_prefetch=1,
            grid=(count,),
            in_specs=[whole(normed.shape), whole(gdown.shape), cols, cols, small]
            + [anywhere] * (2 + len(extra)),
            out_specs=[
                anywhere,
                anywhere,
                pl.BlockSpec((width, 2 * chunk), lambda i, idx: (0, into + i)),
                pl.BlockSpec((9, chunk), lambda i, idx: (0, i)),
            ],
            scratch_shapes=[
                pltpu.VMEM((width, length), BF16),
                pltpu.VMEM((width, length), BF16),
                pltpu.VMEM((length, width), F32),
                pltpu.VMEM((length, width), F32),
                pltpu.VMEM((lines, PAD_ROWS, LANES), F32),
                pltpu.VMEM((lines, PAD_ROWS, LANES), F32),
                pltpu.VMEM((lines, length, LANES), F32),
                pltpu.VMEM((length, chunk), BF16),
                pltpu.VMEM((length, chunk), BF16),
                pltpu.SemaphoreType.DMA((4,)),
                pltpu.SemaphoreType.DMA((width // TILE, 2)),
            ],
        ),
        input_output_aliases=aliases,
        compiler_params=params(),
        name="ffn",
        cost_estimate=cost(14 * count),
    )(idx, normed, gdown, w_up, w_down, kern, normed_t, gdown_t, *extra)


def middle_kernel(
    idx, perm_ref, res_ref, attn_ref, down_ref, gnorm_ref, cot_ref, ma_ref, mb_ref,
    own_ref, wa_ref, wb_ref, mod_ref,
    out_ref, gres_out, gmix_out, sums_out, keep_out, send_out, ordered, total, gattn_s,
):
    share = own_ref.shape[-1]
    width = res_ref.shape[-1]
    group = pl.program_id(0)
    residual = res_ref[...]
    cot = cot_ref[...].astype(F32)
    down = down_ref[...]
    result = residual + mod_ref[5:6, :] * down
    parity = (group // 2) * SIDE + lax.rem(group, 2)
    for row in range(HALF):
        for j in range(width // LANES):
            ordered[j, pl.ds(parity + row * 2 * SIDE, HALF, stride=2), :] = result[
                row * HALF : (row + 1) * HALF, j * LANES : (j + 1) * LANES
            ]
    grad_n = gnorm_ref[...]
    normed, rstd = norm_rows(residual)
    scaled = grad_n * (1.0 + mod_ref[4:5, :])
    mean_a = jnp.mean(scaled, axis=-1, keepdims=True)
    mean_b = jnp.mean(scaled * normed, axis=-1, keepdims=True)
    gres = cot + rstd * (scaled - mean_a - normed * mean_b)
    gres_out[...] = gres
    sums = jnp.concatenate(
        [
            jnp.sum(gres * attn_ref[...], axis=0, keepdims=True),
            jnp.sum(grad_n, axis=0, keepdims=True),
            jnp.sum(grad_n * normed, axis=0, keepdims=True),
            jnp.sum(cot * down, axis=0, keepdims=True),
        ],
        axis=0,
    )
    gattn = (mod_ref[2:3, :] * gres).astype(BF16)
    gattn_s[...] = gattn
    gmix_out[:, :share] = dot(gattn, own_ref[...]).astype(BF16)
    half = wa_ref.shape[0]
    mine, theirs = half_offsets(idx[1], half)
    gmix_out[:, share:] = (
        dot(gattn_s[:, pl.ds(mine, half)], wa_ref[...]) + dot(gattn_s[:, pl.ds(theirs, half)], wb_ref[...])
    ).astype(BF16)
    gattn_t = dot_nt(perm_ref[...], gattn).astype(BF16)
    part = jnp.concatenate([dot(gattn_t, ma_ref[...]), dot(gattn_t, mb_ref[...])], axis=1)

    @pl.when(group == 0)
    def _():
        sums_out[...] = sums
        total[...] = part

    @pl.when(group > 0)
    def _():
        sums_out[...] += sums
        total[...] += part

    @pl.when(group == GROUPS - 1)
    def _():
        half_rows = width // 2
        keep_out[...] = total[pl.ds(pl.multiple_of(idx[1] * half_rows, half_rows), half_rows), :]
        send_out[...] = total[
            pl.ds(pl.multiple_of((1 - idx[1]) * half_rows, half_rows), half_rows), :
        ].astype(BF16)
        for j in range(width // LANES):
            out_ref[:, j * LANES : (j + 1) * LANES] = ordered[j].astype(BF16)


def middle_stage(idx, perm, res, attn, down, gnorm, cot, mixed, o_own, part_a, part_b, mod):
    half = pl.BlockSpec((TILE, o_own.shape[-1]), lambda g, idx: (g, 0))
    length, width = res.shape
    rows = pl.BlockSpec((TILE, width), lambda g, idx: (g, 0))
    half_rows = width // 2
    low = jax.ShapeDtypeStruct((length, width), BF16)
    return pl.pallas_call(
        middle_kernel,
        out_shape=(
            low,
            jax.ShapeDtypeStruct((length, width), F32),
            low,
            jax.ShapeDtypeStruct((4, width), F32),
            jax.ShapeDtypeStruct((half_rows, width), F32),
            jax.ShapeDtypeStruct((half_rows, width), BF16),
        ),
        grid_spec=pltpu.PrefetchScalarGridSpec(
            num_scalar_prefetch=1,
            grid=(GROUPS,),
            in_specs=[whole(perm.shape)]
            + [rows] * 5
            + [half] * 2
            + [whole(o_own.shape), entry(part_a, 3), entry(part_b, 3), whole(mod.shape)],
            out_specs=[
                whole((length, width)),
                rows,
                rows,
                whole((4, width)),
                whole((half_rows, width)),
                whole((half_rows, width)),
            ],
            scratch_shapes=[
                pltpu.VMEM((width // LANES, length, LANES), F32),
                pltpu.VMEM((width, width), F32),
                pltpu.VMEM((TILE, width), BF16),
            ],
        ),
        compiler_params=params(),
        name="middle",
        cost_estimate=cost(17),
    )(idx, perm, res, attn, down, gnorm, cot, *mixed, o_own, part_a, part_b, mod)


def attend_back_kernel(
    idx, qkv_ref, gmix_ref, valid_ref, convt_ref, okeep_ref, osend_ref, gqkv_out, keep_out, send_out, held
):
    share = qkv_ref.shape[-1] // 3
    group = pl.program_id(0)
    rows = pl.ds(pl.multiple_of(group * TILE, TILE), TILE)
    keep = jnp.broadcast_to(valid_ref[0], (TILE, TILE)) > 0
    lane = lax.broadcasted_iota(jnp.int32, (TILE, LANES), 1)
    for pair in range(share // LANES):
        lanes = [slice(t * share + pair * LANES, t * share + (pair + 1) * LANES) for t in range(3)]
        queries = qkv_ref[:, lanes[0]]
        keys = qkv_ref[:, lanes[1]]
        values = qkv_ref[:, lanes[2]]
        gmix = gmix_ref[:, pair * LANES : (pair + 1) * LANES]
        keys_t = keys.astype(F32).T.astype(BF16)
        gq, gk, gv = [], [], []
        for which in range(2):
            probs = soft_keys(head_mask(keys, which), queries, keep)
            gprobs = dot_nt(head_mask(values, which), gmix)
            gv.append(dot(probs.astype(BF16), gmix))
            weighted = probs * gprobs
            gscores = weighted - probs * jnp.sum(weighted, axis=0, keepdims=True)
            graw = (gscores * (HEAD_DIM**-0.5)).astype(BF16)
            gk.append(dot(graw, queries))
            gq.append(dot(keys_t[which * HEAD_DIM : (which + 1) * HEAD_DIM], graw))
        grads = (
            jnp.concatenate(gq, axis=0).T.astype(BF16),
            jnp.where(lane < HEAD_DIM, gk[0], gk[1]).astype(BF16),
            jnp.where(lane < HEAD_DIM, gv[0], gv[1]).astype(BF16),
        )
        for where, grad in zip(lanes, grads, strict=True):
            gqkv_out[:, where] = grad
            held[rows, where] = grad

    @pl.when(group == GROUPS - 1)
    def _():
        half_rows = keep_out.shape[0]
        mine, theirs = half_offsets(idx[1], half_rows)
        for which in range(3):
            cols = slice(which * share, (which + 1) * share)
            send_out[:, cols] = dot(convt_ref[pl.ds(theirs, half_rows), :], held[:, cols]).astype(BF16)
            keep_out[:, cols] = dot(convt_ref[pl.ds(mine, half_rows), :], held[:, cols])
        keep_out[:, 3 * share :] = okeep_ref[...]
        send_out[:, 3 * share :] = osend_ref[...]


def attend_back_stage(idx, qkv, gmix, valid, conv_t, out_keep, out_send, side):
    length = gmix.shape[0]
    cols = qkv.shape[-1]
    share = cols // 3
    half_rows = out_keep.shape[0]
    shape = (half_rows, 4 * share)
    part = pl.BlockSpec((half_rows, share), lambda g, idx: (0, side), pipeline_mode=pl.Buffered(1))
    return pl.pallas_call(
        attend_back_kernel,
        out_shape=(
            jax.ShapeDtypeStruct((length, cols), BF16),
            jax.ShapeDtypeStruct(shape, F32),
            jax.ShapeDtypeStruct(shape, BF16),
        ),
        grid_spec=pltpu.PrefetchScalarGridSpec(
            num_scalar_prefetch=1,
            grid=(GROUPS,),
            in_specs=[
                group_rows(cols),
                pl.BlockSpec((TILE, share), lambda g, idx: (g, side)),
                pl.BlockSpec((1, TILE, 1), lambda g, idx: (g, 0, 0)),
                whole(conv_t.shape),
                part,
                part,
            ],
            out_specs=[group_rows(cols), whole(shape), whole(shape)],
            scratch_shapes=[pltpu.VMEM((length, cols), BF16)],
        ),
        compiler_params=params(),
        name="attend_back",
        cost_estimate=cost(18),
    )(idx, qkv, gmix, valid, conv_t, out_keep, out_send)


def conv_back_kernel(
    idx, ga_ref, gb_ref, own_ref, wa_ref, wb_ref, tok_ref, mod_ref, kern_ref,
    grads_out, kern_out, sums_out, grid_g, normed_s,
):
    width = tok_ref.shape[-1]
    count = width // LANES
    share = own_ref.shape[-1]
    half = wa_ref.shape[1]
    group = pl.program_id(0)

    @pl.when(group == 0)
    def _():
        grid_g[...] = jnp.zeros(grid_g.shape, F32)

    for offset, weight_ref in zip(half_offsets(idx[1], half), (wa_ref, wb_ref), strict=True):
        total = None
        for which in range(3):
            cols = slice(which * share, (which + 1) * share)
            part = dot_nt(ga_ref[:, cols], own_ref[which, pl.ds(offset, half), :])
            part += dot_nt(gb_ref[:, cols], weight_ref[which])
            total = part if total is None else total + part
        for side in range(half // LANES):
            lanes = slice(side * LANES, (side + 1) * LANES)
            for row in range(HALF):
                grid_g[offset // LANES + side, pl.ds(group * GROUP_ROWS + pad_row(0, row), HALF), :] = total[
                    row * HALF : (row + 1) * HALF, lanes
                ]
    normed, _ = norm_rows(tok_ref[...].astype(F32))
    for j in range(count):
        normed_s[j, pl.ds(pl.multiple_of(group * TILE, TILE), TILE), :] = normed[
            :, j * LANES : (j + 1) * LANES
        ]

    @pl.when(group == GROUPS - 1)
    def _():
        for j in range(count):
            lanes = slice(j * LANES, (j + 1) * LANES)
            taps = taps_of(kern_ref, lanes)

            scale, shift = 1.0 + mod_ref[1:2, lanes], mod_ref[0:1, lanes]

            def backward(row, carry, j=j, lanes=lanes, taps=taps, scale=scale, shift=shift):
                sums, (shift_sum, scale_sum) = carry
                found = neighbours(grid_g, j, row)
                for row_par in range(2):
                    for col_par in range(2):
                        at = pl.multiple_of(group_of(row_par, col_par) * TILE + row * HALF, HALF)
                        normed = normed_s[j, pl.ds(at, HALF), :]
                        grad, sums = conv_back_at(found, taps, sums, normed * scale + shift, row_par, col_par)
                        grads_out[pl.ds(at, HALF), lanes] = grad
                        prod = grad * normed
                        shift_sum = shift_sum + (grad[:8] + grad[8:])
                        scale_sum = scale_sum + (prod[:8] + prod[8:])
                return sums, (shift_sum, scale_sum)

            zero = jnp.zeros((8, LANES), F32)
            sums, pair = lax.fori_loop(0, HALF, backward, (no_sums(), (zero, zero)))
            for which in range(2):
                sums_out[which : which + 1, lanes] = jnp.sum(pair[which], axis=0, keepdims=True)
            for tap in range(9):
                kern_out[tap : tap + 1, lanes] = jnp.sum(sums[tap], axis=0, keepdims=True)


def conv_back_stage(idx, g_own, g_other, w_own, part_a, part_b, tok, mod, kern):
    length, width = tok.shape
    count = width // LANES
    cols = g_own.shape[-1]
    return pl.pallas_call(
        conv_back_kernel,
        out_shape=(
            jax.ShapeDtypeStruct((length, width), F32),
            jax.ShapeDtypeStruct((9, width), F32),
            jax.ShapeDtypeStruct((2, width), F32),
        ),
        grid_spec=pltpu.PrefetchScalarGridSpec(
            num_scalar_prefetch=1,
            grid=(GROUPS,),
            in_specs=[
                group_rows(cols),
                group_rows(cols),
                whole(w_own.shape),
                leading(part_a, 3),
                leading(part_b, 3),
                group_rows(width),
                whole(mod.shape),
                whole(kern.shape),
            ],
            out_specs=[whole((length, width)), whole((9, width)), whole((2, width))],
            scratch_shapes=[
                pltpu.VMEM((count, PAD_ROWS, LANES), F32),
                pltpu.VMEM((count, length, LANES), F32),
            ],
        ),
        compiler_params=params(),
        name="conv_back",
        cost_estimate=cost(18),
    )(idx, g_own, g_other, w_own, part_a, part_b, tok, mod, kern)


def norm_back_kernel(grads_ref, tok_ref, gres_ref, mod_ref, gtok_out, ordered):
    width = tok_ref.shape[-1]
    group = pl.program_id(0)
    grads = grads_ref[...]
    normed, rstd = norm_rows(tok_ref[...].astype(F32))
    scaled = grads * (1.0 + mod_ref[1:2, :])
    mean_a = jnp.mean(scaled, axis=-1, keepdims=True)
    mean_b = jnp.mean(scaled * normed, axis=-1, keepdims=True)
    result = gres_ref[...] + rstd * (scaled - mean_a - normed * mean_b)
    parity = (group // 2) * SIDE + lax.rem(group, 2)
    for row in range(HALF):
        for j in range(width // LANES):
            ordered[j, pl.ds(parity + row * 2 * SIDE, HALF, stride=2), :] = result[
                row * HALF : (row + 1) * HALF, j * LANES : (j + 1) * LANES
            ]

    @pl.when(group == GROUPS - 1)
    def _():
        for j in range(width // LANES):
            gtok_out[:, j * LANES : (j + 1) * LANES] = ordered[j].astype(BF16)


def norm_back_stage(grads, tok, gres, mod):
    length, width = tok.shape
    return pl.pallas_call(
        norm_back_kernel,
        out_shape=jax.ShapeDtypeStruct((length, width), BF16),
        grid=(GROUPS,),
        in_specs=[group_rows(width), group_rows(width), group_rows(width), whole(mod.shape)],
        out_specs=whole((length, width)),
        scratch_shapes=[pltpu.VMEM((width // LANES, length, LANES), F32)],
        compiler_params=params(),
        name="norm_back",
        cost_estimate=cost(6),
    )(grads, tok, gres, mod)


def silu_of(values_in):
    return values_in * jax.nn.sigmoid(values_in)


def swap(values_in, axis, bit):
    size = lax.axis_size(axis)
    return lax.ppermute(values_in, axis, [(i, i ^ bit) for i in range(size)])


def spread(size, position):
    if size < 4:
        return position
    quarter = size // 4
    low, rest = position // (2 * quarter), position % (2 * quarter)
    return (rest % quarter) * 4 + (rest // quarter) * 2 + low


def row_permutation(size, width):
    block = width // size
    order = [spread(size, i // block) * block + i % block for i in range(width)]
    source = jnp.array(order, jnp.int32)
    return (source[:, None] == jnp.arange(width, dtype=jnp.int32)[None, :]).astype(BF16)


def tie(values_in, *first):
    return lax.optimization_barrier((values_in, first))[0]


def halving_bits(size):
    bits = [2] if size > 2 else []
    rest = size // 4
    while rest > 1:
        bits.append(rest * 2)
        rest //= 2
    return bits


def unshuffle(tokens_in):
    blocked = tokens_in.reshape(HALF, 2, HALF, 2)
    return blocked.transpose(1, 3, 0, 2).reshape(GROUPS, TILE)


def local(
    tokens,
    valid,
    steps,
    labels,
    w_mod,
    step_table,
    class_table,
    conv_attn,
    w_qkv,
    w_out,
    conv_ffn,
    w_up,
    w_down,
    cotangent,
):
    dp_size = lax.axis_size("dp")
    width = tokens.shape[-1]
    dp_at = lax.axis_index("dp")
    mp_at = lax.axis_index("mp")
    latent = dp_at * tokens.shape[0] + mp_at
    idx = jnp.stack([mp_at, dp_at % 2]).astype(jnp.int32)
    perm = row_permutation(dp_size, width)

    core = dp_at % 2
    half_rows = width // 2
    hidden = w_up.shape[-1]
    chunk = hidden // 3
    share = w_out.shape[-1]
    rows = width // dp_size
    bits = halving_bits(dp_size)

    def split_rows(total, bit):
        rows = total.shape[-2] // 2
        parts = total.reshape(total.shape[:-2] + (2, rows) + total.shape[-1:])
        axis = parts.ndim - 3
        flag = (dp_at // bit) % 2
        mine = lax.dynamic_index_in_dim(parts, flag, axis, keepdims=False)
        theirs = lax.dynamic_index_in_dim(parts, 1 - flag, axis, keepdims=False)
        return mine, theirs.astype(BF16)

    def last_rows(total):
        if len(bits) < 3:
            for bit in bits[1:]:
                mine, theirs = split_rows(total, bit)
                total = mine + swap(theirs, "dp", bit).astype(F32)
            return total
        parts = total.reshape(4, -1, total.shape[-1])
        at = (dp_at // 4) % 4
        kept = lax.dynamic_index_in_dim(parts, at, 0, keepdims=False)
        for by in (1, 2, 3):
            theirs = lax.dynamic_index_in_dim(parts, at ^ by, 0, keepdims=False).astype(BF16)
            kept = kept + swap(theirs, "dp", 4 * by).astype(F32)
        return kept

    def both(mine, theirs):
        place = lax.broadcasted_iota(jnp.int32, (2,) + mine.shape, 0)
        return jnp.where(place == mp_at, mine[None], theirs[None])

    qkv_own = w_qkv.transpose(1, 0, 2)
    stack = jnp.concatenate([qkv_own, w_out[None]], axis=0)
    part_a = swap(lax.dynamic_slice_in_dim(stack, core * half_rows, half_rows, axis=1), "mp", 1)

    embedding = jnp.take(step_table, steps, axis=0).astype(F32) + jnp.take(
        class_table, labels, axis=0
    ).astype(F32)
    silu_value, silu_pull = jax.vjp(silu_of, embedding)
    silu_low = silu_value.astype(BF16)
    my_silu = lax.dynamic_slice_in_dim(silu_low, latent, 1)
    mod = modulation_stage(my_silu, w_mod)

    my_valid = lax.dynamic_index_in_dim(valid, mp_at, 0, keepdims=False)
    keep = unshuffle(my_valid)[:, :, None]

    conved, tok, cot = first_stage(idx, tokens, cotangent, mod, conv_attn)
    up_part, down_part = tie((w_up, w_down), conved)
    ffn_part = jnp.where(core == 0, up_part, down_part)
    part_a, keep = tie((part_a, keep), ffn_part)
    part_b = swap(part_a, "dp", 1)
    ffn_part = tie(ffn_part, part_a)
    ffn_a = swap(ffn_part, "mp", 1)
    conv_t, qkv_x, mixed_x = attend_own_stage(tie(conved, ffn_part), keep, qkv_own, perm)
    qkv_y, mixed_y, attn, res, normed, gdown, normed_t, gdown_t = attend_other_stage(
        idx, tie(conved, mixed_x), keep, part_a, part_b, mixed_x, w_out, tok, cot, mod
    )

    chunks = hidden // chunk
    ahead = chunks - 1
    ffn = partial(ffn_stage, idx)
    shared = (gdown, normed_t, gdown_t)
    *carried, kern_x = ffn(
        normed, *shared, w_up, w_down, conv_ffn, chunk, 0, ahead, (0, 2 * chunks), None
    )
    ffn_a = tie(ffn_a, carried[0])
    kern_other = swap(tie(conv_ffn, ffn_a), "mp", 1)
    ffn_b = swap(ffn_a, "dp", 1)
    *carried, kern_y = ffn(
        tie(normed, ffn_a), *shared, w_up, w_down, conv_ffn, chunk, ahead, 1, (ahead, 2 * chunks), carried
    )
    ffn_a, ffn_b = tie((ffn_a, ffn_b), carried[0])
    up_other = jnp.where(core == 0, ffn_a, ffn_b)
    down_other = jnp.where(core == 0, ffn_b, ffn_a)
    down, gnorm, grads_ffn, kern_z = ffn(
        normed, *shared, up_other, down_other, kern_other, chunk, 0, chunks, (chunks, 2 * chunks), carried
    )
    kern_here = jnp.concatenate([kern_x, kern_y], axis=1)
    sum_ffn = lax.psum_scatter(grads_ffn, "dp", scatter_dimension=0, tiled=True)
    output, gres, gmix, sums_mid, out_keep, out_send = middle_stage(
        idx, perm, res, attn, down, gnorm, cot, (mixed_x, mixed_y), w_out, part_a, part_b, mod
    )
    top, bottom = jnp.split(output, 2, axis=0)
    top_other = swap(top, "mp", 1)
    g_other, c_keep, c_send = attend_back_stage(idx, qkv_y, gmix, keep, conv_t, out_keep, out_send, 1)
    c_got = swap(c_send, "dp", 1)
    bottom_other = swap(tie(bottom, top_other, c_send), "mp", 1)
    g_own, d_keep, d_send = attend_back_stage(
        idx, qkv_x, tie(gmix, c_send, top_other), keep, conv_t, out_keep, out_send, 0
    )
    c_got = tie(c_got, g_own)
    total_c = (c_keep + c_got.astype(F32)).astype(BF16)
    from_x = swap(tie(total_c, bottom_other), "mp", 1)
    d_got = swap(tie(d_send, bottom_other), "dp", 1)
    grads, kern_a, sums_last = conv_back_stage(
        idx, tie(g_own, total_c, bottom_other), g_other, qkv_own, part_a, part_b, tok, mod, conv_attn
    )

    d_got, from_x = tie((d_got, from_x), grads)
    total_d = d_keep + d_got.astype(F32) + from_x.astype(F32)
    mine_d, theirs = split_rows(total_d, bits[0])
    got_d = swap(theirs, "dp", bits[0])

    sent = jnp.concatenate([kern_z.reshape(-1, width), kern_a], axis=0)
    held = jnp.concatenate([kern_here.reshape(-1, width), kern_a], axis=0)
    grad_mod = jnp.concatenate([sums_last, sums_mid], axis=0)
    mine = grad_mod.reshape(1, -1).astype(BF16)
    mod_there, held_there = swap(mine, "mp", 1), swap(sent, "mp", 1)
    gtok = norm_back_stage(tie(grads, theirs, mine, sent), tok, gres, mod)

    gtok_other = swap(tie(gtok, mod_there, held_there), "mp", 1)
    output, top_other, bottom_other = tie((output, top_other, bottom_other), gtok)
    whole_output = both(output, jnp.concatenate([top_other, bottom_other], axis=0))
    got_d, mod_there, held_there = tie((got_d, mod_there, held_there), gtok)
    total_d = mine_d + got_d.astype(F32)
    for bit in bits[1:-2]:
        mine_d, theirs = split_rows(total_d, bit)
        total_d = mine_d + swap(theirs, "dp", bit).astype(F32)
    total_d = last_rows(total_d)
    grad_qkv = total_d[:, : 3 * share].reshape(rows, 3, share)
    grad_out = total_d[:, 3 * share :]
    sum_ffn = tie(sum_ffn, gtok)
    from_f = swap(sum_ffn[:, 2 * hidden :], "mp", 1)
    ffn_sum = sum_ffn[:, : 2 * hidden].astype(F32) + from_f.astype(F32)
    ffn_sum = ffn_sum.reshape(rows, chunks, 2, chunk)
    grad_up = ffn_sum[:, :, 0].reshape(rows, hidden)
    grad_down = ffn_sum[:, :, 1].reshape(rows, hidden)

    gathered = jnp.concatenate([mine, mod_there], axis=0)
    held = held + held_there
    step = 1
    while step < dp_size:
        if 4 * step <= dp_size:
            others = [swap(gathered, "dp", step * by) for by in (1, 2, 3)]
            gathered = jnp.concatenate([gathered, *others], axis=0)
            step *= 4
        else:
            gathered = jnp.concatenate([gathered, swap(gathered, "dp", step)], axis=0)
            step *= 2
    step = 1
    while step < dp_size:
        held = held + swap(held, "dp", step)
        step *= 2
    kern_f = held[:-9].reshape(9, hidden)
    kern_a = held[-9:]
    latents = steps.shape[0]
    order = jnp.arange(latents, dtype=jnp.int32) ^ latent.astype(jnp.int32)
    sort = (order[None, :] == jnp.arange(latents, dtype=jnp.int32)[:, None]).astype(BF16)
    grad_mod_low = jnp.dot(sort, gathered, preferred_element_type=F32).astype(BF16)

    my_cols = lax.dynamic_slice_in_dim(silu_low, dp_at * rows, rows, axis=1)
    grad_w_mod = jnp.einsum("lk,lc->kc", my_cols, grad_mod_low, preferred_element_type=F32)
    grad_silu = jnp.einsum("lc,kc->lk", grad_mod_low, w_mod, preferred_element_type=F32)
    (grad_embedding,) = silu_pull(grad_silu)

    def table_grad(indices, count):
        onehot = (jnp.arange(count, dtype=jnp.int32)[:, None] == indices[None, :]).astype(F32)
        return jnp.dot(onehot, grad_embedding, precision=lax.Precision.HIGHEST)

    return (
        whole_output,
        both(gtok, tie(gtok_other, whole_output, sum_ffn)),
        grad_w_mod,
        table_grad(steps, step_table.shape[0]),
        table_grad(labels, class_table.shape[0]),
        kern_a,
        grad_qkv,
        grad_out,
        kern_f,
        grad_up,
        grad_down,
    )


def solution(mesh):
    in_specs = (
        P("dp", None, None),
        P("dp", None),
        P(),
        P(),
        P(),
        P(),
        P(),
        P(),
        P(None, None, "mp"),
        P(None, "mp"),
        P(None, "mp"),
        P(None, "mp"),
        P(None, "mp"),
        P("dp", None, None),
    )
    out_specs = (
        P("dp", None, None),
        P("dp", None, None),
        P("dp", None),
        P(),
        P(),
        P(),
        P("dp", None, "mp"),
        P("dp", "mp"),
        P(None, "mp"),
        P("dp", "mp"),
        P("dp", "mp"),
    )
    return jax.shard_map(local, mesh=mesh, in_specs=in_specs, out_specs=out_specs, check_vma=False)
```

```python
from functools import partial

import jax
import jax.numpy as jnp
from jax import lax
from jax.experimental import pallas as pl
from jax.experimental.pallas import tpu as pltpu
from jax.sharding import PartitionSpec as P

SIDE = 32
HALF = SIDE // 2
HEAD_DIM = 64
GROUPS = 4
LANES = 128
TILE = 256
EPS = 1e-06
PITCH = HALF + 8
GROUP_ROWS = (HALF + 2) * PITCH + 8
PAD_ROWS = GROUPS * GROUP_ROWS
GELU_A = 0.7978845608028654
GELU_B = 0.044715
F32 = jnp.float32
BF16 = jnp.bfloat16
VMEM_BYTES = 60 * 1024 * 1024


def cost(micros):
    return pl.CostEstimate(flops=int(micros * COST_RATE), bytes_accessed=1000, transcendentals=0)


COST_RATE = 400_000_000


def params(count=1):
    return pltpu.CompilerParams(
        dimension_semantics=("arbitrary",) * count, vmem_limit_bytes=VMEM_BYTES
    )


def whole(shape):
    zeros = (0,) * len(shape)
    return pl.BlockSpec(shape, lambda *_: zeros, pipeline_mode=pl.Buffered(1))


def leading(array, count):
    tail = array.shape[1:]
    return pl.BlockSpec((count,) + tail, lambda *_: (0,) * array.ndim, pipeline_mode=pl.Buffered(1))


def entry(array, which):
    tail = (0,) * (array.ndim - 1)
    return pl.BlockSpec(
        (None,) + array.shape[1:], lambda *_: (which,) + tail, pipeline_mode=pl.Buffered(1)
    )


def dot(left, right):
    return jnp.dot(left, right, preferred_element_type=F32)


def dot_nt(left, right):
    return lax.dot_general(left, right, (((1,), (1,)), ((), ())), preferred_element_type=F32)


def pad_row(group, row, shift=0):
    return group * GROUP_ROWS + (row + 1) * PITCH + 8 + shift


AROUND = ((1, -1), (0, 0), (1, 0), (0, 1))


def neighbours(grid_ref, lane_block, row):
    found = []
    for row_par, row_off in AROUND:
        line = []
        for col_par, col_off in AROUND:
            const = pad_row(row_par * 2 + col_par, row_off, col_off)
            line.append(grid_ref[lane_block, pl.ds(row * PITCH + const, HALF), :])
        found.append(line)
    return found


def taps_of(kern_ref, lanes):
    return [
        jnp.broadcast_to(kern_ref[tap : tap + 1, lanes].astype(F32), (HALF, LANES))
        for tap in range(9)
    ]


def conv_at(found, taps, row_par, col_par):
    total = None
    for row_off in range(3):
        for col_off in range(3):
            term = taps[row_off * 3 + col_off] * found[row_par + row_off][col_par + col_off]
            total = term if total is None else total + term
    return total


def conv_back_at(found, taps, sums, source, row_par, col_par):
    total = None
    sums = list(sums)
    for row_off in range(3):
        for col_off in range(3):
            tap = row_off * 3 + col_off
            near = found[row_par + 2 - row_off][col_par + 2 - col_off]
            term = taps[tap] * near
            total = term if total is None else total + term
            part = source * near
            sums[tap] = sums[tap] + (part[:8] + part[8:])
    return total, tuple(sums)


def no_sums():
    return tuple(jnp.zeros((8, LANES), F32) for _ in range(9))


def split_lanes(values_in):
    count = values_in.shape[-1] // LANES
    return [values_in[:, j * LANES : (j + 1) * LANES] for j in range(count)]


def norm_parts(parts):
    width = len(parts) * LANES
    mean = jnp.sum(sum(parts[1:], parts[0]), axis=-1, keepdims=True) * (1.0 / width)
    centre = [part - mean for part in parts]
    squares = [part * part for part in centre]
    var = jnp.sum(sum(squares[1:], squares[0]), axis=-1, keepdims=True) * (1.0 / width)
    rstd = lax.rsqrt(var + EPS)
    return [part * rstd for part in centre], rstd


def norm_rows(values_in):
    mean = jnp.mean(values_in, axis=-1, keepdims=True)
    centre = values_in - mean
    rstd = lax.rsqrt(jnp.mean(centre * centre, axis=-1, keepdims=True) + EPS)
    return centre * rstd, rstd


def modulation_kernel(silu_ref, weight_ref, mod_out):
    width = silu_ref.shape[-1]
    left = jnp.broadcast_to(silu_ref[...].astype(F32), (16, width)).astype(BF16)
    for which in range(weight_ref.shape[-1] // width):
        row = pl.program_id(0) * 2 + which
        mod_out[pl.ds(row, 1), :] = dot(left, weight_ref[:, which * width : (which + 1) * width])[:1]


def modulation_stage(silu_low, w_mod):
    width = silu_low.shape[-1]
    return pl.pallas_call(
        modulation_kernel,
        out_shape=jax.ShapeDtypeStruct((w_mod.shape[-1] // width, width), F32),
        grid=(w_mod.shape[-1] // (2 * width),),
        in_specs=[whole(silu_low.shape), pl.BlockSpec((width, 2 * width), lambda i: (0, i))],
        out_specs=whole((w_mod.shape[-1] // width, width)),
        compiler_params=params(),
        name="modulation",
        cost_estimate=cost(5),
    )(silu_low, w_mod)


def group_of(row_par, col_par):
    return row_par * 2 + col_par


def first_kernel(
    idx, tok_ref, cot_ref, mod_ref, kern_ref, conv_out, tok_out, cot_out, tok_tmp, cot_tmp, grid
):
    width = tok_ref.shape[-1]
    count = width // LANES
    grid[...] = jnp.zeros(grid.shape, F32)

    def one_row(row, carry):
        for row_par in range(2):
            start = pl.multiple_of((row * 2 + row_par) * SIDE, SIDE)
            values = tok_ref[0, pl.ds(start, SIDE), :].astype(F32)
            grads = cot_ref[0, pl.ds(start, SIDE), :].astype(F32)
            for j in range(count):
                tok_tmp[row_par, j] = values[:, j * LANES : (j + 1) * LANES]
                cot_tmp[row_par, j] = grads[:, j * LANES : (j + 1) * LANES]
        places = [(row_par, col_par) for row_par in range(2) for col_par in range(2)]
        parts = []
        for j in range(count):
            lanes = slice(j * LANES, (j + 1) * LANES)
            lines = []
            for row_par, col_par in places:
                out_row = pl.multiple_of(group_of(row_par, col_par) * TILE + row * HALF, HALF)
                line = tok_tmp[row_par, j, pl.ds(col_par, HALF, stride=2), :]
                lines.append(line)
                tok_out[pl.ds(out_row, HALF), lanes] = line.astype(BF16)
                cot_out[pl.ds(out_row, HALF), lanes] = cot_tmp[
                    row_par, j, pl.ds(col_par, HALF, stride=2), :
                ].astype(BF16)
            parts.append(jnp.concatenate(lines, axis=0))
        normed, _ = norm_parts(parts)
        for j in range(count):
            lanes = slice(j * LANES, (j + 1) * LANES)
            value = normed[j] * (1.0 + mod_ref[1:2, lanes]) + mod_ref[0:1, lanes]
            for at, (row_par, col_par) in enumerate(places):
                grid[j, pl.ds(row * PITCH + pad_row(group_of(row_par, col_par), 0), HALF), :] = value[
                    at * HALF : (at + 1) * HALF
                ]
        return carry

    lax.fori_loop(0, HALF, one_row, 0)
    for j in range(count):
        lanes = slice(j * LANES, (j + 1) * LANES)
        taps = taps_of(kern_ref, lanes)

        def one_conv(row, carry, j=j, lanes=lanes, taps=taps):
            found = neighbours(grid, j, row)
            for row_par in range(2):
                for col_par in range(2):
                    out_row = pl.multiple_of(group_of(row_par, col_par) * TILE + row * HALF, HALF)
                    value = conv_at(found, taps, row_par, col_par)
                    conv_out[pl.ds(out_row, HALF), lanes] = value.astype(BF16)
            return carry

        lax.fori_loop(0, HALF, one_conv, 0)


def first_stage(idx, tokens, cotangent, mod, kern):
    _, length, width = tokens.shape
    shape = jax.ShapeDtypeStruct((length, width), BF16)
    mine = pl.BlockSpec((1, length, width), lambda i, idx: (idx[0], 0, 0))
    return pl.pallas_call(
        first_kernel,
        out_shape=(shape, shape, shape),
        grid_spec=pltpu.PrefetchScalarGridSpec(
            num_scalar_prefetch=1,
            grid=(1,),
            in_specs=[mine, mine, whole(mod.shape), whole(kern.shape)],
            out_specs=[whole((length, width))] * 3,
            scratch_shapes=[
                pltpu.VMEM((2, width // LANES, SIDE, LANES), F32),
                pltpu.VMEM((2, width // LANES, SIDE, LANES), F32),
                pltpu.VMEM((width // LANES, PAD_ROWS, LANES), F32),
            ],
        ),
        compiler_params=params(),
        name="norm_conv",
        cost_estimate=cost(11),
    )(idx, tokens, cotangent, mod, kern)


def head_mask(values_in, which):
    lane = lax.broadcasted_iota(jnp.int32, values_in.shape, 1)
    keep = lane < HEAD_DIM if which == 0 else lane >= HEAD_DIM
    return jnp.where(keep, values_in, jnp.zeros_like(values_in))


def turn(values_in):
    return values_in.astype(F32).T.astype(BF16)


def soft_keys(raw, keep):
    scores = jnp.where(keep, raw * (HEAD_DIM**-0.5), -1e30)
    exponent = jnp.exp(scores - jnp.max(scores, axis=0, keepdims=True))
    return exponent * (1.0 / jnp.sum(exponent, axis=0, keepdims=True))


def attend_heads(keep, share, qkv_out, mixed_out):
    def part(which, pair):
        first = which * share + pair * LANES
        return qkv_out[:, first : first + LANES]

    def scores_of(pair):
        queries_t, keys = turn(part(0, pair)), part(1, pair)
        return [dot(head_mask(keys, which), queries_t) for which in range(2)]

    pairs = share // LANES
    ahead = scores_of(0)
    for pair in range(pairs):
        raws = ahead
        values_t = turn(part(2, pair))
        if pair + 1 < pairs:
            ahead = scores_of(pair + 1)
        probs = [soft_keys(raw, keep).astype(BF16) for raw in raws]
        halves = [dot(values_t[w * HEAD_DIM : (w + 1) * HEAD_DIM], probs[w]) for w in range(2)]
        mixed_out[:, pair * LANES : (pair + 1) * LANES] = jnp.concatenate(halves, axis=0).T.astype(BF16)


def half_offsets(core, size):
    mine = pl.multiple_of(core * size, size)
    theirs = pl.multiple_of((1 - core) * size, size)
    return mine, theirs


def attend_own_kernel(conv_ref, valid_ref, weight_ref, perm_ref, convt_out, qkv_out, mixed_out):
    conved = conv_ref[...]
    share = weight_ref.shape[-1]
    for which in range(3):
        qkv_out[:, which * share : (which + 1) * share] = dot(conved, weight_ref[which]).astype(BF16)
    convt_out[...] = dot_nt(perm_ref[...], conved).astype(BF16)
    keep = jnp.broadcast_to(valid_ref[0], (TILE, TILE)) > 0
    attend_heads(keep, share, qkv_out, mixed_out)


def attend_other_kernel(
    idx, conv_ref, valid_ref, wa_ref, wb_ref, mown_ref, own_ref, tok_ref, cot_ref, mod_ref,
    qkv_out, mixed_out, attn_out, res_out, norm_out, gdown_out, normt_out, gdownt_out,
):
    keep = jnp.broadcast_to(valid_ref[0], (TILE, TILE)) > 0
    share = wa_ref.shape[-1]
    half = wa_ref.shape[1]
    mine, theirs = half_offsets(idx[1], half)
    left_a, left_b = conv_ref[:, pl.ds(mine, half)], conv_ref[:, pl.ds(theirs, half)]
    for which in range(3):
        qkv_out[:, which * share : (which + 1) * share] = (
            dot(left_a, wa_ref[which]) + dot(left_b, wb_ref[which])
        ).astype(BF16)
    attend_heads(keep, share, qkv_out, mixed_out)
    for offset, weight_ref in ((mine, wa_ref), (theirs, wb_ref)):
        attn_out[:, pl.ds(offset, half)] = dot_nt(
            mown_ref[...], own_ref[pl.ds(offset, half), :]
        ) + dot_nt(mixed_out[...], weight_ref[3])
    attn = attn_out[...]
    residual = tok_ref[...].astype(F32) + mod_ref[2:3, :] * attn
    res_out[...] = residual
    normed, _ = norm_rows(residual)
    normed = normed * (1.0 + mod_ref[4:5, :]) + mod_ref[3:4, :]
    norm_out[...] = normed.astype(BF16)
    normt_out[...] = normed.T.astype(BF16)
    gdown = mod_ref[5:6, :] * cot_ref[...].astype(F32)
    gdown_out[...] = gdown.astype(BF16)
    gdownt_out[...] = gdown.T.astype(BF16)


def group_rows(cols):
    return pl.BlockSpec((TILE, cols), lambda g, *_: (g, 0))


def pair_rows(cols):
    return pl.BlockSpec((2 * TILE, cols), lambda i, *_: (i, 0))


def attend_own_stage(conved, valid, w_own, perm):
    length, width = conved.shape
    share = w_own.shape[-1]
    return pl.pallas_call(
        attend_own_kernel,
        out_shape=(
            jax.ShapeDtypeStruct((width, length), BF16),
            jax.ShapeDtypeStruct((length, 3 * share), BF16),
            jax.ShapeDtypeStruct((length, share), BF16),
        ),
        grid=(GROUPS,),
        in_specs=[
            group_rows(width),
            pl.BlockSpec((1, TILE, 1), lambda g: (g, 0, 0)),
            whole(w_own.shape),
            whole(perm.shape),
        ],
        out_specs=[
            pl.BlockSpec((width, TILE), lambda g: (0, g)),
            group_rows(3 * share),
            group_rows(share),
        ],
        compiler_params=params(),
        name="attend_own",
        cost_estimate=cost(14),
    )(conved, valid, w_own, perm)


def attend_other_stage(idx, conved, valid, part_a, part_b, mixed_own, o_own, tok, cot, mod):
    length, width = conved.shape
    share = part_a.shape[-1]
    low = jax.ShapeDtypeStruct((length, width), BF16)
    high = jax.ShapeDtypeStruct((length, width), F32)
    turned = jax.ShapeDtypeStruct((width, length), BF16)
    return pl.pallas_call(
        attend_other_kernel,
        out_shape=(
            jax.ShapeDtypeStruct((length, 3 * share), BF16),
            jax.ShapeDtypeStruct((length, share), BF16),
            high,
            high,
            low,
            low,
            turned,
            turned,
        ),
        grid_spec=pltpu.PrefetchScalarGridSpec(
            num_scalar_prefetch=1,
            grid=(GROUPS,),
            in_specs=[
                group_rows(width),
                pl.BlockSpec((1, TILE, 1), lambda g, idx: (g, 0, 0)),
                whole(part_a.shape),
                whole(part_b.shape),
                group_rows(share),
                whole(o_own.shape),
                group_rows(width),
                group_rows(width),
                whole(mod.shape),
            ],
            out_specs=[group_rows(3 * share), group_rows(share)]
            + [group_rows(width)] * 4
            + [pl.BlockSpec((width, TILE), lambda g, idx: (0, g))] * 2,
        ),
        compiler_params=params(),
        name="attend_other",
        cost_estimate=cost(20),
    )(idx, conved, valid, part_a, part_b, mixed_own, o_own, tok, cot, mod)


def gelu_pair(value):
    square = value * value
    inner = jnp.tanh(GELU_A * (value + GELU_B * (square * value)))
    cdf = 0.5 * (1.0 + inner)
    slope = cdf + (value * (0.5 * GELU_A)) * (1.0 - inner * inner) * (1.0 + (3.0 * GELU_B) * square)
    return value * cdf, slope


def ffn_kernel(
    where, idx, norm_hbm, gdown_hbm, normt_hbm, gdownt_hbm,
    a_now, b_now, a_past, b_past, a_next, b_next, kern_ref, *refs,
):
    into, carried = where
    refs = refs[carried:]
    acc_hbm, grads_hbm, kern_out = refs[:3]
    inputs, turned, acc, halo_a, halo_b, halo_gz, outer_a, outer_b, stage_a, stage_b, in_sems, g_sems, out_sems = refs[3:]
    step = pl.program_id(0)
    count = pl.num_programs(0) - 1
    role = idx[2]
    width = inputs.shape[-1]
    rows_t = turned.shape[1] // GROUPS
    loads = [
        pltpu.make_async_copy(src, dst, in_sems.at[i])
        for i, (src, dst) in enumerate(
            (
                (norm_hbm, inputs.at[0]),
                (gdown_hbm, inputs.at[1]),
                (normt_hbm, turned.at[0]),
                (gdownt_hbm, turned.at[1]),
            )
        )
    ]

    def kind_of(which):
        return jnp.bitwise_xor(role, which)

    def group_slice(group):
        return pl.ds(pl.multiple_of(group * TILE, TILE), TILE)

    def before(halo, which, weight_ref, cols, piece, pieces):
        kind = kind_of(which)
        groups = GROUPS // pieces
        value = dot(inputs[kind, piece * groups * TILE : (piece + 1) * groups * TILE, :], weight_ref[:, cols])
        for group in range(groups):
            for line in range(TILE // LANES):
                for row in range(HALF):
                    at = group * TILE + row * HALF
                    halo[kind, line, pl.ds(pad_row(piece * groups + group, row), HALF), :] = value[
                        at : at + HALF, line * LANES : (line + 1) * LANES
                    ]

    def after(outer, stage, which, weight_ref, cols, piece):
        kind = kind_of(which)
        block, half = piece // 2, piece % 2
        if block < width // TILE:
            out_cols = slice(block * TILE, (block + 1) * TILE)
            rows = slice(half * 2 * TILE, (half + 1) * 2 * TILE)
            acc[kind, rows, out_cols] += dot_nt(outer[kind, rows, :], weight_ref[out_cols, cols])
        else:
            rows = slice(half * width // 2, (half + 1) * width // 2)
            stage[rows, which * TILE : (which + 1) * TILE] = dot(turned[which, rows, :], outer[which]).astype(BF16)

    def forward(halo, outer, which, first, taps):
        lanes = slice(which * LANES, (which + 1) * LANES)
        for row in (2 * first, 2 * first + 1):
            found = neighbours(halo.at[0], which, row)
            for row_par in range(2):
                for col_par in range(2):
                    group = group_of(row_par, col_par)
                    out_row = pl.multiple_of(group * TILE + row * HALF, HALF)
                    centre = pl.ds(row * PITCH + pad_row(group, 0), HALF)
                    act, slope = gelu_pair(conv_at(found, taps, row_par, col_par))
                    outer[1, pl.ds(out_row, HALF), lanes] = act.astype(BF16)
                    halo_gz[which, centre, :] = halo[1, which, centre, :] * slope

    def backward(halo, outer, which, first, taps, sums):
        lanes = slice(which * LANES, (which + 1) * LANES)
        for row in (2 * first, 2 * first + 1):
            found = neighbours(halo_gz, which, row)
            for row_par in range(2):
                for col_par in range(2):
                    group = group_of(row_par, col_par)
                    out_row = pl.multiple_of(group * TILE + row * HALF, HALF)
                    source = halo[0, which, pl.ds(row * PITCH + pad_row(group, 0), HALF), :]
                    grad, sums = conv_back_at(found, taps, sums, source, row_par, col_par)
                    outer[0, pl.ds(out_row, HALF), lanes] = grad.astype(BF16)
        return sums

    def one_chunk(second, halo, outer, past, ahead):
        past_outer, past_stage, past_weights, past_cols = past
        next_halo, next_weights, next_cols = ahead
        base = TILE if second else 0
        for which in range(2):
            taps = taps_of(kern_ref, slice(base + which * LANES, base + (which + 1) * LANES))

            for first in range(HALF // 2):
                after(past_outer, past_stage, which, past_weights[which], past_cols, first)
                forward(halo, outer, which, first, taps)
        for which in range(2):
            lanes = slice(base + which * LANES, base + (which + 1) * LANES)
            taps = taps_of(kern_ref, lanes)

            sums = no_sums()
            for first in range(HALF // 2):
                if first % (8 // 4) == 0:
                    before(next_halo, which, next_weights[which], next_cols, first // (8 // 4), 4)
                sums = backward(halo, outer, which, first, taps, sums)
            for tap in range(9):
                kern_out[tap : tap + 1, lanes] = jnp.sum(sums[tap], axis=0, keepdims=True)

    def store_of(stage, chunk, sem):
        cols = pl.ds(pl.multiple_of((into + chunk) * (2 * TILE), 2 * TILE), 2 * TILE)
        return pltpu.make_async_copy(stage, grads_hbm.at[:, cols], g_sems.at[sem])

    left_cols, right_cols, all_cols = slice(0, TILE), slice(TILE, 2 * TILE), slice(0, TILE)

    @pl.when(step == 0)
    def _():
        for load in loads:
            load.start()
        for ref in (acc, outer_b):
            ref[...] = jnp.zeros(ref.shape, ref.dtype)
        for line in range(TILE // LANES):
            for halo in (halo_a.at[0, line], halo_b.at[0, line], halo_gz.at[line]):
                for group in range(GROUPS):
                    for row in range(-1, HALF + 2):
                        size = PITCH if row in (-1, HALF) else 8
                        halo[pl.ds(pad_row(group, row) - 8, size), :] = jnp.zeros((size, LANES), F32)
        for load in loads:
            load.wait()

        for which, weight_ref in enumerate((a_now, b_now)):
            before(halo_a, which, weight_ref, left_cols, 0, 1)

    @pl.when(jnp.logical_and(step > 1, step < count))
    def _():
        store_of(stage_b, 2 * step - 3, 1).wait()

    @pl.when(step < count)
    def _():
        one_chunk(
            False, halo_a, outer_a,
            (outer_b, stage_b, (a_past, b_past), all_cols), (halo_b, (a_now, b_now), right_cols),
        )

        @pl.when(step > 0)
        def _():
            store_of(stage_b, 2 * step - 1, 1).start()
            store_of(stage_a, 2 * step - 2, 0).wait()

        one_chunk(
            True, halo_b, outer_b,
            (outer_a, stage_a, (a_now, b_now), left_cols), (halo_a, (a_next, b_next), all_cols),
        )
        store_of(stage_a, 2 * step, 0).start()

    @pl.when(step == count)
    def _():
        pl.when(count > 1)(lambda: store_of(stage_b, 2 * step - 3, 1).wait())
        for which, weight_ref in enumerate((a_past, b_past)):
            kind = kind_of(which)
            for piece in range(2 * (width // TILE + 1)):
                after(outer_b, stage_b, which, weight_ref, all_cols, piece)
            pltpu.make_async_copy(acc.at[kind], acc_hbm.at[kind], out_sems.at[which]).start()
        store_of(stage_b, 2 * step - 1, 1).start()
        for which in range(2):
            kind = kind_of(which)
            pltpu.make_async_copy(acc.at[kind], acc_hbm.at[kind], out_sems.at[which]).wait()
        store_of(stage_a, 2 * step - 2, 0).wait()
        store_of(stage_b, 2 * step - 1, 1).wait()


def ffn_stage(idx, normed, gdown, normed_t, gdown_t, w_a, w_b, kern, into, total, carried):
    length, width = normed.shape
    hidden = kern.shape[-1]
    pairs = hidden // (2 * TILE)
    last = 2 * pairs - 1
    now = pl.BlockSpec((width, 2 * TILE), lambda i, idx: (0, jnp.minimum(i, pairs - 1)))
    past = pl.BlockSpec((width, TILE), lambda i, idx: (0, jnp.maximum(2 * i - 1, 0)))
    ahead = pl.BlockSpec((width, TILE), lambda i, idx: (0, jnp.minimum(2 * i + 2, last)))
    small = pl.BlockSpec((9, 2 * TILE), lambda i, idx: (0, jnp.minimum(i, pairs - 1)))
    anywhere = pl.BlockSpec(memory_space=pl.ANY)
    extra = () if carried is None else (carried,)
    lines = TILE // LANES
    halo = pltpu.VMEM((2, lines, PAD_ROWS, LANES), F32)
    outer = pltpu.VMEM((2, length, TILE), BF16)
    stage = pltpu.VMEM((width, 2 * TILE), BF16)
    return pl.pallas_call(
        partial(ffn_kernel, (into, len(extra))),
        out_shape=(
            jax.ShapeDtypeStruct((2, length, width), F32),
            jax.ShapeDtypeStruct((width, total * 2 * TILE), BF16),
            jax.ShapeDtypeStruct((9, hidden), F32),
        ),
        grid_spec=pltpu.PrefetchScalarGridSpec(
            num_scalar_prefetch=1,
            grid=(pairs + 1,),
            in_specs=[anywhere] * 4
            + [now, now, past, past, ahead, ahead, small]
            + [anywhere] * len(extra),
            out_specs=[anywhere, anywhere, small],
            scratch_shapes=[
                pltpu.VMEM((2, length, width), BF16),
                pltpu.VMEM((2, width, length), BF16),
                pltpu.VMEM((2, length, width), F32),
                halo,
                halo,
                pltpu.VMEM((lines, PAD_ROWS, LANES), F32),
                outer,
                outer,
                stage,
                stage,
                pltpu.SemaphoreType.DMA((4,)),
                pltpu.SemaphoreType.DMA((2,)),
                pltpu.SemaphoreType.DMA((2,)),
            ],
        ),
        input_output_aliases={} if carried is None else {12: 1},
        compiler_params=params(),
        name="ffn",
        cost_estimate=cost(38),
    )(idx, normed, gdown, normed_t, gdown_t, w_a, w_b, w_a, w_b, w_a, w_b, kern, *extra)


def middle_kernel(
    idx, perm_ref, res_ref, attn_ref, da_ref, db_ref, ga_ref, gb_ref, cot_ref, ma_ref, mb_ref,
    own_ref, wa_ref, wb_ref, mod_ref,
    out_ref, gres_out, gmix_out, sums_out, keep_out, send_out, ordered, total, gattn_s,
):
    share = own_ref.shape[-1]
    width = res_ref.shape[-1]
    group = pl.program_id(0)
    residual = res_ref[...]
    cot = cot_ref[...].astype(F32)
    down = da_ref[...] + db_ref[...]
    result = residual + mod_ref[5:6, :] * down
    parity = (group // 2) * SIDE + lax.rem(group, 2)
    for row in range(HALF):
        for j in range(width // LANES):
            ordered[j, pl.ds(parity + row * 2 * SIDE, HALF, stride=2), :] = result[
                row * HALF : (row + 1) * HALF, j * LANES : (j + 1) * LANES
            ]
    grad_n = ga_ref[...] + gb_ref[...]
    normed, rstd = norm_rows(residual)
    scaled = grad_n * (1.0 + mod_ref[4:5, :])
    mean_a = jnp.mean(scaled, axis=-1, keepdims=True)
    mean_b = jnp.mean(scaled * normed, axis=-1, keepdims=True)
    gres = cot + rstd * (scaled - mean_a - normed * mean_b)
    gres_out[...] = gres
    sums = jnp.concatenate(
        [
            jnp.sum(gres * attn_ref[...], axis=0, keepdims=True),
            jnp.sum(grad_n, axis=0, keepdims=True),
            jnp.sum(grad_n * normed, axis=0, keepdims=True),
            jnp.sum(cot * down, axis=0, keepdims=True),
        ],
        axis=0,
    )
    gattn = (mod_ref[2:3, :] * gres).astype(BF16)
    gattn_s[...] = gattn
    gmix_out[:, :share] = dot(gattn, own_ref[...]).astype(BF16)
    half = wa_ref.shape[0]
    mine, theirs = half_offsets(idx[1], half)
    gmix_out[:, share:] = (
        dot(gattn_s[:, pl.ds(mine, half)], wa_ref[...]) + dot(gattn_s[:, pl.ds(theirs, half)], wb_ref[...])
    ).astype(BF16)
    gattn_t = dot_nt(perm_ref[...], gattn).astype(BF16)
    part = jnp.concatenate([dot(gattn_t, ma_ref[...]), dot(gattn_t, mb_ref[...])], axis=1)

    @pl.when(group == 0)
    def _():
        sums_out[...] = sums
        total[...] = part

    @pl.when(group > 0)
    def _():
        sums_out[...] += sums
        total[...] += part

    @pl.when(group == GROUPS - 1)
    def _():
        half_rows = width // 2
        keep_out[...] = total[pl.ds(pl.multiple_of(idx[1] * half_rows, half_rows), half_rows), :]
        send_out[...] = total[
            pl.ds(pl.multiple_of((1 - idx[1]) * half_rows, half_rows), half_rows), :
        ].astype(BF16)
        for j in range(width // LANES):
            out_ref[:, j * LANES : (j + 1) * LANES] = ordered[j].astype(BF16)


def middle_stage(idx, perm, res, attn, acc_a, acc_b, cot, mixed, o_own, part_a, part_b, mod):
    half = pl.BlockSpec((TILE, o_own.shape[-1]), lambda g, idx: (g, 0))

    def kind(which):
        return pl.BlockSpec((None, TILE, o_own.shape[0]), lambda g, idx: (which, g, 0))

    length, width = res.shape
    rows = pl.BlockSpec((TILE, width), lambda g, idx: (g, 0))
    half_rows = width // 2
    low = jax.ShapeDtypeStruct((length, width), BF16)
    return pl.pallas_call(
        middle_kernel,
        out_shape=(
            low,
            jax.ShapeDtypeStruct((length, width), F32),
            low,
            jax.ShapeDtypeStruct((4, width), F32),
            jax.ShapeDtypeStruct((half_rows, width), F32),
            jax.ShapeDtypeStruct((half_rows, width), BF16),
        ),
        grid_spec=pltpu.PrefetchScalarGridSpec(
            num_scalar_prefetch=1,
            grid=(GROUPS,),
            in_specs=[whole(perm.shape)]
            + [rows] * 2
            + [kind(1)] * 2
            + [kind(0)] * 2
            + [rows]
            + [half] * 2
            + [whole(o_own.shape), entry(part_a, 3), entry(part_b, 3), whole(mod.shape)],
            out_specs=[
                whole((length, width)),
                rows,
                rows,
                whole((4, width)),
                whole((half_rows, width)),
                whole((half_rows, width)),
            ],
            scratch_shapes=[
                pltpu.VMEM((width // LANES, length, LANES), F32),
                pltpu.VMEM((width, width), F32),
                pltpu.VMEM((TILE, width), BF16),
            ],
        ),
        compiler_params=params(),
        name="middle",
        cost_estimate=cost(17),
    )(idx, perm, res, attn, acc_a, acc_b, acc_a, acc_b, cot, *mixed, o_own, part_a, part_b, mod)


def attend_back_kernel(
    idx, qkv_ref, gmix_ref, valid_ref, convt_ref, okeep_ref, osend_ref, gqkv_out, keep_out, send_out, held
):
    share = qkv_ref.shape[-1] // 3
    group = pl.program_id(0)
    rows = pl.ds(pl.multiple_of(group * TILE, TILE), TILE)
    keep = jnp.broadcast_to(valid_ref[0], (TILE, TILE)) > 0
    lane = lax.broadcasted_iota(jnp.int32, (TILE, LANES), 1)
    pairs = share // LANES

    def part(which, pair):
        first = which * share + pair * LANES
        return qkv_ref[:, first : first + LANES]

    def products_of(pair):
        queries_t, keys, values = turn(part(0, pair)), part(1, pair), part(2, pair)
        gmix_t = turn(gmix_ref[:, pair * LANES : (pair + 1) * LANES])
        return [
            (dot(head_mask(keys, which), queries_t), dot(head_mask(values, which), gmix_t))
            for which in range(2)
        ]

    def weights_of(raw, gprobs):
        probs = soft_keys(raw, keep)
        weighted = probs * gprobs
        gscores = weighted - probs * jnp.sum(weighted, axis=0, keepdims=True)
        return probs.astype(BF16), (gscores * (HEAD_DIM**-0.5)).astype(BF16)

    def finish(pair, weights):
        queries, keys_t = part(0, pair), turn(part(1, pair))
        gmix = gmix_ref[:, pair * LANES : (pair + 1) * LANES]
        gq, gk, gv = [], [], []
        for which, (probs, graw) in enumerate(weights):
            gv.append(dot(probs, gmix))
            gk.append(dot(graw, queries))
            gq.append(dot(keys_t[which * HEAD_DIM : (which + 1) * HEAD_DIM], graw))
        grads = (
            jnp.concatenate(gq, axis=0).T.astype(BF16),
            jnp.where(lane < HEAD_DIM, gk[0], gk[1]).astype(BF16),
            jnp.where(lane < HEAD_DIM, gv[0], gv[1]).astype(BF16),
        )
        for which, grad in enumerate(grads):
            where = slice(which * share + pair * LANES, which * share + (pair + 1) * LANES)
            gqkv_out[:, where] = grad
            held[rows, where] = grad

    ahead, behind = products_of(0), None
    for pair in range(pairs):
        products = ahead
        if pair + 1 < pairs:
            ahead = products_of(pair + 1)
        if behind is not None:
            finish(pair - 1, behind)
        behind = [weights_of(*each) for each in products]
    finish(pairs - 1, behind)

    @pl.when(group == GROUPS - 1)
    def _():
        half_rows = keep_out.shape[0]
        mine, theirs = half_offsets(idx[1], half_rows)
        for which in range(3):
            cols = slice(which * share, (which + 1) * share)
            send_out[:, cols] = dot(convt_ref[pl.ds(theirs, half_rows), :], held[:, cols]).astype(BF16)
            keep_out[:, cols] = dot(convt_ref[pl.ds(mine, half_rows), :], held[:, cols])
        keep_out[:, 3 * share :] = okeep_ref[...]
        send_out[:, 3 * share :] = osend_ref[...]


def attend_back_stage(idx, qkv, gmix, valid, conv_t, out_keep, out_send, side):
    length = gmix.shape[0]
    cols = qkv.shape[-1]
    share = cols // 3
    half_rows = out_keep.shape[0]
    shape = (half_rows, 4 * share)
    part = pl.BlockSpec((half_rows, share), lambda g, idx: (0, side), pipeline_mode=pl.Buffered(1))
    return pl.pallas_call(
        attend_back_kernel,
        out_shape=(
            jax.ShapeDtypeStruct((length, cols), BF16),
            jax.ShapeDtypeStruct(shape, F32),
            jax.ShapeDtypeStruct(shape, BF16),
        ),
        grid_spec=pltpu.PrefetchScalarGridSpec(
            num_scalar_prefetch=1,
            grid=(GROUPS,),
            in_specs=[
                group_rows(cols),
                pl.BlockSpec((TILE, share), lambda g, idx: (g, side)),
                pl.BlockSpec((1, TILE, 1), lambda g, idx: (g, 0, 0)),
                whole(conv_t.shape),
                part,
                part,
            ],
            out_specs=[group_rows(cols), whole(shape), whole(shape)],
            scratch_shapes=[pltpu.VMEM((length, cols), BF16)],
        ),
        compiler_params=params(),
        name="attend_back",
        cost_estimate=cost(18),
    )(idx, qkv, gmix, valid, conv_t, out_keep, out_send)


def conv_back_kernel(
    idx, ga_ref, gb_ref, own_ref, wa_ref, wb_ref, tok_ref, mod_ref, kern_ref,
    grads_out, kern_out, sums_out, grid_g, normed_s,
):
    width = tok_ref.shape[-1]
    count = width // LANES
    share = own_ref.shape[-1]
    half = wa_ref.shape[1]
    step = pl.program_id(0)

    @pl.when(step == 0)
    def _():
        grid_g[...] = jnp.zeros(grid_g.shape, F32)

    for offset, weight_ref in zip(half_offsets(idx[1], half), (wa_ref, wb_ref), strict=True):
        total = None
        for which in range(3):
            cols = slice(which * share, (which + 1) * share)
            part = dot_nt(ga_ref[:, cols], own_ref[which, pl.ds(offset, half), :])
            part += dot_nt(gb_ref[:, cols], weight_ref[which])
            total = part if total is None else total + part
        for side in range(half // LANES):
            lanes = slice(side * LANES, (side + 1) * LANES)
            for row in range(2 * HALF):
                at = (step * 2 + row // HALF) * GROUP_ROWS + pad_row(0, row % HALF)
                grid_g[offset // LANES + side, pl.ds(at, HALF), :] = total[
                    row * HALF : (row + 1) * HALF, lanes
                ]
    normed, _ = norm_rows(tok_ref[...].astype(F32))
    for j in range(count):
        normed_s[j, pl.ds(pl.multiple_of(step * 2 * TILE, 2 * TILE), 2 * TILE), :] = normed[
            :, j * LANES : (j + 1) * LANES
        ]

    @pl.when(step == GROUPS // 2 - 1)
    def _():
        for j in range(count):
            lanes = slice(j * LANES, (j + 1) * LANES)
            taps = taps_of(kern_ref, lanes)

            scale, shift = 1.0 + mod_ref[1:2, lanes], mod_ref[0:1, lanes]

            def backward(row, carry, j=j, lanes=lanes, taps=taps, scale=scale, shift=shift):
                sums, (shift_sum, scale_sum) = carry
                found = neighbours(grid_g, j, row)
                for row_par in range(2):
                    for col_par in range(2):
                        at = pl.multiple_of(group_of(row_par, col_par) * TILE + row * HALF, HALF)
                        normed = normed_s[j, pl.ds(at, HALF), :]
                        grad, sums = conv_back_at(found, taps, sums, normed * scale + shift, row_par, col_par)
                        grads_out[pl.ds(at, HALF), lanes] = grad
                        prod = grad * normed
                        shift_sum = shift_sum + (grad[:8] + grad[8:])
                        scale_sum = scale_sum + (prod[:8] + prod[8:])
                return sums, (shift_sum, scale_sum)

            zero = jnp.zeros((8, LANES), F32)
            sums, pair = lax.fori_loop(0, HALF, backward, (no_sums(), (zero, zero)))
            for which in range(2):
                sums_out[which : which + 1, lanes] = jnp.sum(pair[which], axis=0, keepdims=True)
            for tap in range(9):
                kern_out[tap : tap + 1, lanes] = jnp.sum(sums[tap], axis=0, keepdims=True)


def conv_back_stage(idx, g_own, g_other, w_own, part_a, part_b, tok, mod, kern):
    length, width = tok.shape
    count = width // LANES
    cols = g_own.shape[-1]
    return pl.pallas_call(
        conv_back_kernel,
        out_shape=(
            jax.ShapeDtypeStruct((length, width), F32),
            jax.ShapeDtypeStruct((9, width), F32),
            jax.ShapeDtypeStruct((2, width), F32),
        ),
        grid_spec=pltpu.PrefetchScalarGridSpec(
            num_scalar_prefetch=1,
            grid=(GROUPS // 2,),
            in_specs=[
                pair_rows(cols),
                pair_rows(cols),
                whole(w_own.shape),
                leading(part_a, 3),
                leading(part_b, 3),
                pair_rows(width),
                whole(mod.shape),
                whole(kern.shape),
            ],
            out_specs=[whole((length, width)), whole((9, width)), whole((2, width))],
            scratch_shapes=[
                pltpu.VMEM((count, PAD_ROWS, LANES), F32),
                pltpu.VMEM((count, length, LANES), F32),
            ],
        ),
        compiler_params=params(),
        name="conv_back",
        cost_estimate=cost(18),
    )(idx, g_own, g_other, w_own, part_a, part_b, tok, mod, kern)


def norm_back_kernel(grads_ref, tok_ref, gres_ref, mod_ref, gtok_out, ordered):
    width = tok_ref.shape[-1]
    group = pl.program_id(0)
    grads = grads_ref[...]
    normed, rstd = norm_rows(tok_ref[...].astype(F32))
    scaled = grads * (1.0 + mod_ref[1:2, :])
    mean_a = jnp.mean(scaled, axis=-1, keepdims=True)
    mean_b = jnp.mean(scaled * normed, axis=-1, keepdims=True)
    result = gres_ref[...] + rstd * (scaled - mean_a - normed * mean_b)
    parity = (group // 2) * SIDE + lax.rem(group, 2)
    for row in range(HALF):
        for j in range(width // LANES):
            ordered[j, pl.ds(parity + row * 2 * SIDE, HALF, stride=2), :] = result[
                row * HALF : (row + 1) * HALF, j * LANES : (j + 1) * LANES
            ]

    @pl.when(group == GROUPS - 1)
    def _():
        for j in range(width // LANES):
            gtok_out[:, j * LANES : (j + 1) * LANES] = ordered[j].astype(BF16)


def norm_back_stage(grads, tok, gres, mod):
    length, width = tok.shape
    return pl.pallas_call(
        norm_back_kernel,
        out_shape=jax.ShapeDtypeStruct((length, width), BF16),
        grid=(GROUPS,),
        in_specs=[group_rows(width), group_rows(width), group_rows(width), whole(mod.shape)],
        out_specs=whole((length, width)),
        scratch_shapes=[pltpu.VMEM((width // LANES, length, LANES), F32)],
        compiler_params=params(),
        name="norm_back",
        cost_estimate=cost(6),
    )(grads, tok, gres, mod)


def silu_of(values_in):
    return values_in * jax.nn.sigmoid(values_in)


def swap(values_in, axis, bit):
    size = lax.axis_size(axis)
    return lax.ppermute(values_in, axis, [(i, i ^ bit) for i in range(size)])


def spread(size, position):
    if size < 4:
        return position
    quarter = size // 4
    low, rest = position // (2 * quarter), position % (2 * quarter)
    return (rest % quarter) * 4 + (rest // quarter) * 2 + low


def row_permutation(size, width):
    block = width // size
    order = [spread(size, i // block) * block + i % block for i in range(width)]
    source = jnp.array(order, jnp.int32)
    return (source[:, None] == jnp.arange(width, dtype=jnp.int32)[None, :]).astype(BF16)


def tie(values_in, *first):
    return lax.optimization_barrier((values_in, first))[0]


def halving_bits(size):
    bits = [2] if size > 2 else []
    rest = size // 4
    while rest > 1:
        bits.append(rest * 2)
        rest //= 2
    return bits


def unshuffle(tokens_in):
    blocked = tokens_in.reshape(HALF, 2, HALF, 2)
    return blocked.transpose(1, 3, 0, 2).reshape(GROUPS, TILE)


def local(
    tokens,
    valid,
    steps,
    labels,
    w_mod,
    step_table,
    class_table,
    conv_attn,
    w_qkv,
    w_out,
    conv_ffn,
    w_up,
    w_down,
    cotangent,
):
    dp_size = lax.axis_size("dp")
    width = tokens.shape[-1]
    dp_at = lax.axis_index("dp")
    mp_at = lax.axis_index("mp")
    latent = dp_at * tokens.shape[0] + mp_at
    idx = jnp.stack([mp_at, dp_at % 2, 0]).astype(jnp.int32)
    perm = row_permutation(dp_size, width)

    core = dp_at % 2
    half_rows = width // 2
    hidden = w_up.shape[-1]
    share = w_out.shape[-1]
    rows = width // dp_size
    bits = halving_bits(dp_size)

    def split_rows(total, bit):
        rows = total.shape[-2] // 2
        parts = total.reshape(total.shape[:-2] + (2, rows) + total.shape[-1:])
        axis = parts.ndim - 3
        flag = (dp_at // bit) % 2
        mine = lax.dynamic_index_in_dim(parts, flag, axis, keepdims=False)
        theirs = lax.dynamic_index_in_dim(parts, 1 - flag, axis, keepdims=False)
        return mine, theirs.astype(BF16)

    def last_rows(total, *first):
        if len(bits) < 3:
            sent = []
            for bit in bits[1:]:
                mine, theirs = split_rows(total, bit)
                sent.append(theirs)
                total = mine + swap(theirs, "dp", bit).astype(F32)
            return total, sent
        parts = total.reshape(4, -1, total.shape[-1])
        at = (dp_at // 4) % 4
        kept = lax.dynamic_index_in_dim(parts, at, 0, keepdims=False)
        sent = [
            lax.dynamic_index_in_dim(parts, at ^ by, 0, keepdims=False).astype(BF16) for by in (1, 2, 3)
        ]
        for by, theirs in zip((1, 2, 3), sent, strict=True):
            kept = kept + tie(swap(theirs, "dp", 4 * by), *first).astype(F32)
        return kept, sent

    def both(mine, theirs):
        place = lax.broadcasted_iota(jnp.int32, (2,) + mine.shape, 0)
        return jnp.where(place == mp_at, mine[None], theirs[None])

    qkv_own = w_qkv.transpose(1, 0, 2)
    stack = jnp.concatenate([qkv_own, w_out[None]], axis=0)
    part_a = swap(lax.dynamic_slice_in_dim(stack, core * half_rows, half_rows, axis=1), "mp", 1)

    embedding = jnp.take(step_table, steps, axis=0).astype(F32) + jnp.take(
        class_table, labels, axis=0
    ).astype(F32)
    silu_value, silu_pull = jax.vjp(silu_of, embedding)
    silu_low = silu_value.astype(BF16)
    my_silu = lax.dynamic_slice_in_dim(silu_low, latent, 1)
    mod = modulation_stage(my_silu, w_mod)

    my_valid = lax.dynamic_index_in_dim(valid, mp_at, 0, keepdims=False)
    keep = unshuffle(my_valid)[:, :, None]

    conved, tok, cot = first_stage(idx, tokens, cotangent, mod, conv_attn)
    up_part, down_part = tie((w_up, w_down), conved)
    ffn_part = jnp.where(core == 0, up_part, down_part)
    part_a, keep = tie((part_a, keep), ffn_part)
    part_b = swap(part_a, "dp", 1)
    ffn_part = tie(ffn_part, part_a)
    ffn_a = swap(ffn_part, "mp", 1)
    conv_t, qkv_x, mixed_x = attend_own_stage(tie(conved, ffn_part), keep, qkv_own, perm)
    qkv_y, mixed_y, attn, res, normed, gdown, normed_t, gdown_t = attend_other_stage(
        idx, tie(conved, mixed_x), keep, part_a, part_b, mixed_x, w_out, tok, cot, mod
    )

    chunks = hidden // TILE
    shared = (normed, gdown, normed_t, gdown_t)
    acc_own, grads_ffn, kern_here = ffn_stage(idx, *shared, w_up, w_down, conv_ffn, 0, 2 * chunks, None)
    ffn_a = tie(ffn_a, acc_own)
    ffn_b = swap(ffn_a, "dp", 1)
    kern_other = swap(tie(conv_ffn, ffn_a), "mp", 1)
    idx_other = jnp.stack([mp_at, core, core]).astype(jnp.int32)
    acc_other, grads_ffn, kern_z = ffn_stage(
        idx_other, *shared, ffn_a, ffn_b, kern_other, chunks, 2 * chunks, grads_ffn
    )
    sum_ffn = lax.psum_scatter(grads_ffn, "dp", scatter_dimension=0, tiled=True)
    output, gres, gmix, sums_mid, out_keep, out_send = middle_stage(
        idx, perm, res, attn, acc_own, acc_other, cot, (mixed_x, mixed_y), w_out, part_a, part_b, mod
    )
    top, bottom = jnp.split(output, 2, axis=0)
    top_other = swap(top, "mp", 1)
    g_other, c_keep, c_send = attend_back_stage(idx, qkv_y, gmix, keep, conv_t, out_keep, out_send, 1)
    c_got = swap(c_send, "dp", 1)
    bottom_other = swap(tie(bottom, top_other, c_send), "mp", 1)
    g_own, d_keep, d_send = attend_back_stage(
        idx, qkv_x, tie(gmix, c_send, top_other), keep, conv_t, out_keep, out_send, 0
    )
    c_got = tie(c_got, g_own)
    total_c = (c_keep + c_got.astype(F32)).astype(BF16)
    from_x = swap(tie(total_c, bottom_other), "mp", 1)
    d_got = swap(tie(d_send, bottom_other), "dp", 1)
    grads, kern_a, sums_last = conv_back_stage(
        idx, tie(g_own, total_c, bottom_other), g_other, qkv_own, part_a, part_b, tok, mod, conv_attn
    )

    sent = jnp.concatenate([kern_z.reshape(-1, width), kern_a], axis=0)
    held = jnp.concatenate([kern_here.reshape(-1, width), kern_a], axis=0)
    grad_mod = jnp.concatenate([sums_last, sums_mid], axis=0)
    mine = grad_mod.reshape(1, -1).astype(BF16)
    mod_there, held_there = swap(mine, "mp", 1), swap(sent, "mp", 1)
    gtok = norm_back_stage(tie(grads, mine, sent), tok, gres, mod)

    gtok_other = swap(tie(gtok, mod_there, held_there), "mp", 1)
    d_got, from_x, mod_there, held_there = tie((d_got, from_x, mod_there, held_there), gtok)
    total_d = d_keep + d_got.astype(F32) + from_x.astype(F32)
    mine_d, theirs = split_rows(total_d, bits[0])
    held = held + held_there
    held = held + swap(held, "dp", 1)
    held_y = swap(held, "dp", 2) if dp_size > 2 else None
    got_d = swap(tie(theirs, held), "dp", bits[0])
    gathered = jnp.concatenate([mine, mod_there], axis=0)
    step = 1
    while step < dp_size:
        if 4 * step <= dp_size:
            others = [swap(gathered, "dp", step * by) for by in (1, 2, 3)]
            gathered = jnp.concatenate([gathered, *others], axis=0)
            step *= 4
        else:
            gathered = jnp.concatenate([gathered, swap(gathered, "dp", step)], axis=0)
            step *= 2
    latents = steps.shape[0]
    order = jnp.arange(latents, dtype=jnp.int32) ^ latent.astype(jnp.int32)
    sort = (order[None, :] == jnp.arange(latents, dtype=jnp.int32)[:, None]).astype(BF16)
    grad_mod_low = jnp.dot(sort, gathered, preferred_element_type=F32).astype(BF16)
    grad_silu = jnp.einsum("lc,kc->lk", grad_mod_low, w_mod, preferred_element_type=F32)

    total_d = mine_d + got_d.astype(F32)
    for bit in bits[1:-2]:
        mine_d, theirs = split_rows(total_d, bit)
        total_d = mine_d + swap(theirs, "dp", bit).astype(F32)
    far_ffn = tie(sum_ffn, gtok)[:, 2 * hidden :]
    total_d, sent_d = last_rows(total_d, far_ffn)
    from_f = swap(far_ffn, "mp", 1)
    output, top_other, bottom_other = tie((output, top_other, bottom_other), sent_d)
    whole_output = both(output, jnp.concatenate([top_other, bottom_other], axis=0))
    whole_gtok = both(gtok, tie(gtok_other, whole_output))
    grad_silu, grad_mod_low = tie((grad_silu, grad_mod_low), sent_d, far_ffn)

    if dp_size > 2:
        held = held + held_y
    step = 4
    while step < dp_size:
        held = held + swap(held, "dp", step)
        step *= 2
    kern_f = held[:-9].reshape(9, hidden)
    kern_a = held[-9:]
    (grad_embedding,) = silu_pull(grad_silu)
    my_cols = lax.dynamic_slice_in_dim(silu_low, dp_at * rows, rows, axis=1)
    grad_w_mod = jnp.einsum("lk,lc->kc", my_cols, grad_mod_low, preferred_element_type=F32)

    grad_qkv = total_d[:, : 3 * share].reshape(rows, 3, share)
    grad_out = total_d[:, 3 * share :]
    ffn_sum = sum_ffn[:, : 2 * hidden].astype(F32) + from_f.astype(F32)
    ffn_sum = ffn_sum.reshape(rows, chunks, 2, TILE)
    grad_up = ffn_sum[:, :, 0].reshape(rows, hidden)
    grad_down = ffn_sum[:, :, 1].reshape(rows, hidden)

    def table_grad(indices, count):
        onehot = (jnp.arange(count, dtype=jnp.int32)[:, None] == indices[None, :]).astype(F32)
        return jnp.dot(onehot, grad_embedding, precision=lax.Precision.HIGHEST)

    return (
        whole_output,
        whole_gtok,
        grad_w_mod,
        table_grad(steps, step_table.shape[0]),
        table_grad(labels, class_table.shape[0]),
        kern_a,
        grad_qkv,
        grad_out,
        kern_f,
        grad_up,
        grad_down,
    )


def solution(mesh):
    in_specs = (
        P("dp", None, None),
        P("dp", None),
        P(),
        P(),
        P(),
        P(),
        P(),
        P(),
        P(None, None, "mp"),
        P(None, "mp"),
        P(None, "mp"),
        P(None, "mp"),
        P(None, "mp"),
        P("dp", None, None),
    )
    out_specs = (
        P("dp", None, None),
        P("dp", None, None),
        P("dp", None),
        P(),
        P(),
        P(),
        P("dp", None, "mp"),
        P("dp", "mp"),
        P(None, "mp"),
        P("dp", "mp"),
        P("dp", "mp"),
    )
    return jax.shard_map(local, mesh=mesh, in_specs=in_specs, out_specs=out_specs, check_vma=False)
```

```python
from functools import partial

import jax
import jax.numpy as jnp
from jax import lax
from jax.experimental import pallas as pl
from jax.experimental.pallas import tpu as pltpu
from jax.sharding import PartitionSpec as P

SIDE = 32
HALF = SIDE // 2
HEAD_DIM = 64
GROUPS = 4
LANES = 128
TILE = 256
EPS = 1e-06
PITCH = HALF + 8
GROUP_ROWS = (HALF + 2) * PITCH + 8
PAD_ROWS = GROUPS * GROUP_ROWS
GELU_A = 0.7978845608028654
GELU_B = 0.044715
F32 = jnp.float32
BF16 = jnp.bfloat16
VMEM_BYTES = 60 * 1024 * 1024


def cost(micros):
    return pl.CostEstimate(flops=int(micros * COST_RATE), bytes_accessed=1000, transcendentals=0)


COST_RATE = 400_000_000


def params(count=1):
    return pltpu.CompilerParams(
        dimension_semantics=("arbitrary",) * count, vmem_limit_bytes=VMEM_BYTES
    )


def whole(shape):
    zeros = (0,) * len(shape)
    return pl.BlockSpec(shape, lambda *_: zeros, pipeline_mode=pl.Buffered(1))


def leading(array, count):
    tail = array.shape[1:]
    return pl.BlockSpec((count,) + tail, lambda *_: (0,) * array.ndim, pipeline_mode=pl.Buffered(1))


def entry(array, which):
    tail = (0,) * (array.ndim - 1)
    return pl.BlockSpec(
        (None,) + array.shape[1:], lambda *_: (which,) + tail, pipeline_mode=pl.Buffered(1)
    )


def dot(left, right):
    return jnp.dot(left, right, preferred_element_type=F32)


def dot_nt(left, right):
    return lax.dot_general(left, right, (((1,), (1,)), ((), ())), preferred_element_type=F32)


def pad_row(group, row, shift=0):
    return group * GROUP_ROWS + (row + 1) * PITCH + 8 + shift


AROUND = ((1, -1), (0, 0), (1, 0), (0, 1))


def neighbours(grid_ref, lane_block, row):
    found = []
    for row_par, row_off in AROUND:
        line = []
        for col_par, col_off in AROUND:
            const = pad_row(row_par * 2 + col_par, row_off, col_off)
            line.append(grid_ref[lane_block, pl.ds(row * PITCH + const, HALF), :])
        found.append(line)
    return found


def taps_of(kern_ref, lanes):
    return [
        jnp.broadcast_to(kern_ref[tap : tap + 1, lanes].astype(F32), (HALF, LANES))
        for tap in range(9)
    ]


def conv_at(found, taps, row_par, col_par):
    total = None
    for row_off in range(3):
        for col_off in range(3):
            term = taps[row_off * 3 + col_off] * found[row_par + row_off][col_par + col_off]
            total = term if total is None else total + term
    return total


def conv_back_at(found, taps, sums, source, row_par, col_par):
    total = None
    sums = list(sums)
    for row_off in range(3):
        for col_off in range(3):
            tap = row_off * 3 + col_off
            near = found[row_par + 2 - row_off][col_par + 2 - col_off]
            term = taps[tap] * near
            total = term if total is None else total + term
            part = source * near
            sums[tap] = sums[tap] + (part[:8] + part[8:])
    return total, tuple(sums)


def no_sums():
    return tuple(jnp.zeros((8, LANES), F32) for _ in range(9))


def split_lanes(values_in):
    count = values_in.shape[-1] // LANES
    return [values_in[:, j * LANES : (j + 1) * LANES] for j in range(count)]


def norm_parts(parts):
    width = len(parts) * LANES
    mean = jnp.sum(sum(parts[1:], parts[0]), axis=-1, keepdims=True) * (1.0 / width)
    centre = [part - mean for part in parts]
    squares = [part * part for part in centre]
    var = jnp.sum(sum(squares[1:], squares[0]), axis=-1, keepdims=True) * (1.0 / width)
    rstd = lax.rsqrt(var + EPS)
    return [part * rstd for part in centre], rstd


def norm_rows(values_in):
    mean = jnp.mean(values_in, axis=-1, keepdims=True)
    centre = values_in - mean
    rstd = lax.rsqrt(jnp.mean(centre * centre, axis=-1, keepdims=True) + EPS)
    return centre * rstd, rstd


def modulation_kernel(silu_ref, weight_ref, mod_out):
    width = silu_ref.shape[-1]
    left = jnp.broadcast_to(silu_ref[...].astype(F32), (16, width)).astype(BF16)
    for which in range(weight_ref.shape[-1] // width):
        row = pl.program_id(0) * 2 + which
        mod_out[pl.ds(row, 1), :] = dot(left, weight_ref[:, which * width : (which + 1) * width])[:1]


def modulation_stage(silu_low, w_mod):
    width = silu_low.shape[-1]
    return pl.pallas_call(
        modulation_kernel,
        out_shape=jax.ShapeDtypeStruct((w_mod.shape[-1] // width, width), F32),
        grid=(w_mod.shape[-1] // (2 * width),),
        in_specs=[whole(silu_low.shape), pl.BlockSpec((width, 2 * width), lambda i: (0, i))],
        out_specs=whole((w_mod.shape[-1] // width, width)),
        compiler_params=params(),
        name="modulation",
        cost_estimate=cost(5),
    )(silu_low, w_mod)


def group_of(row_par, col_par):
    return row_par * 2 + col_par


def first_kernel(
    idx, tok_ref, cot_ref, mod_ref, kern_ref, conv_out, tok_out, cot_out, tok_tmp, cot_tmp, grid
):
    width = tok_ref.shape[-1]
    count = width // LANES
    grid[...] = jnp.zeros(grid.shape, F32)

    def one_row(row, carry):
        for row_par in range(2):
            start = pl.multiple_of((row * 2 + row_par) * SIDE, SIDE)
            values = tok_ref[0, pl.ds(start, SIDE), :].astype(F32)
            grads = cot_ref[0, pl.ds(start, SIDE), :].astype(F32)
            for j in range(count):
                tok_tmp[row_par, j] = values[:, j * LANES : (j + 1) * LANES]
                cot_tmp[row_par, j] = grads[:, j * LANES : (j + 1) * LANES]
        places = [(row_par, col_par) for row_par in range(2) for col_par in range(2)]
        parts = []
        for j in range(count):
            lanes = slice(j * LANES, (j + 1) * LANES)
            lines = []
            for row_par, col_par in places:
                out_row = pl.multiple_of(group_of(row_par, col_par) * TILE + row * HALF, HALF)
                line = tok_tmp[row_par, j, pl.ds(col_par, HALF, stride=2), :]
                lines.append(line)
                tok_out[pl.ds(out_row, HALF), lanes] = line.astype(BF16)
                cot_out[pl.ds(out_row, HALF), lanes] = cot_tmp[
                    row_par, j, pl.ds(col_par, HALF, stride=2), :
                ].astype(BF16)
            parts.append(jnp.concatenate(lines, axis=0))
        normed, _ = norm_parts(parts)
        for j in range(count):
            lanes = slice(j * LANES, (j + 1) * LANES)
            value = normed[j] * (1.0 + mod_ref[1:2, lanes]) + mod_ref[0:1, lanes]
            for at, (row_par, col_par) in enumerate(places):
                grid[j, pl.ds(row * PITCH + pad_row(group_of(row_par, col_par), 0), HALF), :] = value[
                    at * HALF : (at + 1) * HALF
                ]
        return carry

    lax.fori_loop(0, HALF, one_row, 0)
    for j in range(count):
        lanes = slice(j * LANES, (j + 1) * LANES)
        taps = taps_of(kern_ref, lanes)

        def one_conv(row, carry, j=j, lanes=lanes, taps=taps):
            found = neighbours(grid, j, row)
            for row_par in range(2):
                for col_par in range(2):
                    out_row = pl.multiple_of(group_of(row_par, col_par) * TILE + row * HALF, HALF)
                    value = conv_at(found, taps, row_par, col_par)
                    conv_out[pl.ds(out_row, HALF), lanes] = value.astype(BF16)
            return carry

        lax.fori_loop(0, HALF, one_conv, 0)


def first_stage(idx, tokens, cotangent, mod, kern):
    _, length, width = tokens.shape
    shape = jax.ShapeDtypeStruct((length, width), BF16)
    mine = pl.BlockSpec((1, length, width), lambda i, idx: (idx[0], 0, 0))
    return pl.pallas_call(
        first_kernel,
        out_shape=(shape, shape, shape),
        grid_spec=pltpu.PrefetchScalarGridSpec(
            num_scalar_prefetch=1,
            grid=(1,),
            in_specs=[mine, mine, whole(mod.shape), whole(kern.shape)],
            out_specs=[whole((length, width))] * 3,
            scratch_shapes=[
                pltpu.VMEM((2, width // LANES, SIDE, LANES), F32),
                pltpu.VMEM((2, width // LANES, SIDE, LANES), F32),
                pltpu.VMEM((width // LANES, PAD_ROWS, LANES), F32),
            ],
        ),
        compiler_params=params(),
        name="norm_conv",
        cost_estimate=cost(11),
    )(idx, tokens, cotangent, mod, kern)


def head_mask(values_in, which):
    lane = lax.broadcasted_iota(jnp.int32, values_in.shape, 1)
    keep = lane < HEAD_DIM if which == 0 else lane >= HEAD_DIM
    return jnp.where(keep, values_in, jnp.zeros_like(values_in))


def turn(values_in):
    return values_in.astype(F32).T.astype(BF16)


def soft_keys(raw, keep):
    scores = jnp.where(keep, raw * (HEAD_DIM**-0.5), -1e30)
    exponent = jnp.exp(scores - jnp.max(scores, axis=0, keepdims=True))
    return exponent * (1.0 / jnp.sum(exponent, axis=0, keepdims=True))


def attend_heads(keep, share, qkv_out, mixed_out):
    def part(which, pair):
        first = which * share + pair * LANES
        return qkv_out[:, first : first + LANES]

    def scores_of(pair):
        queries_t, keys = turn(part(0, pair)), part(1, pair)
        return [dot(head_mask(keys, which), queries_t) for which in range(2)]

    pairs = share // LANES
    ahead = scores_of(0)
    for pair in range(pairs):
        raws = ahead
        values_t = turn(part(2, pair))
        if pair + 1 < pairs:
            ahead = scores_of(pair + 1)
        probs = [soft_keys(raw, keep).astype(BF16) for raw in raws]
        halves = [dot(values_t[w * HEAD_DIM : (w + 1) * HEAD_DIM], probs[w]) for w in range(2)]
        mixed_out[:, pair * LANES : (pair + 1) * LANES] = jnp.concatenate(halves, axis=0).T.astype(BF16)


def half_offsets(core, size):
    mine = pl.multiple_of(core * size, size)
    theirs = pl.multiple_of((1 - core) * size, size)
    return mine, theirs


def attend_own_kernel(conv_ref, valid_ref, weight_ref, perm_ref, convt_out, qkv_out, mixed_out):
    conved = conv_ref[...]
    share = weight_ref.shape[-1]
    for which in range(3):
        qkv_out[:, which * share : (which + 1) * share] = dot(conved, weight_ref[which]).astype(BF16)
    convt_out[...] = dot_nt(perm_ref[...], conved).astype(BF16)
    keep = jnp.broadcast_to(valid_ref[0], (TILE, TILE)) > 0
    attend_heads(keep, share, qkv_out, mixed_out)


def attend_other_kernel(
    idx, conv_ref, valid_ref, wa_ref, wb_ref, mown_ref, own_ref, tok_ref, cot_ref, mod_ref,
    qkv_out, mixed_out, attn_out, res_out, norm_out, gdown_out, normt_out, gdownt_out,
):
    keep = jnp.broadcast_to(valid_ref[0], (TILE, TILE)) > 0
    share = wa_ref.shape[-1]
    half = wa_ref.shape[1]
    mine, theirs = half_offsets(idx[1], half)
    left_a, left_b = conv_ref[:, pl.ds(mine, half)], conv_ref[:, pl.ds(theirs, half)]
    for which in range(3):
        qkv_out[:, which * share : (which + 1) * share] = (
            dot(left_a, wa_ref[which]) + dot(left_b, wb_ref[which])
        ).astype(BF16)
    attend_heads(keep, share, qkv_out, mixed_out)
    for offset, weight_ref in ((mine, wa_ref), (theirs, wb_ref)):
        attn_out[:, pl.ds(offset, half)] = dot_nt(
            mown_ref[...], own_ref[pl.ds(offset, half), :]
        ) + dot_nt(mixed_out[...], weight_ref[3])
    attn = attn_out[...]
    residual = tok_ref[...].astype(F32) + mod_ref[2:3, :] * attn
    res_out[...] = residual
    normed, _ = norm_rows(residual)
    normed = normed * (1.0 + mod_ref[4:5, :]) + mod_ref[3:4, :]
    norm_out[...] = normed.astype(BF16)
    normt_out[...] = normed.T.astype(BF16)
    gdown = mod_ref[5:6, :] * cot_ref[...].astype(F32)
    gdown_out[...] = gdown.astype(BF16)
    gdownt_out[...] = gdown.T.astype(BF16)


def group_rows(cols):
    return pl.BlockSpec((TILE, cols), lambda g, *_: (g, 0))


def pair_rows(cols):
    return pl.BlockSpec((2 * TILE, cols), lambda i, *_: (i, 0))


def attend_own_stage(conved, valid, w_own, perm):
    length, width = conved.shape
    share = w_own.shape[-1]
    return pl.pallas_call(
        attend_own_kernel,
        out_shape=(
            jax.ShapeDtypeStruct((width, length), BF16),
            jax.ShapeDtypeStruct((length, 3 * share), BF16),
            jax.ShapeDtypeStruct((length, share), BF16),
        ),
        grid=(GROUPS,),
        in_specs=[
            group_rows(width),
            pl.BlockSpec((1, TILE, 1), lambda g: (g, 0, 0)),
            whole(w_own.shape),
            whole(perm.shape),
        ],
        out_specs=[
            pl.BlockSpec((width, TILE), lambda g: (0, g)),
            group_rows(3 * share),
            group_rows(share),
        ],
        compiler_params=params(),
        name="attend_own",
        cost_estimate=cost(14),
    )(conved, valid, w_own, perm)


def attend_other_stage(idx, conved, valid, part_a, part_b, mixed_own, o_own, tok, cot, mod):
    length, width = conved.shape
    share = part_a.shape[-1]
    low = jax.ShapeDtypeStruct((length, width), BF16)
    high = jax.ShapeDtypeStruct((length, width), F32)
    turned = jax.ShapeDtypeStruct((width, length), BF16)
    return pl.pallas_call(
        attend_other_kernel,
        out_shape=(
            jax.ShapeDtypeStruct((length, 3 * share), BF16),
            jax.ShapeDtypeStruct((length, share), BF16),
            high,
            high,
            low,
            low,
            turned,
            turned,
        ),
        grid_spec=pltpu.PrefetchScalarGridSpec(
            num_scalar_prefetch=1,
            grid=(GROUPS,),
            in_specs=[
                group_rows(width),
                pl.BlockSpec((1, TILE, 1), lambda g, idx: (g, 0, 0)),
                whole(part_a.shape),
                whole(part_b.shape),
                group_rows(share),
                whole(o_own.shape),
                group_rows(width),
                group_rows(width),
                whole(mod.shape),
            ],
            out_specs=[group_rows(3 * share), group_rows(share)]
            + [group_rows(width)] * 4
            + [pl.BlockSpec((width, TILE), lambda g, idx: (0, g))] * 2,
        ),
        compiler_params=params(),
        name="attend_other",
        cost_estimate=cost(20),
    )(idx, conved, valid, part_a, part_b, mixed_own, o_own, tok, cot, mod)


def gelu_pair(value):
    square = value * value
    inner = jnp.tanh(GELU_A * (value + GELU_B * (square * value)))
    cdf = 0.5 * (1.0 + inner)
    slope = cdf + (value * (0.5 * GELU_A)) * (1.0 - inner * inner) * (1.0 + (3.0 * GELU_B) * square)
    return value * cdf, slope


def ffn_kernel(
    where, idx, norm_hbm, gdown_hbm, normt_hbm, gdownt_hbm,
    a_now, b_now, a_past, b_past, a_next, b_next, kern_ref, *refs,
):
    into, carried = where
    refs = refs[carried:]
    acc_hbm, grads_hbm, kern_out = refs[:3]
    inputs, turned, acc, halo_a, halo_b, halo_gz, outer_a, outer_b, stage_a, stage_b, in_sems, g_sems, out_sems = refs[3:]
    step = pl.program_id(0)
    count = pl.num_programs(0) - 1
    role = idx[2]
    width = inputs.shape[-1]
    rows_t = turned.shape[1] // GROUPS
    loads = [
        pltpu.make_async_copy(src, dst, in_sems.at[i])
        for i, (src, dst) in enumerate(
            (
                (norm_hbm, inputs.at[0]),
                (gdown_hbm, inputs.at[1]),
                (normt_hbm, turned.at[0]),
                (gdownt_hbm, turned.at[1]),
            )
        )
    ]

    def kind_of(which):
        return jnp.bitwise_xor(role, which)

    def group_slice(group):
        return pl.ds(pl.multiple_of(group * TILE, TILE), TILE)

    def before(halo, which, weight_ref, cols, piece, pieces):
        kind = kind_of(which)
        groups = GROUPS // pieces
        value = dot(inputs[kind, piece * groups * TILE : (piece + 1) * groups * TILE, :], weight_ref[:, cols])
        for group in range(groups):
            for line in range(TILE // LANES):
                for row in range(HALF):
                    at = group * TILE + row * HALF
                    halo[kind, line, pl.ds(pad_row(piece * groups + group, row), HALF), :] = value[
                        at : at + HALF, line * LANES : (line + 1) * LANES
                    ]

    def after(outer, stage, which, weight_ref, cols, piece):
        kind = kind_of(which)
        block, half = piece // 2, piece % 2
        if block < width // TILE:
            out_cols = slice(block * TILE, (block + 1) * TILE)
            rows = slice(half * 2 * TILE, (half + 1) * 2 * TILE)
            acc[kind, rows, out_cols] += dot_nt(outer[kind, rows, :], weight_ref[out_cols, cols])
        else:
            rows = slice(half * width // 2, (half + 1) * width // 2)
            stage[rows, which * TILE : (which + 1) * TILE] = dot(turned[which, rows, :], outer[which]).astype(BF16)

    def forward(halo, outer, which, first, taps):
        lanes = slice(which * LANES, (which + 1) * LANES)
        for row in (2 * first, 2 * first + 1):
            found = neighbours(halo.at[0], which, row)
            for row_par in range(2):
                for col_par in range(2):
                    group = group_of(row_par, col_par)
                    out_row = pl.multiple_of(group * TILE + row * HALF, HALF)
                    centre = pl.ds(row * PITCH + pad_row(group, 0), HALF)
                    act, slope = gelu_pair(conv_at(found, taps, row_par, col_par))
                    outer[1, pl.ds(out_row, HALF), lanes] = act.astype(BF16)
                    halo_gz[which, centre, :] = halo[1, which, centre, :] * slope

    def backward(halo, outer, which, first, taps, sums):
        lanes = slice(which * LANES, (which + 1) * LANES)
        for row in (2 * first, 2 * first + 1):
            found = neighbours(halo_gz, which, row)
            for row_par in range(2):
                for col_par in range(2):
                    group = group_of(row_par, col_par)
                    out_row = pl.multiple_of(group * TILE + row * HALF, HALF)
                    source = halo[0, which, pl.ds(row * PITCH + pad_row(group, 0), HALF), :]
                    grad, sums = conv_back_at(found, taps, sums, source, row_par, col_par)
                    outer[0, pl.ds(out_row, HALF), lanes] = grad.astype(BF16)
        return sums

    def one_chunk(second, halo, outer, past, ahead):
        past_outer, past_stage, past_weights, past_cols = past
        next_halo, next_weights, next_cols = ahead
        base = TILE if second else 0
        for which in range(2):
            taps = taps_of(kern_ref, slice(base + which * LANES, base + (which + 1) * LANES))

            for first in range(HALF // 2):
                after(past_outer, past_stage, which, past_weights[which], past_cols, first)
                forward(halo, outer, which, first, taps)
        for which in range(2):
            lanes = slice(base + which * LANES, base + (which + 1) * LANES)
            taps = taps_of(kern_ref, lanes)

            sums = no_sums()
            for first in range(HALF // 2):
                if first % (8 // 4) == 0:
                    before(next_halo, which, next_weights[which], next_cols, first // (8 // 4), 4)
                sums = backward(halo, outer, which, first, taps, sums)
            for tap in range(9):
                kern_out[tap : tap + 1, lanes] = jnp.sum(sums[tap], axis=0, keepdims=True)

    def store_of(stage, chunk, sem):
        cols = pl.ds(pl.multiple_of((into + chunk) * (2 * TILE), 2 * TILE), 2 * TILE)
        return pltpu.make_async_copy(stage, grads_hbm.at[:, cols], g_sems.at[sem])

    left_cols, right_cols, all_cols = slice(0, TILE), slice(TILE, 2 * TILE), slice(0, TILE)

    @pl.when(step == 0)
    def _():
        for load in loads:
            load.start()
        for ref in (acc, outer_b):
            ref[...] = jnp.zeros(ref.shape, ref.dtype)
        for line in range(TILE // LANES):
            for halo in (halo_a.at[0, line], halo_b.at[0, line], halo_gz.at[line]):
                for group in range(GROUPS):
                    for row in range(-1, HALF + 2):
                        size = PITCH if row in (-1, HALF) else 8
                        halo[pl.ds(pad_row(group, row) - 8, size), :] = jnp.zeros((size, LANES), F32)
        for load in loads:
            load.wait()

        for which, weight_ref in enumerate((a_now, b_now)):
            before(halo_a, which, weight_ref, left_cols, 0, 1)

    @pl.when(jnp.logical_and(step > 1, step < count))
    def _():
        store_of(stage_b, 2 * step - 3, 1).wait()

    @pl.when(step < count)
    def _():
        one_chunk(
            False, halo_a, outer_a,
            (outer_b, stage_b, (a_past, b_past), all_cols), (halo_b, (a_now, b_now), right_cols),
        )

        @pl.when(step > 0)
        def _():
            store_of(stage_b, 2 * step - 1, 1).start()
            store_of(stage_a, 2 * step - 2, 0).wait()

        one_chunk(
            True, halo_b, outer_b,
            (outer_a, stage_a, (a_now, b_now), left_cols), (halo_a, (a_next, b_next), all_cols),
        )
        store_of(stage_a, 2 * step, 0).start()

    @pl.when(step == count)
    def _():
        pl.when(count > 1)(lambda: store_of(stage_b, 2 * step - 3, 1).wait())
        for which, weight_ref in enumerate((a_past, b_past)):
            kind = kind_of(which)
            for piece in range(2 * (width // TILE + 1)):
                after(outer_b, stage_b, which, weight_ref, all_cols, piece)
            pltpu.make_async_copy(acc.at[kind], acc_hbm.at[kind], out_sems.at[which]).start()
        store_of(stage_b, 2 * step - 1, 1).start()
        for which in range(2):
            kind = kind_of(which)
            pltpu.make_async_copy(acc.at[kind], acc_hbm.at[kind], out_sems.at[which]).wait()
        store_of(stage_a, 2 * step - 2, 0).wait()
        store_of(stage_b, 2 * step - 1, 1).wait()


def ffn_stage(idx, normed, gdown, normed_t, gdown_t, w_a, w_b, kern, into, total, carried):
    length, width = normed.shape
    hidden = kern.shape[-1]
    pairs = hidden // (2 * TILE)
    last = 2 * pairs - 1
    now = pl.BlockSpec((width, 2 * TILE), lambda i, idx: (0, jnp.minimum(i, pairs - 1)))
    past = pl.BlockSpec((width, TILE), lambda i, idx: (0, jnp.maximum(2 * i - 1, 0)))
    ahead = pl.BlockSpec((width, TILE), lambda i, idx: (0, jnp.minimum(2 * i + 2, last)))
    small = pl.BlockSpec((9, 2 * TILE), lambda i, idx: (0, jnp.minimum(i, pairs - 1)))
    anywhere = pl.BlockSpec(memory_space=pl.ANY)
    extra = () if carried is None else (carried,)
    lines = TILE // LANES
    halo = pltpu.VMEM((2, lines, PAD_ROWS, LANES), F32)
    outer = pltpu.VMEM((2, length, TILE), BF16)
    stage = pltpu.VMEM((width, 2 * TILE), BF16)
    return pl.pallas_call(
        partial(ffn_kernel, (into, len(extra))),
        out_shape=(
            jax.ShapeDtypeStruct((2, length, width), F32),
            jax.ShapeDtypeStruct((width, total * 2 * TILE), BF16),
            jax.ShapeDtypeStruct((9, hidden), F32),
        ),
        grid_spec=pltpu.PrefetchScalarGridSpec(
            num_scalar_prefetch=1,
            grid=(pairs + 1,),
            in_specs=[anywhere] * 4
            + [now, now, past, past, ahead, ahead, small]
            + [anywhere] * len(extra),
            out_specs=[anywhere, anywhere, small],
            scratch_shapes=[
                pltpu.VMEM((2, length, width), BF16),
                pltpu.VMEM((2, width, length), BF16),
                pltpu.VMEM((2, length, width), F32),
                halo,
                halo,
                pltpu.VMEM((lines, PAD_ROWS, LANES), F32),
                outer,
                outer,
                stage,
                stage,
                pltpu.SemaphoreType.DMA((4,)),
                pltpu.SemaphoreType.DMA((2,)),
                pltpu.SemaphoreType.DMA((2,)),
            ],
        ),
        input_output_aliases={} if carried is None else {12: 1},
        compiler_params=params(),
        name="ffn",
        cost_estimate=cost(38),
    )(idx, normed, gdown, normed_t, gdown_t, w_a, w_b, w_a, w_b, w_a, w_b, kern, *extra)


def middle_kernel(
    idx, perm_ref, res_ref, attn_ref, da_ref, db_ref, ga_ref, gb_ref, cot_ref, ma_ref, mb_ref,
    own_ref, wa_ref, wb_ref, mod_ref,
    top_ref, bottom_ref, gres_out, gmix_out, sums_out, keep_out, send_out, ordered, total, gattn_s,
):
    share = own_ref.shape[-1]
    width = res_ref.shape[-1]
    group = pl.program_id(0)
    residual = res_ref[...]
    cot = cot_ref[...].astype(F32)
    down = da_ref[...] + db_ref[...]
    result = residual + mod_ref[5:6, :] * down
    parity = (group // 2) * SIDE + lax.rem(group, 2)
    for row in range(HALF):
        for j in range(width // LANES):
            ordered[j, pl.ds(parity + row * 2 * SIDE, HALF, stride=2), :] = result[
                row * HALF : (row + 1) * HALF, j * LANES : (j + 1) * LANES
            ]
    grad_n = ga_ref[...] + gb_ref[...]
    normed, rstd = norm_rows(residual)
    scaled = grad_n * (1.0 + mod_ref[4:5, :])
    mean_a = jnp.mean(scaled, axis=-1, keepdims=True)
    mean_b = jnp.mean(scaled * normed, axis=-1, keepdims=True)
    gres = cot + rstd * (scaled - mean_a - normed * mean_b)
    gres_out[...] = gres
    sums = jnp.concatenate(
        [
            jnp.sum(gres * attn_ref[...], axis=0, keepdims=True),
            jnp.sum(grad_n, axis=0, keepdims=True),
            jnp.sum(grad_n * normed, axis=0, keepdims=True),
            jnp.sum(cot * down, axis=0, keepdims=True),
        ],
        axis=0,
    )
    gattn = (mod_ref[2:3, :] * gres).astype(BF16)
    gattn_s[...] = gattn
    gmix_out[:, :share] = dot(gattn, own_ref[...]).astype(BF16)
    half = wa_ref.shape[0]
    mine, theirs = half_offsets(idx[1], half)
    gmix_out[:, share:] = (
        dot(gattn_s[:, pl.ds(mine, half)], wa_ref[...]) + dot(gattn_s[:, pl.ds(theirs, half)], wb_ref[...])
    ).astype(BF16)
    gattn_t = dot_nt(perm_ref[...], gattn).astype(BF16)
    part = jnp.concatenate([dot(gattn_t, ma_ref[...]), dot(gattn_t, mb_ref[...])], axis=1)

    @pl.when(group == 0)
    def _():
        sums_out[...] = sums
        total[...] = part

    @pl.when(group > 0)
    def _():
        sums_out[...] += sums
        total[...] += part

    @pl.when(group == GROUPS - 1)
    def _():
        half_rows = width // 2
        keep_out[...] = total[pl.ds(pl.multiple_of(idx[1] * half_rows, half_rows), half_rows), :]
        send_out[...] = total[
            pl.ds(pl.multiple_of((1 - idx[1]) * half_rows, half_rows), half_rows), :
        ].astype(BF16)
        for j in range(width // LANES):
            lanes = slice(j * LANES, (j + 1) * LANES)
            for at, half_ref in enumerate((top_ref, bottom_ref)):
                size = half_ref.shape[0]
                half_ref[:, lanes] = ordered[j, at * size : (at + 1) * size, :].astype(BF16)


def middle_stage(idx, perm, res, attn, acc_a, acc_b, cot, mixed, o_own, part_a, part_b, mod):
    half = pl.BlockSpec((TILE, o_own.shape[-1]), lambda g, idx: (g, 0))

    def kind(which):
        return pl.BlockSpec((None, TILE, o_own.shape[0]), lambda g, idx: (which, g, 0))

    length, width = res.shape
    rows = pl.BlockSpec((TILE, width), lambda g, idx: (g, 0))
    half_rows = width // 2
    low = jax.ShapeDtypeStruct((length, width), BF16)
    piece = jax.ShapeDtypeStruct((length // 2, width), BF16)
    return pl.pallas_call(
        middle_kernel,
        out_shape=(
            piece,
            piece,
            jax.ShapeDtypeStruct((length, width), F32),
            low,
            jax.ShapeDtypeStruct((4, width), F32),
            jax.ShapeDtypeStruct((half_rows, width), F32),
            jax.ShapeDtypeStruct((half_rows, width), BF16),
        ),
        grid_spec=pltpu.PrefetchScalarGridSpec(
            num_scalar_prefetch=1,
            grid=(GROUPS,),
            in_specs=[whole(perm.shape)]
            + [rows] * 2
            + [kind(1)] * 2
            + [kind(0)] * 2
            + [rows]
            + [half] * 2
            + [whole(o_own.shape), entry(part_a, 3), entry(part_b, 3), whole(mod.shape)],
            out_specs=[
                whole(piece.shape),
                whole(piece.shape),
                rows,
                rows,
                whole((4, width)),
                whole((half_rows, width)),
                whole((half_rows, width)),
            ],
            scratch_shapes=[
                pltpu.VMEM((width // LANES, length, LANES), F32),
                pltpu.VMEM((width, width), F32),
                pltpu.VMEM((TILE, width), BF16),
            ],
        ),
        compiler_params=params(),
        name="middle",
        cost_estimate=cost(17),
    )(idx, perm, res, attn, acc_a, acc_b, acc_a, acc_b, cot, *mixed, o_own, part_a, part_b, mod)


def attend_back_kernel(
    idx, qkv_ref, gmix_ref, valid_ref, convt_ref, okeep_ref, osend_ref, gqkv_out, keep_out, send_out, held
):
    share = qkv_ref.shape[-1] // 3
    group = pl.program_id(0)
    rows = pl.ds(pl.multiple_of(group * TILE, TILE), TILE)
    keep = jnp.broadcast_to(valid_ref[0], (TILE, TILE)) > 0
    lane = lax.broadcasted_iota(jnp.int32, (TILE, LANES), 1)
    pairs = share // LANES

    def part(which, pair):
        first = which * share + pair * LANES
        return qkv_ref[:, first : first + LANES]

    def products_of(pair):
        queries_t, keys, values = turn(part(0, pair)), part(1, pair), part(2, pair)
        gmix_t = turn(gmix_ref[:, pair * LANES : (pair + 1) * LANES])
        return [
            (dot(head_mask(keys, which), queries_t), dot(head_mask(values, which), gmix_t))
            for which in range(2)
        ]

    def weights_of(raw, gprobs):
        probs = soft_keys(raw, keep)
        weighted = probs * gprobs
        gscores = weighted - probs * jnp.sum(weighted, axis=0, keepdims=True)
        return probs.astype(BF16), (gscores * (HEAD_DIM**-0.5)).astype(BF16)

    def finish(pair, weights):
        queries, keys_t = part(0, pair), turn(part(1, pair))
        gmix = gmix_ref[:, pair * LANES : (pair + 1) * LANES]
        gq, gk, gv = [], [], []
        for which, (probs, graw) in enumerate(weights):
            gv.append(dot(probs, gmix))
            gk.append(dot(graw, queries))
            gq.append(dot(keys_t[which * HEAD_DIM : (which + 1) * HEAD_DIM], graw))
        grads = (
            jnp.concatenate(gq, axis=0).T.astype(BF16),
            jnp.where(lane < HEAD_DIM, gk[0], gk[1]).astype(BF16),
            jnp.where(lane < HEAD_DIM, gv[0], gv[1]).astype(BF16),
        )
        for which, grad in enumerate(grads):
            where = slice(which * share + pair * LANES, which * share + (pair + 1) * LANES)
            gqkv_out[:, where] = grad
            held[rows, where] = grad

    ahead, behind = products_of(0), None
    for pair in range(pairs):
        products = ahead
        if pair + 1 < pairs:
            ahead = products_of(pair + 1)
        if behind is not None:
            finish(pair - 1, behind)
        behind = [weights_of(*each) for each in products]
    finish(pairs - 1, behind)

    @pl.when(group == GROUPS - 1)
    def _():
        half_rows = keep_out.shape[0]
        mine, theirs = half_offsets(idx[1], half_rows)
        for which in range(3):
            cols = slice(which * share, (which + 1) * share)
            send_out[:, cols] = dot(convt_ref[pl.ds(theirs, half_rows), :], held[:, cols]).astype(BF16)
            keep_out[:, cols] = dot(convt_ref[pl.ds(mine, half_rows), :], held[:, cols])
        keep_out[:, 3 * share :] = okeep_ref[...]
        send_out[:, 3 * share :] = osend_ref[...]


def attend_back_stage(idx, qkv, gmix, valid, conv_t, out_keep, out_send, side):
    length = gmix.shape[0]
    cols = qkv.shape[-1]
    share = cols // 3
    half_rows = out_keep.shape[0]
    shape = (half_rows, 4 * share)
    part = pl.BlockSpec((half_rows, share), lambda g, idx: (0, side), pipeline_mode=pl.Buffered(1))
    return pl.pallas_call(
        attend_back_kernel,
        out_shape=(
            jax.ShapeDtypeStruct((length, cols), BF16),
            jax.ShapeDtypeStruct(shape, F32),
            jax.ShapeDtypeStruct(shape, BF16),
        ),
        grid_spec=pltpu.PrefetchScalarGridSpec(
            num_scalar_prefetch=1,
            grid=(GROUPS,),
            in_specs=[
                group_rows(cols),
                pl.BlockSpec((TILE, share), lambda g, idx: (g, side)),
                pl.BlockSpec((1, TILE, 1), lambda g, idx: (g, 0, 0)),
                whole(conv_t.shape),
                part,
                part,
            ],
            out_specs=[group_rows(cols), whole(shape), whole(shape)],
            scratch_shapes=[pltpu.VMEM((length, cols), BF16)],
        ),
        compiler_params=params(),
        name="attend_back",
        cost_estimate=cost(18),
    )(idx, qkv, gmix, valid, conv_t, out_keep, out_send)


def conv_back_kernel(
    idx, ga_ref, gb_ref, own_ref, wa_ref, wb_ref, tok_ref, mod_ref, kern_ref,
    grads_out, kern_out, sums_out, grid_g, normed_s,
):
    width = tok_ref.shape[-1]
    count = width // LANES
    share = own_ref.shape[-1]
    half = wa_ref.shape[1]
    step = pl.program_id(0)

    @pl.when(step == 0)
    def _():
        grid_g[...] = jnp.zeros(grid_g.shape, F32)

    for offset, weight_ref in zip(half_offsets(idx[1], half), (wa_ref, wb_ref), strict=True):
        total = None
        for which in range(3):
            cols = slice(which * share, (which + 1) * share)
            part = dot_nt(ga_ref[:, cols], own_ref[which, pl.ds(offset, half), :])
            part += dot_nt(gb_ref[:, cols], weight_ref[which])
            total = part if total is None else total + part
        for side in range(half // LANES):
            lanes = slice(side * LANES, (side + 1) * LANES)
            for row in range(2 * HALF):
                at = (step * 2 + row // HALF) * GROUP_ROWS + pad_row(0, row % HALF)
                grid_g[offset // LANES + side, pl.ds(at, HALF), :] = total[
                    row * HALF : (row + 1) * HALF, lanes
                ]
    normed, _ = norm_rows(tok_ref[...].astype(F32))
    for j in range(count):
        normed_s[j, pl.ds(pl.multiple_of(step * 2 * TILE, 2 * TILE), 2 * TILE), :] = normed[
            :, j * LANES : (j + 1) * LANES
        ]

    @pl.when(step == GROUPS // 2 - 1)
    def _():
        for j in range(count):
            lanes = slice(j * LANES, (j + 1) * LANES)
            taps = taps_of(kern_ref, lanes)

            scale, shift = 1.0 + mod_ref[1:2, lanes], mod_ref[0:1, lanes]

            def backward(row, carry, j=j, lanes=lanes, taps=taps, scale=scale, shift=shift):
                sums, (shift_sum, scale_sum) = carry
                found = neighbours(grid_g, j, row)
                for row_par in range(2):
                    for col_par in range(2):
                        at = pl.multiple_of(group_of(row_par, col_par) * TILE + row * HALF, HALF)
                        normed = normed_s[j, pl.ds(at, HALF), :]
                        grad, sums = conv_back_at(found, taps, sums, normed * scale + shift, row_par, col_par)
                        grads_out[pl.ds(at, HALF), lanes] = grad
                        prod = grad * normed
                        shift_sum = shift_sum + (grad[:8] + grad[8:])
                        scale_sum = scale_sum + (prod[:8] + prod[8:])
                return sums, (shift_sum, scale_sum)

            zero = jnp.zeros((8, LANES), F32)
            sums, pair = lax.fori_loop(0, HALF, backward, (no_sums(), (zero, zero)))
            for which in range(2):
                sums_out[which : which + 1, lanes] = jnp.sum(pair[which], axis=0, keepdims=True)
            for tap in range(9):
                kern_out[tap : tap + 1, lanes] = jnp.sum(sums[tap], axis=0, keepdims=True)


def conv_back_stage(idx, g_own, g_other, w_own, part_a, part_b, tok, mod, kern):
    length, width = tok.shape
    count = width // LANES
    cols = g_own.shape[-1]
    return pl.pallas_call(
        conv_back_kernel,
        out_shape=(
            jax.ShapeDtypeStruct((length, width), F32),
            jax.ShapeDtypeStruct((9, width), F32),
            jax.ShapeDtypeStruct((2, width), F32),
        ),
        grid_spec=pltpu.PrefetchScalarGridSpec(
            num_scalar_prefetch=1,
            grid=(GROUPS // 2,),
            in_specs=[
                pair_rows(cols),
                pair_rows(cols),
                whole(w_own.shape),
                leading(part_a, 3),
                leading(part_b, 3),
                pair_rows(width),
                whole(mod.shape),
                whole(kern.shape),
            ],
            out_specs=[whole((length, width)), whole((9, width)), whole((2, width))],
            scratch_shapes=[
                pltpu.VMEM((count, PAD_ROWS, LANES), F32),
                pltpu.VMEM((count, length, LANES), F32),
            ],
        ),
        compiler_params=params(),
        name="conv_back",
        cost_estimate=cost(18),
    )(idx, g_own, g_other, w_own, part_a, part_b, tok, mod, kern)


def norm_back_kernel(grads_ref, tok_ref, gres_ref, mod_ref, gtok_out, ordered):
    width = tok_ref.shape[-1]
    group = pl.program_id(0)
    grads = grads_ref[...]
    normed, rstd = norm_rows(tok_ref[...].astype(F32))
    scaled = grads * (1.0 + mod_ref[1:2, :])
    mean_a = jnp.mean(scaled, axis=-1, keepdims=True)
    mean_b = jnp.mean(scaled * normed, axis=-1, keepdims=True)
    result = gres_ref[...] + rstd * (scaled - mean_a - normed * mean_b)
    parity = (group // 2) * SIDE + lax.rem(group, 2)
    for row in range(HALF):
        for j in range(width // LANES):
            ordered[j, pl.ds(parity + row * 2 * SIDE, HALF, stride=2), :] = result[
                row * HALF : (row + 1) * HALF, j * LANES : (j + 1) * LANES
            ]

    @pl.when(group == GROUPS - 1)
    def _():
        for j in range(width // LANES):
            gtok_out[:, j * LANES : (j + 1) * LANES] = ordered[j].astype(BF16)


def norm_back_stage(grads, tok, gres, mod):
    length, width = tok.shape
    return pl.pallas_call(
        norm_back_kernel,
        out_shape=jax.ShapeDtypeStruct((length, width), BF16),
        grid=(GROUPS,),
        in_specs=[group_rows(width), group_rows(width), group_rows(width), whole(mod.shape)],
        out_specs=whole((length, width)),
        scratch_shapes=[pltpu.VMEM((width // LANES, length, LANES), F32)],
        compiler_params=params(),
        name="norm_back",
        cost_estimate=cost(6),
    )(grads, tok, gres, mod)


def silu_of(values_in):
    return values_in * jax.nn.sigmoid(values_in)


def swap(values_in, axis, bit):
    size = lax.axis_size(axis)
    return lax.ppermute(values_in, axis, [(i, i ^ bit) for i in range(size)])


def spread(size, position):
    if size < 4:
        return position
    quarter = size // 4
    low, rest = position // (2 * quarter), position % (2 * quarter)
    return (rest % quarter) * 4 + (rest // quarter) * 2 + low


def row_permutation(size, width):
    block = width // size
    order = [spread(size, i // block) * block + i % block for i in range(width)]
    source = jnp.array(order, jnp.int32)
    return (source[:, None] == jnp.arange(width, dtype=jnp.int32)[None, :]).astype(BF16)


def tie(values_in, *first):
    return lax.optimization_barrier((values_in, first))[0]


def halving_bits(size):
    bits = [2] if size > 2 else []
    rest = size // 4
    while rest > 1:
        bits.append(rest * 2)
        rest //= 2
    return bits


def unshuffle(tokens_in):
    blocked = tokens_in.reshape(HALF, 2, HALF, 2)
    return blocked.transpose(1, 3, 0, 2).reshape(GROUPS, TILE)


def local(
    tokens,
    valid,
    steps,
    labels,
    w_mod,
    step_table,
    class_table,
    conv_attn,
    w_qkv,
    w_out,
    conv_ffn,
    w_up,
    w_down,
    cotangent,
):
    dp_size = lax.axis_size("dp")
    width = tokens.shape[-1]
    dp_at = lax.axis_index("dp")
    mp_at = lax.axis_index("mp")
    latent = dp_at * tokens.shape[0] + mp_at
    idx = jnp.stack([mp_at, dp_at % 2, 0]).astype(jnp.int32)
    perm = row_permutation(dp_size, width)

    core = dp_at % 2
    half_rows = width // 2
    hidden = w_up.shape[-1]
    share = w_out.shape[-1]
    rows = width // dp_size
    bits = halving_bits(dp_size)

    def split_rows(total, bit):
        rows = total.shape[-2] // 2
        parts = total.reshape(total.shape[:-2] + (2, rows) + total.shape[-1:])
        axis = parts.ndim - 3
        flag = (dp_at // bit) % 2
        mine = lax.dynamic_index_in_dim(parts, flag, axis, keepdims=False)
        theirs = lax.dynamic_index_in_dim(parts, 1 - flag, axis, keepdims=False)
        return mine, theirs.astype(BF16)

    def last_rows(total, *first):
        if len(bits) < 3:
            sent = []
            for bit in bits[1:]:
                mine, theirs = split_rows(total, bit)
                sent.append(theirs)
                total = mine + swap(theirs, "dp", bit).astype(F32)
            return total, sent
        parts = total.reshape(4, -1, total.shape[-1])
        at = (dp_at // 4) % 4
        kept = lax.dynamic_index_in_dim(parts, at, 0, keepdims=False)
        sent = [
            lax.dynamic_index_in_dim(parts, at ^ by, 0, keepdims=False).astype(BF16) for by in (1, 2, 3)
        ]
        for by, theirs in zip((1, 2, 3), sent, strict=True):
            kept = kept + tie(swap(theirs, "dp", 4 * by), *first).astype(F32)
        return kept, sent

    def both(mine, theirs):
        place = lax.broadcasted_iota(jnp.int32, (2,) + mine.shape, 0)
        return jnp.where(place == mp_at, mine[None], theirs[None])

    qkv_own = w_qkv.transpose(1, 0, 2)
    stack = jnp.concatenate([qkv_own, w_out[None]], axis=0)
    part_a = swap(lax.dynamic_slice_in_dim(stack, core * half_rows, half_rows, axis=1), "mp", 1)

    embedding = jnp.take(step_table, steps, axis=0).astype(F32) + jnp.take(
        class_table, labels, axis=0
    ).astype(F32)
    silu_value, silu_pull = jax.vjp(silu_of, embedding)
    silu_low = silu_value.astype(BF16)
    my_silu = lax.dynamic_slice_in_dim(silu_low, latent, 1)
    mod = modulation_stage(my_silu, w_mod)

    my_valid = lax.dynamic_index_in_dim(valid, mp_at, 0, keepdims=False)
    keep = unshuffle(my_valid)[:, :, None]

    conved, tok, cot = first_stage(idx, tokens, cotangent, mod, conv_attn)
    up_part, down_part = tie((w_up, w_down), conved)
    ffn_part = jnp.where(core == 0, up_part, down_part)
    part_a = tie(part_a, ffn_part, perm, keep)
    part_b = swap(part_a, "dp", 1)
    ffn_part = tie(ffn_part, part_a)
    ffn_a = swap(ffn_part, "mp", 1)
    conv_t, qkv_x, mixed_x = attend_own_stage(tie(conved, ffn_part), keep, qkv_own, perm)
    qkv_y, mixed_y, attn, res, normed, gdown, normed_t, gdown_t = attend_other_stage(
        idx, tie(conved, mixed_x), keep, part_a, part_b, mixed_x, w_out, tok, cot, mod
    )

    chunks = hidden // TILE
    shared = (normed, gdown, normed_t, gdown_t)
    acc_own, grads_ffn, kern_here = ffn_stage(idx, *shared, w_up, w_down, conv_ffn, 0, 2 * chunks, None)
    ffn_a = tie(ffn_a, acc_own)
    ffn_b = swap(ffn_a, "dp", 1)
    kern_other = swap(tie(conv_ffn, ffn_a), "mp", 1)
    idx_other = jnp.stack([mp_at, core, core]).astype(jnp.int32)
    acc_other, grads_ffn, kern_z = ffn_stage(
        idx_other, *shared, ffn_a, ffn_b, kern_other, chunks, 2 * chunks, grads_ffn
    )
    sum_ffn = lax.psum_scatter(grads_ffn, "dp", scatter_dimension=0, tiled=True)
    top, bottom, gres, gmix, sums_mid, out_keep, out_send = middle_stage(
        idx, perm, res, attn, acc_own, acc_other, cot, (mixed_x, mixed_y), w_out, part_a, part_b, mod
    )
    top_other = swap(top, "mp", 1)
    g_other, c_keep, c_send = attend_back_stage(idx, qkv_y, gmix, keep, conv_t, out_keep, out_send, 1)
    c_got = swap(c_send, "dp", 1)
    bottom_other = swap(tie(bottom, top_other, c_send), "mp", 1)
    kern_here, kern_z = kern_here.reshape(-1, width), kern_z.reshape(-1, width)
    g_own, d_keep, d_send = attend_back_stage(
        idx, qkv_x, tie(gmix, c_send, top_other, kern_here, kern_z), keep, conv_t, out_keep, out_send, 0
    )
    c_got = tie(c_got, g_own)
    total_c = (c_keep + c_got.astype(F32)).astype(BF16)
    from_x = swap(tie(total_c, bottom_other), "mp", 1)
    d_got = swap(tie(d_send, bottom_other), "dp", 1)
    grads, kern_a, sums_last = conv_back_stage(
        idx, tie(g_own, total_c, bottom_other), g_other, qkv_own, part_a, part_b, tok, mod, conv_attn
    )

    sent = jnp.concatenate([kern_z, kern_a], axis=0)
    held = jnp.concatenate([kern_here, kern_a], axis=0)
    grad_mod = jnp.concatenate([sums_last, sums_mid], axis=0)
    mine = grad_mod.reshape(1, -1).astype(BF16)
    mod_there, held_there = swap(mine, "mp", 1), swap(sent, "mp", 1)
    gtok = norm_back_stage(tie(grads, mine, sent), tok, gres, mod)

    gtok_other = swap(tie(gtok, mod_there, held_there), "mp", 1)
    d_got, from_x, mod_there, held_there = tie((d_got, from_x, mod_there, held_there), gtok)
    total_d = d_keep + d_got.astype(F32) + from_x.astype(F32)
    mine_d, theirs = split_rows(total_d, bits[0])
    held = held + held_there
    held = held + swap(held, "dp", 1)
    held_y = swap(held, "dp", 2) if dp_size > 2 else None
    got_d = swap(tie(theirs, held), "dp", bits[0])
    gathered = jnp.concatenate([mine, mod_there], axis=0)
    step = 1
    while step < dp_size:
        if 4 * step <= dp_size:
            others = [swap(gathered, "dp", step * by) for by in (1, 2, 3)]
            gathered = jnp.concatenate([gathered, *others], axis=0)
            step *= 4
        else:
            gathered = jnp.concatenate([gathered, swap(gathered, "dp", step)], axis=0)
            step *= 2
    latents = steps.shape[0]
    order = jnp.arange(latents, dtype=jnp.int32) ^ latent.astype(jnp.int32)
    sort = (order[None, :] == jnp.arange(latents, dtype=jnp.int32)[:, None]).astype(BF16)
    grad_mod_low = jnp.dot(sort, gathered, preferred_element_type=F32).astype(BF16)
    grad_silu = jnp.einsum("lc,kc->lk", grad_mod_low, w_mod, preferred_element_type=F32)

    total_d = mine_d + got_d.astype(F32)
    for bit in bits[1:-2]:
        mine_d, theirs = split_rows(total_d, bit)
        total_d = mine_d + swap(theirs, "dp", bit).astype(F32)
    far_ffn = tie(sum_ffn, gtok)[:, 2 * hidden :]
    total_d, sent_d = last_rows(total_d, far_ffn)
    from_f = swap(far_ffn, "mp", 1)
    top, bottom, top_other, bottom_other = tie((top, bottom, top_other, bottom_other), sent_d)
    whole_output = both(
        jnp.concatenate([top, bottom], axis=0), jnp.concatenate([top_other, bottom_other], axis=0)
    )
    whole_gtok = both(gtok, tie(gtok_other, whole_output))
    grad_silu, grad_mod_low = tie((grad_silu, grad_mod_low), sent_d, far_ffn)

    if dp_size > 2:
        held = held + held_y
    step = 4
    while step < dp_size:
        held = held + swap(held, "dp", step)
        step *= 2
    kern_f = held[:-9].reshape(9, hidden)
    kern_a = held[-9:]
    (grad_embedding,) = silu_pull(grad_silu)
    my_cols = lax.dynamic_slice_in_dim(silu_low, dp_at * rows, rows, axis=1)
    grad_w_mod = jnp.einsum("lk,lc->kc", my_cols, grad_mod_low, preferred_element_type=F32)

    grad_qkv = total_d[:, : 3 * share].reshape(rows, 3, share)
    grad_out = total_d[:, 3 * share :]
    ffn_sum = sum_ffn[:, : 2 * hidden].astype(F32) + from_f.astype(F32)
    ffn_sum = ffn_sum.reshape(rows, chunks, 2, TILE)
    grad_up = ffn_sum[:, :, 0].reshape(rows, hidden)
    grad_down = ffn_sum[:, :, 1].reshape(rows, hidden)

    def table_grad(indices, count):
        onehot = (jnp.arange(count, dtype=jnp.int32)[:, None] == indices[None, :]).astype(F32)
        return jnp.dot(onehot, grad_embedding, precision=lax.Precision.HIGHEST)

    return (
        whole_output,
        whole_gtok,
        grad_w_mod,
        table_grad(steps, step_table.shape[0]),
        table_grad(labels, class_table.shape[0]),
        kern_a,
        grad_qkv,
        grad_out,
        kern_f,
        grad_up,
        grad_down,
    )


def solution(mesh):
    in_specs = (
        P("dp", None, None),
        P("dp", None),
        P(),
        P(),
        P(),
        P(),
        P(),
        P(),
        P(None, None, "mp"),
        P(None, "mp"),
        P(None, "mp"),
        P(None, "mp"),
        P(None, "mp"),
        P("dp", None, None),
    )
    out_specs = (
        P("dp", None, None),
        P("dp", None, None),
        P("dp", None),
        P(),
        P(),
        P(),
        P("dp", None, "mp"),
        P("dp", "mp"),
        P(None, "mp"),
        P("dp", "mp"),
        P("dp", "mp"),
    )
    return jax.shard_map(local, mesh=mesh, in_specs=in_specs, out_specs=out_specs, check_vma=False)
```
